32 devices in a mesh: ctx: 8 (over z, x), fsdp: 4 (over y, core).
Axes of the slice: x: 2, y: 2, z: 4, core: 2. Of those that a mesh axis runs over, the one named last changes fastest.
Arguments:
- proj_xbc: bfloat16 [4, 1024, 10240], P('fsdp', 'ctx'), may hold values from -6 to 6
- proj_dt: bfloat16 [4, 1024, 128], P('fsdp', 'ctx'), may hold values from -3 to 3
- proj_gate: bfloat16 [4, 1024, 8192], P('fsdp', 'ctx'), may hold values from -6 to 6
- out_grad: bfloat16 [4, 1024, 8192], P('fsdp', 'ctx'), may hold values from -6 to 6
- conv_weight: float32 [4, 10240], P(None, 'fsdp'), may hold values from -3 to 3
- conv_bias: float32 [10240], P('fsdp'), may hold values from -0.5 to 0.5
- decay_log: float32 [128], P('fsdp'), may hold values from -12 to -3
- step_bias: float32 [128], P('fsdp'), may hold values from -0.5 to 0.5
- skip_gain: float32 [128], P('fsdp'), may hold values from 0.5 to 1.5
- norm_gain: float32 [8192], P('fsdp'), may hold values from 0.5 to 1.5
Outputs:
- grad_xbc: bfloat16 [4, 1024, 10240], P('fsdp', 'ctx')
- grad_dt: float32 [4, 1024, 128], P('fsdp', 'ctx')
- grad_gate: bfloat16 [4, 1024, 8192], P('fsdp', 'ctx')
- grad_conv_weight: float32 [4, 10240], P(None, 'fsdp')
- grad_conv_bias: float32 [10240], P('fsdp')
- grad_decay_log: float32 [128], P('fsdp')
- grad_step_bias: float32 [128], P('fsdp')
- grad_skip_gain: float32 [128], P('fsdp')
- grad_norm_gain: float32 [8192], P('fsdp')
The draws below stay inside these ranges and needn't reach their ends.
All inputs are finite; a program needn't handle non-finite values.
Results may differ from the reference program's by a relative error of at most 0.012.
Values may be sent and summed in bfloat16 or wider, within the bound.
No kernel may reach another device: no remote copies, remote signals or barrier semaphores. Data moves between devices by JAX's collectives and lax.ppermute only.
A program may use at most 320 MiB of HBM per device.

```python
import math
import jax
import jax.numpy as jnp
from jax import lax

HEADS = 128
HEAD_DIM = 64
STATE = 128
GROUPS = 8
KERNEL = 4
BLOCK = 64
INNER = 8192
CHANNELS = 10240
SEQ = 1024
BATCH = 4
TOKENS = 4096


def draw_decay_log(key, part):
    key_pick, key_slow, key_fast = jax.random.split(key, 3)
    chooser = jax.random.uniform(key_pick, (HEADS,), jnp.float32)
    keep_share = 0.5
    slow_rate = jax.random.uniform(key_slow, (HEADS,), jnp.float32, 0.3, 1.0) * (3.0 / SEQ)
    fast_rate = jax.random.uniform(key_fast, (HEADS,), jnp.float32, 1.0 / 40.0, 1.0 / 22.0)
    return jnp.log(jnp.where(chooser < keep_share, slow_rate, fast_rate)).astype(jnp.float32)


def shard_levels(key, dims, shards, smallest, high):
    gain, own = 1.0, jax.random.fold_in(key, 6)
    for dim, parts in shards:
        steps = jnp.exp(jax.random.uniform(jax.random.fold_in(own, dim), (parts,), jnp.float32, smallest / len(shards), high / len(shards)))
        gain = gain * jnp.repeat(steps, dims[dim] // parts).reshape([-1 if axis == dim else 1 for axis in range(len(dims))])
    return gain


def normal_values(key, dims, scale, limit, shards=(), kind=jnp.bfloat16):
    loudness = shard_levels(key, dims, shards, -0.22, 0.18) if shards else 1.0
    values = jax.random.normal(key, dims, jnp.float32) * scale * loudness
    return jnp.minimum(jnp.maximum(values, -limit), limit).astype(kind)


def setup_inputs(seed: int = 0) -> dict:
    splits = jax.random.split(jax.random.key(seed), 11)
    return {
        "proj_xbc": normal_values(splits[0], (BATCH, SEQ, CHANNELS), 1.0, 6.0, ((0, 4), (1, 8))),
        "proj_dt": normal_values(splits[1], (BATCH, SEQ, HEADS), 0.5, 3.0, ((0, 4), (1, 8))),
        "proj_gate": normal_values(splits[2], (BATCH, SEQ, INNER), 1.0, 6.0, ((0, 4), (1, 8))),
        "out_grad": normal_values(splits[3], (BATCH, SEQ, INNER), 1.0, 6.0, ((0, 4), (1, 8))),
        "conv_weight": normal_values(splits[4], (KERNEL, CHANNELS), KERNEL ** -0.5, 3.0, ((1, 4),), jnp.float32),
        "conv_bias": jnp.clip(jax.random.uniform(splits[5], (CHANNELS,), jnp.float32, -0.5, 0.5) * shard_levels(splits[5], (CHANNELS,), ((0, 4),), -0.4, 0.0), -0.5, 0.5),
        "decay_log": draw_decay_log(jax.random.fold_in(splits[10], 71), 0),
        "step_bias": jnp.clip(jax.random.uniform(splits[7], (HEADS,), jnp.float32, -0.5, 0.5) * shard_levels(splits[7], (HEADS,), ((0, 4),), -0.4, 0.0), -0.5, 0.5),
        "skip_gain": jnp.clip(0.5 + 1.0 * jax.random.uniform(splits[8], (HEADS,), jnp.float32) ** shard_levels(splits[8], (HEADS,), ((0, 4),), -0.2, 0.2), 0.5, 1.5),
        "norm_gain": jnp.clip(1.0 + 0.1 * jax.random.normal(splits[9], (INNER,), jnp.float32), 0.5, 1.5),
    }


EPSILON = 1e-05
HIGHEST = lax.Precision.HIGHEST

def block_step(states, pieces):
    values, keys_in, queries, log_decay, step_size = pieces
    length = values.shape[0]
    running = jnp.cumsum(log_decay, axis=0)
    running_t = running.T
    row_index = lax.broadcasted_iota(jnp.int32, (length, length), 0)
    col_index = lax.broadcasted_iota(jnp.int32, (length, length), 1)
    causal = (row_index >= col_index)[None]
    spread = running_t[:, :, None] - running_t[:, None, :]
    decay = jnp.where(causal, jnp.exp(jnp.minimum(spread, 0.0)), 0.0)
    scores = jnp.dot(queries, keys_in.T, precision=HIGHEST)
    mixing = scores[None] * decay * step_size.T[:, None, :]
    inside = jnp.einsum('hts,shp->thp', mixing, values, precision=HIGHEST)
    carried = jnp.einsum('tn,hpn->thp', queries, states, precision=HIGHEST) * jnp.exp(running)[:, :, None]
    closing = running[-1]
    weight = jnp.exp(closing[None, :] - running) * step_size
    update = jnp.einsum('shp,sn->hpn', values * weight[:, :, None], keys_in, precision=HIGHEST)
    return (jnp.exp(closing)[:, None, None] * states + update, inside + carried)

def group_scan(pieces, block):
    values, keys_in, queries, log_decay, step_size, start = pieces
    length = values.shape[0]
    count = length // block
    blocks = (values.reshape((count, block) + values.shape[1:]), keys_in.reshape(count, block, keys_in.shape[1]), queries.reshape(count, block, queries.shape[1]), log_decay.reshape(count, block, log_decay.shape[1]), step_size.reshape(count, block, step_size.shape[1]))
    finals, outputs = lax.scan(jax.checkpoint(block_step), start, blocks)
    return outputs.reshape((length,) + outputs.shape[2:])

def split_channels(mixed_in, heads, groups):
    length = mixed_in.shape[0]
    width = heads * HEAD_DIM
    values = mixed_in[:, :width].reshape(length, groups, heads // groups, HEAD_DIM)
    keys_in = mixed_in[:, width:width + groups * STATE].reshape(length, groups, STATE)
    queries = mixed_in[:, width + groups * STATE:].reshape(length, groups, STATE)
    return (values, keys_in, queries)

def decays(raw_step, step_bias, decay_log):
    step_size = jax.nn.softplus(raw_step + step_bias)
    return (step_size, -jnp.exp(decay_log) * step_size)

def mixer(mixed_in, raw_step, step_bias, decay_log, skip_gain, start, block, groups):
    length, heads = raw_step.shape
    values, keys_in, queries = split_channels(mixed_in, heads, groups)
    step_size, log_decay = decays(raw_step, step_bias, decay_log)
    per_group = heads // groups
    pieces = (jnp.moveaxis(values, 1, 0), jnp.moveaxis(keys_in, 1, 0), jnp.moveaxis(queries, 1, 0), jnp.moveaxis(log_decay.reshape(length, groups, per_group), 1, 0), jnp.moveaxis(step_size.reshape(length, groups, per_group), 1, 0), start.reshape(groups, per_group, HEAD_DIM, STATE))
    outputs = lax.map(lambda member: group_scan(member, block), pieces)
    outputs = jnp.moveaxis(outputs, 0, 1).reshape(length, heads, HEAD_DIM)
    direct = values.reshape(length, heads, HEAD_DIM) * skip_gain[None, :, None]
    return (outputs + direct).reshape(length, heads * HEAD_DIM)

def gated_norm(mixed_out, gate_in, norm_gain):
    length = mixed_out.shape[0]
    gated = mixed_out * jax.nn.silu(gate_in)
    grouped = gated.reshape(length, GROUPS, -1)
    scaling = lax.rsqrt(lax.optimization_barrier(jnp.mean(grouped * grouped, axis=-1, keepdims=True)) + EPSILON)
    return (grouped * scaling).reshape(length, -1) * norm_gain

def silu_slope(pre_act):
    sigma = jax.nn.sigmoid(pre_act)
    return sigma * (1.0 + pre_act * (1.0 - sigma))

def convolve(padded, taps, offsets, length):
    total = jnp.zeros((length, taps.shape[1]), jnp.float32) + offsets[None, :]
    for offset in range(KERNEL):
        total = total + taps[offset][None, :] * padded[offset:offset + length]
    return total

def convolve_back(trailing, taps, length):
    total = jnp.zeros((length, taps.shape[1]), jnp.float32)
    for offset in range(KERNEL):
        lead = KERNEL - 1 - offset
        total = total + taps[offset][None, :] * trailing[lead:lead + length]
    return total

def taps_grad(grad_pre, padded, length):
    return jnp.stack([lax.optimization_barrier(jnp.sum(grad_pre * padded[offset:offset + length], axis=0)) for offset in range(KERNEL)], axis=0)

def one_sequence(members, weights):
    proj_in, raw_in, gate_in, grad_in = members
    conv_weight, conv_bias, decay_log, step_bias, skip_gain, norm_gain = weights
    length = proj_in.shape[0]
    channels = proj_in.shape[1]
    padded = jnp.concatenate([jnp.zeros((KERNEL - 1, channels), jnp.float32), proj_in.astype(jnp.float32)], axis=0)
    pre_act = convolve(padded, conv_weight, conv_bias, length)
    rounded = jax.nn.silu(pre_act).astype(jnp.bfloat16)
    mixed_f = lax.optimization_barrier(rounded).astype(jnp.float32)
    start = jnp.zeros((HEADS, HEAD_DIM, STATE), jnp.float32)

    def forward(mixed_arg, raw_arg, bias_arg, decay_arg, skip_arg):
        return mixer(mixed_arg, raw_arg, bias_arg, decay_arg, skip_arg, start, BLOCK, GROUPS)
    mixed_out, mix_back = jax.vjp(forward, mixed_f, raw_in.astype(jnp.float32), step_bias, decay_log, skip_gain)
    out_rounded = mixed_out.astype(jnp.bfloat16)
    out_f = lax.optimization_barrier(out_rounded).astype(jnp.float32)
    normed, norm_back = jax.vjp(gated_norm, out_f, gate_in.astype(jnp.float32), norm_gain)
    grad_out, grad_gate, gain_part = norm_back(grad_in.astype(jnp.float32))
    grad_rounded = grad_out.astype(jnp.bfloat16)
    grad_f = lax.optimization_barrier(grad_rounded).astype(jnp.float32)
    grad_mixed, grad_raw, bias_part, decay_part, skip_part = mix_back(grad_f)
    grad_pre = grad_mixed * silu_slope(pre_act)
    trailing = jnp.concatenate([grad_pre, jnp.zeros((KERNEL - 1, channels), jnp.float32)], axis=0)
    grad_proj = convolve_back(trailing, conv_weight, length)
    weight_part = taps_grad(grad_pre, padded, length)
    return (grad_proj.astype(jnp.bfloat16), grad_raw, grad_gate.astype(jnp.bfloat16), weight_part, lax.optimization_barrier(jnp.sum(grad_pre, axis=0)), decay_part, bias_part, skip_part, gain_part)

def reference(proj_xbc, proj_dt, proj_gate, out_grad, conv_weight, conv_bias, decay_log, step_bias, skip_gain, norm_gain):
    weights = (conv_weight, conv_bias, decay_log, step_bias, skip_gain, norm_gain)
    results = lax.map(lambda member: one_sequence(member, weights), (proj_xbc, proj_dt, proj_gate, out_grad))
    scaling = 1.0 / math.sqrt(TOKENS)
    return (results[0], results[1], results[2], lax.optimization_barrier(jnp.sum(results[3], axis=0)) * scaling, lax.optimization_barrier(jnp.sum(results[4], axis=0)) * scaling, lax.optimization_barrier(jnp.sum(results[5], axis=0)) * scaling, lax.optimization_barrier(jnp.sum(results[6], axis=0)) * scaling, lax.optimization_barrier(jnp.sum(results[7], axis=0)) * scaling, lax.optimization_barrier(jnp.sum(results[8], axis=0)) * scaling)
```

```python
import math

import jax
import jax.numpy as jnp
from jax import lax
from jax.experimental import pallas as pl
from jax.experimental.pallas import tpu as pltpu
from jax.sharding import PartitionSpec as P

HEAD_DIM = 64
STATE = 128
GROUPS = 8
KERNEL = 4
EPSILON = 1e-05
HALO = KERNEL - 1
PAD = 8
F32 = jnp.float32
BF16 = jnp.bfloat16
HIGHEST = lax.Precision.HIGHEST


def mm(a, b):
    return jnp.dot(a, b, preferred_element_type=F32)


def mm_nt(a, b):
    return lax.dot_general(a, b, (((1,), (1,)), ((), ())), preferred_element_type=F32)


def sigmoid(v):
    return 0.5 * jnp.tanh(0.5 * v) + 0.5


def softplus(v):
    return jnp.maximum(v, 0.0) + jnp.log(1.0 + jnp.exp(-jnp.abs(v)))


def spread_heads(table, group, per_group):
    heads = table.shape[1]
    table = pltpu.roll(table, lax.rem(heads - group * per_group, heads), 1)
    rows = table.shape[0]
    pair = 128 // HEAD_DIM
    lane = lax.broadcasted_iota(jnp.int32, (rows, 128), 1)
    tiles = []
    for i in range(per_group // pair):
        tile = jnp.broadcast_to(table[:, pair * i : pair * i + 1], (rows, 128))
        for p in range(1, pair):
            col = jnp.broadcast_to(table[:, pair * i + p : pair * i + p + 1], (rows, 128))
            tile = jnp.where(lane >= p * HEAD_DIM, col, tile)
        tiles.append(tile)
    return jnp.concatenate(tiles, axis=1)


def sum_heads(values, group, per_group, heads):
    width = values.shape[1]
    row = lax.broadcasted_iota(jnp.int32, (width, heads), 0) // HEAD_DIM + group * per_group
    col = lax.broadcasted_iota(jnp.int32, (width, heads), 1)
    pick = jnp.where(row == col, 1.0, 0.0).astype(BF16)
    high = values.astype(BF16)
    low = (values - high.astype(F32)).astype(BF16)
    return mm(high, pick) + mm(low, pick)


def lower_mask(n):
    return lax.broadcasted_iota(jnp.int32, (n, n), 0) >= lax.broadcasted_iota(jnp.int32, (n, n), 1)


def upper_mask(n):
    return lax.broadcasted_iota(jnp.int32, (n, n), 0) <= lax.broadcasted_iota(jnp.int32, (n, n), 1)


def conv_pre(x_ref, halo_ref, w_ref, xs):
    length = x_ref.shape[0]
    xs[PAD - HALO : PAD, :] = halo_ref[...].astype(F32)
    xs[PAD : PAD + length, :] = x_ref[...].astype(F32)
    pre = jnp.broadcast_to(w_ref[KERNEL : KERNEL + 1, :], (length, x_ref.shape[1]))
    for k in range(KERNEL):
        pre = pre + w_ref[k : k + 1, :] * xs[PAD - HALO + k : PAD - HALO + k + length, :]
    return pre


def front_kernel(per_group, x_ref, halo_ref, w_ref, dt_ref, sb_ref, dl_ref,
                 mixed_ref, vp_ref, ut_ref, ec_ref, ei_ref, et_ref, xs, ks):
    j = pl.program_id(0)
    length = x_ref.shape[0]

    @pl.when(j == 0)
    def _():
        step = softplus(dt_ref[...].astype(F32) + sb_ref[...])
        ld = -jnp.exp(dl_ref[...]) * step
        tril = jnp.where(lower_mask(length), 1.0, 0.0).astype(F32)
        cum = jnp.dot(tril, ld, precision=HIGHEST, preferred_element_type=F32)
        ec_ref[...] = jnp.exp(cum)
        ei_ref[...] = jnp.exp(-cum) * step

    pre = conv_pre(x_ref, halo_ref, w_ref, xs)
    mixed = (pre * sigmoid(pre)).astype(BF16)
    mixed_ref[...] = mixed

    @pl.when(j == 0)
    def _():
        for g in range(GROUPS):
            ks[g] = mixed[:, g * STATE : (g + 1) * STATE]

    @pl.when(j >= 2)
    def _():
        g = j - 2
        eix = spread_heads(ei_ref[...], g, per_group)
        vp = (mixed.astype(F32) * eix).astype(BF16)
        vp_ref[...] = vp
        et = spread_heads(ec_ref[length - 8 : length, :], g, per_group)[7:8, :]
        et_ref[...] = et
        ut = mm(ks[g].astype(F32).T.astype(BF16), vp) * et
        reps, _, part = ut_ref.shape
        for r in range(reps):
            ut_ref[r] = ut[:, r * part : (r + 1) * part].astype(BF16)


def join_parts(ref):
    if ref.shape[0] == 1:
        return ref[0]
    return jnp.concatenate([ref[r] for r in range(ref.shape[0])], axis=1)


def middle_kernel(per_group, v_ref, k_ref, q_ref, vp_ref, st_ref, ec_ref, gate_ref, og_ref, gain_ref, skip_ref,
                  dy_ref, dyp_ref, gg_ref, gt_ref, rows_ref, a1_ref):
    g = pl.program_id(0)
    length, width = v_ref.shape
    heads = ec_ref.shape[1]
    q = q_ref[...]
    z = jnp.where(lower_mask(length), mm_nt(q, k_ref[...]), 0.0).astype(BF16)
    yn = mm(jnp.concatenate([z, q], axis=1), jnp.concatenate([vp_ref[...], join_parts(st_ref)], axis=0))
    ecx = spread_heads(ec_ref[...], g, per_group)
    v = v_ref[...].astype(F32)
    y = (ecx * yn + skip_ref[...] * v).astype(BF16).astype(F32)
    gate = gate_ref[...].astype(F32)
    og = og_ref[...].astype(F32)
    sig = sigmoid(gate)
    act = gate * sig
    gated = y * act
    scale = lax.rsqrt(jnp.sum(gated * gated, axis=1, keepdims=True) * (1.0 / width) + EPSILON)
    dgn = og * gain_ref[...]
    inner = jnp.sum(dgn * gated, axis=1, keepdims=True) * (1.0 / width)
    dgated = scale * dgn - gated * (scale * scale * scale * inner)
    dyb = (dgated * act).astype(BF16)
    dy_ref[...] = dyb
    gg_ref[...] = (dgated * y * (sig + act * (1.0 - sig))).astype(BF16)
    dy = dyb.astype(F32)
    dyp = (ecx * dy).astype(BF16)
    dyp_ref[...] = dyp
    gt = mm(q.astype(F32).T.astype(BF16), dyp)
    reps, _, part = gt_ref.shape
    for r in range(reps):
        gt_ref[r] = gt[:, r * part : (r + 1) * part].astype(BF16)
    rows_ref[...] = jnp.zeros(rows_ref.shape, F32)
    rows_ref[0:1, :] = jnp.sum(og * gated * scale, axis=0, keepdims=True)
    rows_ref[1:2, :] = jnp.sum(dy * v, axis=0, keepdims=True)

    @pl.when(g == 0)
    def _():
        a1_ref[...] = jnp.zeros(a1_ref.shape, F32)

    a1_ref[...] += sum_heads(dyp.astype(F32) * yn, g, per_group, heads)


def back_kernel(per_group, v_ref, k_ref, q_ref, vp_ref, st_ref, en_ref, dy_ref, dyp_ref, x_ref, halo_ref, w_ref,
                skip_ref, et_ref, ei_ref, a1_ref, dt_ref, sb_ref, dl_ref,
                gx_ref, edge_ref, wr_ref, gdt_ref, hs_ref, xs, gs, gm, dkq, a2, last):
    j = pl.program_id(0)
    length, width = v_ref.shape
    heads = ei_ref.shape[1]

    @pl.when(j == 0)
    def _():
        a2[...] = jnp.zeros(a2.shape, F32)
        last[...] = jnp.zeros(last.shape, F32)
        gs[length:, :] = jnp.zeros((gs.shape[0] - length, gs.shape[1]), F32)

    @pl.when(j < GROUPS)
    def _():
        k = k_ref[...]
        q = q_ref[...]
        vp = vp_ref[...]
        dyp = dyp_ref[...]
        st = join_parts(st_ref)
        en = (et_ref[...] * join_parts(en_ref).astype(F32)).astype(BF16)
        low = lower_mask(length)
        zt = jnp.where(upper_mask(length), mm_nt(k, q), 0.0).astype(BF16)
        dvp = mm(jnp.concatenate([zt, k], axis=1), jnp.concatenate([dyp, en], axis=0))
        eix = spread_heads(ei_ref[...], j, per_group)
        gm[...] = eix * dvp + skip_ref[...] * dy_ref[...].astype(F32)
        a2[...] += sum_heads(vp.astype(F32) * dvp, j, per_group, heads)
        ends = en.astype(F32) * (st.astype(F32) + mm(k.astype(F32).T.astype(BF16), vp))
        ends = jnp.broadcast_to(jnp.sum(ends, axis=0, keepdims=True), (8, width))
        last[...] += sum_heads(ends, j, per_group, heads)
        dz = jnp.where(low, mm_nt(dyp, vp), 0.0)
        dzb = dz.astype(BF16)
        cols = pl.ds(pl.multiple_of(j * STATE, STATE), STATE)
        dkq[0, :, cols] = mm(dz.T.astype(BF16), q) + mm_nt(vp, en)
        dkq[1, :, cols] = mm(dzb, k) + mm_nt(dyp, st)

    @pl.when(j >= GROUPS)
    def _():
        gm[...] = dkq[j - GROUPS]

    pre = conv_pre(x_ref, halo_ref, w_ref, xs)
    sig = sigmoid(pre)
    gp = gm[...] * (sig * (1.0 + pre * (1.0 - sig)))
    gs[0:length, :] = gp
    wr_ref[...] = jnp.zeros(wr_ref.shape, F32)
    total = jnp.zeros(gp.shape, F32)
    for k in range(KERNEL):
        lead = HALO - k
        total = total + w_ref[k : k + 1, :] * gs[lead : lead + length, :]
        wr_ref[k : k + 1, :] = jnp.sum(gp * xs[PAD - HALO + k : PAD - HALO + k + length, :], axis=0, keepdims=True)
    wr_ref[KERNEL : KERNEL + 1, :] = jnp.sum(gp, axis=0, keepdims=True)
    gx_ref[...] = total.astype(BF16)
    edge_ref[...] = jnp.zeros(edge_ref.shape, F32)
    edge_ref[0:HALO, :] = gp[0:HALO, :]
    edge_ref[HALO : 2 * HALO, :] = total[length - HALO : length, :]

    @pl.when(j == pl.num_programs(0) - 1)
    def _():
        raw = dt_ref[...].astype(F32) + sb_ref[...]
        step = softplus(raw)
        rate = jnp.exp(dl_ref[...])
        row = lax.broadcasted_iota(jnp.int32, (length, heads), 0)
        dcum = a1_ref[...] - a2[...] + jnp.where(row == length - 1, last[0:1, :], 0.0)
        triu = jnp.where(upper_mask(length), 1.0, 0.0).astype(F32)
        dld = jnp.dot(triu, dcum, precision=HIGHEST, preferred_element_type=F32)
        gdt = (a2[...] / step - rate * dld) * sigmoid(raw)
        gdt_ref[...] = gdt
        hs_ref[...] = jnp.zeros(hs_ref.shape, F32)
        hs_ref[0:1, :] = jnp.sum(-rate * step * dld, axis=0, keepdims=True)
        hs_ref[1:2, :] = jnp.sum(gdt, axis=0, keepdims=True)


def scan_kernel(backward, u_ref, d_ref, o_ref):
    count = u_ref.shape[0]
    acc = jnp.zeros(u_ref.shape[1:], F32)
    order = range(count - 1, -1, -1) if backward else range(count)
    for i in order:
        o_ref[i] = acc.astype(BF16)
        acc = d_ref[i : i + 1, :] * acc + u_ref[i].astype(F32)


PARAMS = pltpu.CompilerParams(vmem_limit_bytes=48 * 1024 * 1024)


def scan_states(states, decay, backward):
    count, rows, wide = states.shape
    tile = 32
    return pl.pallas_call(
        lambda *refs: scan_kernel(backward, *refs),
        out_shape=jax.ShapeDtypeStruct(states.shape, BF16),
        grid=(rows // tile,),
        in_specs=[
            pl.BlockSpec((count, tile, wide), lambda i: (0, i, 0)),
            pl.BlockSpec((count, wide), lambda i: (0, 0)),
        ],
        out_specs=pl.BlockSpec((count, tile, wide), lambda i: (0, i, 0)),
        compiler_params=PARAMS,
        name="scan_back" if backward else "scan_front",
    )(states, decay)


def body(proj_xbc, proj_dt, proj_gate, out_grad, conv_weight, conv_bias, decay_log, step_bias, skip_gain, norm_gain):
    x, dt, gate, og = proj_xbc[0], proj_dt[0], proj_gate[0], out_grad[0]
    length, channels = x.shape
    heads = dt.shape[1]
    inner = heads * HEAD_DIM
    ranks = lax.axis_size("ctx")
    shards = lax.axis_size("fsdp")
    per_group = heads // GROUPS
    width = per_group * HEAD_DIM
    reps = ranks // GROUPS
    wide = inner // ranks
    own_heads = heads // ranks
    c_loc, g_loc, h_loc = channels // shards, inner // shards, heads // shards
    spare = c_loc - g_loc - 3 * h_loc
    groups = GROUPS
    blocks = channels // width

    ahead = [(i, i + 1) for i in range(ranks - 1)]
    behind = [(i + 1, i) for i in range(ranks - 1)]
    halo = lax.ppermute(x[length - HALO :, :], "ctx", ahead)

    def pack_row(gain, decay, step, skip):
        return jnp.concatenate([gain, decay, step, skip, jnp.zeros(gain.shape[:-1] + (spare,), F32)], axis=-1)

    packed = jnp.concatenate(
        [conv_weight, conv_bias[None], pack_row(norm_gain, decay_log, step_bias, skip_gain)[None],
         jnp.zeros((8 - KERNEL - 2, c_loc), F32)], axis=0)
    full = lax.all_gather(packed, "fsdp", axis=1, tiled=True)
    extra = full[KERNEL + 1].reshape(shards, c_loc)
    gain = extra[:, :g_loc].reshape(1, inner)
    decay = extra[:, g_loc : g_loc + h_loc].reshape(1, heads)
    step_b = extra[:, g_loc + h_loc : g_loc + 2 * h_loc].reshape(1, heads)
    skip = extra[:, g_loc + 2 * h_loc : g_loc + 3 * h_loc].reshape(1, heads)
    skip_x = jnp.repeat(skip, HEAD_DIM, axis=1)

    rate = jnp.exp(-jnp.exp(decay[0]) * jnp.sum(jax.nn.softplus(dt.astype(F32) + step_b), axis=0))
    rates = lax.all_to_all(rate.reshape(ranks, own_heads), "ctx", 0, 0, tiled=True)
    rates_x = jnp.repeat(rates, HEAD_DIM, axis=1)

    def col(j):
        return jnp.where(j < 2, groups + j, j - 2)

    def grp(j):
        return jnp.maximum(j - 2, 0)

    full_head = pl.BlockSpec((length, heads), lambda j: (0, 0))
    row_head = pl.BlockSpec((1, heads), lambda j: (0, 0))
    state_shape = jax.ShapeDtypeStruct((ranks, STATE, wide), BF16)
    mixed, vp, ut, ec, ei, et = pl.pallas_call(
        lambda *refs: front_kernel(per_group, *refs),
        out_shape=(
            jax.ShapeDtypeStruct((length, channels), BF16),
            jax.ShapeDtypeStruct((length, inner), BF16),
            state_shape,
            jax.ShapeDtypeStruct((length, heads), F32),
            jax.ShapeDtypeStruct((length, heads), F32),
            jax.ShapeDtypeStruct((1, inner), F32),
        ),
        grid=(blocks,),
        in_specs=[
            pl.BlockSpec((length, width), lambda j: (0, col(j))),
            pl.BlockSpec((HALO, width), lambda j: (0, col(j))),
            pl.BlockSpec((8, width), lambda j: (0, col(j))),
            full_head, row_head, row_head,
        ],
        out_specs=(
            pl.BlockSpec((length, width), lambda j: (0, col(j))),
            pl.BlockSpec((length, width), lambda j: (0, grp(j))),
            pl.BlockSpec((reps, STATE, wide), lambda j: (grp(j), 0, 0)),
            full_head, full_head,
            pl.BlockSpec((1, width), lambda j: (0, grp(j))),
        ),
        scratch_shapes=[pltpu.VMEM((PAD + length, width), F32), pltpu.VMEM((GROUPS, length, STATE), BF16)],
        compiler_params=PARAMS,
        name="front",
    )(x, halo, full, dt, step_b, decay)

    def swap(states):
        return lax.all_to_all(states, "ctx", 0, 0, tiled=True)

    starts = swap(scan_states(swap(ut), rates_x, False))

    wide_spec = pl.BlockSpec((length, width), lambda g: (0, g))
    line_spec = pl.BlockSpec((1, width), lambda g: (0, g))
    k_at = inner // STATE
    q_at = k_at + GROUPS
    state_spec = pl.BlockSpec((reps, STATE, wide), lambda g: (g, 0, 0))
    dy, dyp, grad_gate, gt, rows, a1 = pl.pallas_call(
        lambda *refs: middle_kernel(per_group, *refs),
        out_shape=(
            jax.ShapeDtypeStruct((length, inner), BF16),
            jax.ShapeDtypeStruct((length, inner), BF16),
            jax.ShapeDtypeStruct((length, inner), BF16),
            state_shape,
            jax.ShapeDtypeStruct((8, inner), F32),
            jax.ShapeDtypeStruct((length, heads), F32),
        ),
        grid=(GROUPS,),
        in_specs=[
            wide_spec,
            pl.BlockSpec((length, STATE), lambda g: (0, k_at + g)),
            pl.BlockSpec((length, STATE), lambda g: (0, q_at + g)),
            wide_spec, state_spec, full_head, wide_spec, wide_spec, line_spec, line_spec,
        ],
        out_specs=(wide_spec, wide_spec, wide_spec, state_spec, pl.BlockSpec((8, width), lambda g: (0, g)), full_head),
        compiler_params=PARAMS,
        name="middle",
    )(mixed, mixed, mixed, vp, starts, ec, gate, og, gain, skip_x)

    ends = swap(scan_states(swap(gt), rates_x, True))

    def cap(j):
        return jnp.minimum(j, GROUPS - 1)

    wide_cap = pl.BlockSpec((length, width), lambda j: (0, cap(j)))
    line_cap = pl.BlockSpec((1, width), lambda j: (0, cap(j)))
    state_cap = pl.BlockSpec((reps, STATE, wide), lambda j: (cap(j), 0, 0))
    eight = pl.BlockSpec((8, width), lambda j: (0, j))
    wide_all = pl.BlockSpec((length, width), lambda j: (0, j))
    gx, edge, wr, grad_dt, hs = pl.pallas_call(
        lambda *refs: back_kernel(per_group, *refs),
        out_shape=(
            jax.ShapeDtypeStruct((length, channels), BF16),
            jax.ShapeDtypeStruct((8, channels), F32),
            jax.ShapeDtypeStruct((8, channels), F32),
            jax.ShapeDtypeStruct((length, heads), F32),
            jax.ShapeDtypeStruct((8, heads), F32),
        ),
        grid=(blocks,),
        in_specs=[
            wide_cap,
            pl.BlockSpec((length, STATE), lambda j: (0, k_at + cap(j))),
            pl.BlockSpec((length, STATE), lambda j: (0, q_at + cap(j))),
            wide_cap, state_cap, state_cap, wide_cap, wide_cap,
            wide_all,
            pl.BlockSpec((HALO, width), lambda j: (0, j)),
            eight, line_cap, line_cap, full_head, full_head, full_head, row_head, row_head,
        ],
        out_specs=(wide_all, eight, eight, full_head, pl.BlockSpec((8, heads), lambda j: (0, 0))),
        scratch_shapes=[
            pltpu.VMEM((PAD + length, width), F32),
            pltpu.VMEM((PAD + length, width), F32),
            pltpu.VMEM((length, width), F32),
            pltpu.VMEM((2, length, width), F32),
            pltpu.VMEM((length, heads), F32),
            pltpu.VMEM((8, heads), F32),
        ],
        compiler_params=PARAMS,
        name="back",
    )(mixed, mixed, mixed, vp, starts, ends, dy, dyp, x, halo, full, skip_x, et, ei, a1, dt, step_b, decay)

    next_gp = lax.ppermute(edge[:HALO], "ctx", behind)
    fixed = []
    for i in range(HALO):
        row = edge[HALO + i]
        for k in range(i + 1):
            row = row + full[k] * next_gp[i - k]
        fixed.append(row)
    grad_xbc = lax.dynamic_update_slice(gx, jnp.stack(fixed).astype(BF16), (length - HALO, 0))

    skip_grad = jnp.sum(rows[1].reshape(heads, HEAD_DIM), axis=1)
    extra_row = pack_row(
        rows[0].reshape(shards, g_loc), hs[0].reshape(shards, h_loc), hs[1].reshape(shards, h_loc),
        skip_grad.reshape(shards, h_loc)).reshape(1, channels)
    parts = jnp.concatenate([wr[: KERNEL + 1], extra_row, jnp.zeros((8 - KERNEL - 2, channels), F32)], axis=0)
    split = ranks // 8
    piece = c_loc // split
    parts = parts.reshape(8, shards, split, piece).transpose(0, 2, 1, 3).reshape(ranks * shards, piece)
    summed = jnp.sum(lax.all_to_all(parts, ("ctx", "fsdp"), 0, 0, tiled=True), axis=0)
    summed = summed * (1.0 / math.sqrt(length * ranks * shards))
    mine = lax.all_gather(summed, "ctx", axis=0, tiled=True).reshape(8, c_loc)
    tail = mine[KERNEL + 1]
    return (
        grad_xbc[None],
        grad_dt[None],
        grad_gate[None],
        mine[:KERNEL],
        mine[KERNEL],
        tail[g_loc : g_loc + h_loc],
        tail[g_loc + h_loc : g_loc + 2 * h_loc],
        tail[g_loc + 2 * h_loc : g_loc + 3 * h_loc],
        tail[:g_loc],
    )


def solution(mesh):
    data = P("fsdp", "ctx", None)
    one = P("fsdp")
    return jax.shard_map(
        body,
        mesh=mesh,
        in_specs=(data, data, data, data, P(None, "fsdp"), one, one, one, one, one),
        out_specs=(data, data, data, P(None, "fsdp"), one, one, one, one, one),
        check_vma=False,
    )
```

```python
import math

import jax
import jax.numpy as jnp
from jax import lax
from jax.experimental import pallas as pl
from jax.experimental.pallas import tpu as pltpu
from jax.sharding import PartitionSpec as P

HEAD_DIM = 64
STATE = 128
GROUPS = 8
KERNEL = 4
EPSILON = 1e-05
HALO = KERNEL - 1
PAD = 8
CHUNKS = 4
F32 = jnp.float32
BF16 = jnp.bfloat16
HIGHEST = lax.Precision.HIGHEST


def mm(a, b):
    return jnp.dot(a, b, preferred_element_type=F32)


def mm_nt(a, b):
    return lax.dot_general(a, b, (((1,), (1,)), ((), ())), preferred_element_type=F32)


def sigmoid(v):
    return 0.5 * jnp.tanh(0.5 * v) + 0.5


def softplus(v):
    return jnp.maximum(v, 0.0) + jnp.log(1.0 + jnp.exp(-jnp.abs(v)))


def spread_heads(table, group, per_group):
    heads = table.shape[1]
    table = pltpu.roll(table, lax.rem(heads - group * per_group, heads), 1)
    rows = table.shape[0]
    pair = 128 // HEAD_DIM
    lane = lax.broadcasted_iota(jnp.int32, (rows, 128), 1)
    tiles = []
    for i in range(per_group // pair):
        tile = jnp.broadcast_to(table[:, pair * i : pair * i + 1], (rows, 128))
        for p in range(1, pair):
            col = jnp.broadcast_to(table[:, pair * i + p : pair * i + p + 1], (rows, 128))
            tile = jnp.where(lane >= p * HEAD_DIM, col, tile)
        tiles.append(tile)
    return jnp.concatenate(tiles, axis=1)


def sum_heads(values, group, per_group, heads):
    width = values.shape[1]
    row = lax.broadcasted_iota(jnp.int32, (width, heads), 0) // HEAD_DIM + group * per_group
    col = lax.broadcasted_iota(jnp.int32, (width, heads), 1)
    pick = jnp.where(row == col, 1.0, 0.0).astype(BF16)
    high = values.astype(BF16)
    low = (values - high.astype(F32)).astype(BF16)
    return mm(high, pick) + mm(low, pick)


def lower_mask(n):
    return lax.broadcasted_iota(jnp.int32, (n, n), 0) >= lax.broadcasted_iota(jnp.int32, (n, n), 1)


def upper_mask(n):
    return lax.broadcasted_iota(jnp.int32, (n, n), 0) <= lax.broadcasted_iota(jnp.int32, (n, n), 1)


def conv_pre(x_ref, halo_ref, w_ref, xs):
    length = x_ref.shape[0]
    xs[PAD - HALO : PAD, :] = halo_ref[...].astype(F32)
    xs[PAD : PAD + length, :] = x_ref[...].astype(F32)
    pre = jnp.broadcast_to(w_ref[KERNEL : KERNEL + 1, :], (length, x_ref.shape[1]))
    for k in range(KERNEL):
        pre = pre + w_ref[k : k + 1, :] * xs[PAD - HALO + k : PAD - HALO + k + length, :]
    return pre


def split_halves(state, mine, own_ref, send_ref):
    half = state.shape[0] // 2
    low, high = state[:half].astype(BF16), state[half:].astype(BF16)
    own_ref[0] = jnp.where(mine == 0, low, high)
    send_ref[0] = jnp.where(mine == 0, high, low)


def join_halves(own_ref, other_ref, mine):
    own, other = own_ref[0], other_ref[0]
    return jnp.concatenate([jnp.where(mine == 0, own, other), jnp.where(mine == 0, other, own)], axis=0)


def front_kernel(per_group, side_ref, x_ref, halo_ref, w_ref, dt_ref, sb_ref, dl_ref,
                 mixed_ref, vp_ref, own_ref, send_ref, ec_ref, ei_ref, et_ref, xs, ks):
    j = pl.program_id(0)
    length = x_ref.shape[0]

    @pl.when(j == 0)
    def _():
        step = softplus(dt_ref[...].astype(F32) + sb_ref[...])
        ld = -jnp.exp(dl_ref[...]) * step
        tril = jnp.where(lower_mask(length), 1.0, 0.0).astype(F32)
        cum = jnp.dot(tril, ld, precision=HIGHEST, preferred_element_type=F32)
        ec_ref[...] = jnp.exp(cum)
        ei_ref[...] = jnp.exp(-cum) * step

    pre = conv_pre(x_ref, halo_ref, w_ref, xs)
    mixed = (pre * sigmoid(pre)).astype(BF16)
    mixed_ref[...] = mixed

    @pl.when(j == 0)
    def _():
        for g in range(GROUPS):
            ks[g] = mixed[:, g * STATE : (g + 1) * STATE]

    @pl.when(j >= 2)
    def _():
        g = j - 2
        eix = spread_heads(ei_ref[...], g, per_group)
        vp = (mixed.astype(F32) * eix).astype(BF16)
        vp_ref[...] = vp
        et = spread_heads(ec_ref[length - 8 : length, :], g, per_group)[7:8, :]
        et_ref[...] = et
        ut = mm(ks[g].astype(F32).T.astype(BF16), vp) * et
        split_halves(ut, side_ref[0], own_ref, send_ref)


def middle_kernel(per_group, side_ref, v_ref, k_ref, q_ref, vp_ref, so_ref, st_ref, ec_ref, gate_ref, og_ref, gain_ref, skip_ref,
                  dy_ref, dyp_ref, gg_ref, own_ref, send_ref, rows_ref, a1_ref):
    g = pl.program_id(0)
    length, width = v_ref.shape
    heads = ec_ref.shape[1]
    q = q_ref[...]
    z = jnp.where(lower_mask(length), mm_nt(q, k_ref[...]), 0.0).astype(BF16)
    yn = mm(jnp.concatenate([z, q], axis=1), jnp.concatenate([vp_ref[...], join_halves(so_ref, st_ref, side_ref[0])], axis=0))
    ecx = spread_heads(ec_ref[...], g, per_group)
    v = v_ref[...].astype(F32)
    y = (ecx * yn + skip_ref[...] * v).astype(BF16).astype(F32)
    gate = gate_ref[...].astype(F32)
    og = og_ref[...].astype(F32)
    sig = sigmoid(gate)
    act = gate * sig
    gated = y * act
    scale = lax.rsqrt(jnp.sum(gated * gated, axis=1, keepdims=True) * (1.0 / width) + EPSILON)
    dgn = og * gain_ref[...]
    inner = jnp.sum(dgn * gated, axis=1, keepdims=True) * (1.0 / width)
    dgated = scale * dgn - gated * (scale * scale * scale * inner)
    dyb = (dgated * act).astype(BF16)
    dy_ref[...] = dyb
    gg_ref[...] = (dgated * y * (sig + act * (1.0 - sig))).astype(BF16)
    dy = dyb.astype(F32)
    dyp = (ecx * dy).astype(BF16)
    dyp_ref[...] = dyp
    gt = mm(q.astype(F32).T.astype(BF16), dyp)
    split_halves(gt, side_ref[1], own_ref, send_ref)
    rows_ref[...] = jnp.zeros(rows_ref.shape, F32)
    rows_ref[0:1, :] = jnp.sum(og * gated * scale, axis=0, keepdims=True)
    rows_ref[1:2, :] = jnp.sum(dy * v, axis=0, keepdims=True)

    @pl.when(g == 0)
    def _():
        a1_ref[...] = jnp.zeros(a1_ref.shape, F32)

    a1_ref[...] += sum_heads(dyp.astype(F32) * yn, g, per_group, heads)


def back_kernel(per_group, side_ref, v_ref, k_ref, q_ref, vp_ref, so_ref, st_ref, eo_ref, en_ref, dy_ref, dyp_ref, x_ref, halo_ref, w_ref,
                skip_ref, et_ref, ei_ref, a1_ref, dt_ref, sb_ref, dl_ref,
                gx_ref, edge_ref, wr_ref, gdt_ref, hs_ref, xs, gs, gm, dkq, a2, last):
    j = pl.program_id(0)
    length, width = v_ref.shape
    heads = ei_ref.shape[1]

    @pl.when(j == 0)
    def _():
        a2[...] = jnp.zeros(a2.shape, F32)
        last[...] = jnp.zeros(last.shape, F32)
        gs[length:, :] = jnp.zeros((gs.shape[0] - length, gs.shape[1]), F32)

    @pl.when(j < GROUPS)
    def _():
        k = k_ref[...]
        q = q_ref[...]
        vp = vp_ref[...]
        dyp = dyp_ref[...]
        st = join_halves(so_ref, st_ref, side_ref[0])
        en = (et_ref[...] * join_halves(eo_ref, en_ref, side_ref[1]).astype(F32)).astype(BF16)
        low = lower_mask(length)
        zt = jnp.where(upper_mask(length), mm_nt(k, q), 0.0).astype(BF16)
        dvp = mm(jnp.concatenate([zt, k], axis=1), jnp.concatenate([dyp, en], axis=0))
        eix = spread_heads(ei_ref[...], j, per_group)
        gm[...] = eix * dvp + skip_ref[...] * dy_ref[...].astype(F32)
        a2[...] += sum_heads(vp.astype(F32) * dvp, j, per_group, heads)
        ends = en.astype(F32) * (st.astype(F32) + mm(k.astype(F32).T.astype(BF16), vp))
        ends = jnp.broadcast_to(jnp.sum(ends, axis=0, keepdims=True), (8, width))
        last[...] += sum_heads(ends, j, per_group, heads)
        dz = jnp.where(low, mm_nt(dyp, vp), 0.0)
        dzb = dz.astype(BF16)
        cols = pl.ds(pl.multiple_of(j * STATE, STATE), STATE)
        dkq[0, :, cols] = mm(dz.T.astype(BF16), q) + mm_nt(vp, en)
        dkq[1, :, cols] = mm(dzb, k) + mm_nt(dyp, st)

    @pl.when(j >= GROUPS)
    def _():
        gm[...] = dkq[j - GROUPS]

    pre = conv_pre(x_ref, halo_ref, w_ref, xs)
    sig = sigmoid(pre)
    gp = gm[...] * (sig * (1.0 + pre * (1.0 - sig)))
    gs[0:length, :] = gp
    wr_ref[...] = jnp.zeros(wr_ref.shape, F32)
    total = jnp.zeros(gp.shape, F32)
    for k in range(KERNEL):
        lead = HALO - k
        total = total + w_ref[k : k + 1, :] * gs[lead : lead + length, :]
        wr_ref[k : k + 1, :] = jnp.sum(gp * xs[PAD - HALO + k : PAD - HALO + k + length, :], axis=0, keepdims=True)
    wr_ref[KERNEL : KERNEL + 1, :] = jnp.sum(gp, axis=0, keepdims=True)
    gx_ref[...] = total.astype(BF16)
    edge_ref[...] = jnp.zeros(edge_ref.shape, F32)
    edge_ref[0:HALO, :] = gp[0:HALO, :]
    edge_ref[HALO : 2 * HALO, :] = total[length - HALO : length, :]

    @pl.when(j == pl.num_programs(0) - 1)
    def _():
        raw = dt_ref[...].astype(F32) + sb_ref[...]
        step = softplus(raw)
        rate = jnp.exp(dl_ref[...])
        row = lax.broadcasted_iota(jnp.int32, (length, heads), 0)
        dcum = a1_ref[...] - a2[...] + jnp.where(row == length - 1, last[0:1, :], 0.0)
        triu = jnp.where(upper_mask(length), 1.0, 0.0).astype(F32)
        dld = jnp.dot(triu, dcum, precision=HIGHEST, preferred_element_type=F32)
        gdt = (a2[...] / step - rate * dld) * sigmoid(raw)
        gdt_ref[...] = gdt
        hs_ref[...] = jnp.zeros(hs_ref.shape, F32)
        hs_ref[0:1, :] = jnp.sum(-rate * step * dld, axis=0, keepdims=True)
        hs_ref[1:2, :] = jnp.sum(gdt, axis=0, keepdims=True)


PARAMS = pltpu.CompilerParams(vmem_limit_bytes=48 * 1024 * 1024)


def grid_call(kernel, name, steps, in_specs, out_specs, out_shape, scratch=()):
    return pl.pallas_call(
        kernel,
        out_shape=out_shape,
        grid_spec=pltpu.PrefetchScalarGridSpec(
            num_scalar_prefetch=1, grid=(steps,), in_specs=in_specs, out_specs=out_specs, scratch_shapes=scratch),
        compiler_params=PARAMS,
        name=name,
    )


def hop_kernel(has_carry, at_ref, own_ref, got_ref, mine_ref, pair_ref, *refs):
    if has_carry:
        carry_ref, next_ref, give_ref, keep_ref = refs
        carry = carry_ref[...].astype(F32)
    else:
        next_ref, give_ref, keep_ref = refs
        carry = jnp.zeros(got_ref.shape, F32)
    first = at_ref[1] == 0
    own, got = own_ref[0].astype(F32), got_ref[...].astype(F32)
    mine, pair = mine_ref[...], pair_ref[...]
    inner = jnp.where(first, mine, pair) * carry + jnp.where(first, own, got)
    next_ref[...] = (jnp.where(first, pair, mine) * inner + jnp.where(first, got, own)).astype(BF16)
    give_ref[...] = jnp.where(first, inner, carry).astype(BF16)
    keep_ref[...] = jnp.where(first, carry, inner).astype(BF16)


def in_hbm(value):
    return pltpu.with_memory_space_constraint(value, pltpu.HBM)


def chain_states(own, send, rate, pair_rate, flip):
    count, rows, lanes = own.shape
    ranks = lax.axis_size("ctx")
    depth = ranks // 2
    rank = lax.axis_index("ctx")
    rank = ranks - 1 - rank if flip else rank
    side, place = rank % 2, rank // 2
    steps = count + depth - 1
    tile = lanes // 2

    def physical(r):
        return ranks - 1 - r if flip else r

    def live(s):
        return [z for z in range(depth) if 0 <= s - z < count]

    def swap(value, s):
        pairs = [(physical(2 * z + p), physical(2 * z + 1 - p)) for z in live(s) for p in range(2)]
        return lax.ppermute(value, "ctx", pairs)

    def up(value, s):
        pairs = [(physical(2 * z + p), physical(2 * z + 2 + p)) for z in live(s) if z + 1 < depth for p in range(2)]
        return lax.ppermute(value, "ctx", pairs) if pairs else None

    got = [
        swap(lax.dynamic_index_in_dim(send, jnp.clip(s - place, 0, count - 1), 0, keepdims=False), s)
        for s in range(steps)
    ]
    per = lanes // tile
    flat = pl.BlockSpec((rows, tile), lambda i, at: (0, i))
    line = pl.BlockSpec((1, tile), lambda i, at: (0, at[0] * per + i))
    read = pl.BlockSpec((1, rows, tile), lambda i, at: (at[0], 0, i))
    chunk_shape = jax.ShapeDtypeStruct((rows, lanes), BF16)
    keeps, backs = [], []
    carry = None
    for s in range(steps):
        has_carry = s > 0
        at = jnp.stack([jnp.clip(s - place, 0, count - 1), side]).astype(jnp.int32)
        after, give, keep = pl.pallas_call(
            lambda *refs, has_carry=has_carry: hop_kernel(has_carry, *refs),
            out_shape=(chunk_shape,) * 3,
            grid_spec=pltpu.PrefetchScalarGridSpec(
                num_scalar_prefetch=1,
                grid=(per,),
                in_specs=[read, flat, line, line] + [flat] * has_carry,
                out_specs=[flat] * 3,
            ),
            compiler_params=PARAMS,
            name="hop",
        )(at, in_hbm(own), in_hbm(got[s]), rate, pair_rate, *([in_hbm(carry)] if has_carry else []))
        keeps.append(keep)
        carry = up(after, s)
        backs.append(swap(give, s))
    return jnp.stack(keeps), jnp.stack(backs)


def body(proj_xbc, proj_dt, proj_gate, out_grad, conv_weight, conv_bias, decay_log, step_bias, skip_gain, norm_gain):
    x, dt, gate, og = proj_xbc[0], proj_dt[0], proj_gate[0], out_grad[0]
    length, channels = x.shape
    heads = dt.shape[1]
    inner = heads * HEAD_DIM
    ranks = lax.axis_size("ctx")
    shards = lax.axis_size("fsdp")
    per_group = heads // GROUPS
    width = per_group * HEAD_DIM
    side = lax.axis_index("ctx") % 2
    place = lax.axis_index("ctx") // 2
    sides = jnp.stack([side, 1 - side, place, ranks // 2 - 1 - place]).astype(jnp.int32)
    part = inner // CHUNKS
    per = part // width
    c_loc, g_loc, h_loc = channels // shards, inner // shards, heads // shards
    spare = c_loc - g_loc - 3 * h_loc
    groups = GROUPS
    blocks = channels // width

    ahead = [(i, i + 1) for i in range(ranks - 1)]
    behind = [(i + 1, i) for i in range(ranks - 1)]
    halo = lax.ppermute(x[length - HALO :, :], "ctx", ahead)

    def pack_row(gain, decay, step, skip):
        return jnp.concatenate([gain, decay, step, skip, jnp.zeros(gain.shape[:-1] + (spare,), F32)], axis=-1)

    packed = jnp.concatenate(
        [conv_weight, conv_bias[None], pack_row(norm_gain, decay_log, step_bias, skip_gain)[None],
         jnp.zeros((8 - KERNEL - 2, c_loc), F32)], axis=0)
    full = lax.all_gather(packed, "fsdp", axis=1, tiled=True)
    extra = full[KERNEL + 1].reshape(shards, c_loc)
    gain = extra[:, :g_loc].reshape(1, inner)
    decay = extra[:, g_loc : g_loc + h_loc].reshape(1, heads)
    step_b = extra[:, g_loc + h_loc : g_loc + 2 * h_loc].reshape(1, heads)
    skip = extra[:, g_loc + 2 * h_loc : g_loc + 3 * h_loc].reshape(1, heads)
    skip_x = jnp.repeat(skip, HEAD_DIM, axis=1)

    def col(j):
        return jnp.where(j < 2, groups + j, j - 2)

    def grp(j):
        return jnp.maximum(j - 2, 0)

    full_head = pl.BlockSpec((length, heads), lambda j, at: (0, 0))
    row_head = pl.BlockSpec((1, heads), lambda j, at: (0, 0))
    state_shape = jax.ShapeDtypeStruct((CHUNKS, STATE // 2, part), BF16)
    mixed, vp, own, send, ec, ei, et = grid_call(
        lambda *refs: front_kernel(per_group, *refs), "front", blocks,
        out_shape=(
            jax.ShapeDtypeStruct((length, channels), BF16),
            jax.ShapeDtypeStruct((length, inner), BF16),
            state_shape,
            state_shape,
            jax.ShapeDtypeStruct((length, heads), F32),
            jax.ShapeDtypeStruct((length, heads), F32),
            jax.ShapeDtypeStruct((1, inner), F32),
        ),
        in_specs=[
            pl.BlockSpec((length, width), lambda j, at: (0, col(j))),
            pl.BlockSpec((HALO, width), lambda j, at: (0, col(j))),
            pl.BlockSpec((8, width), lambda j, at: (0, col(j))),
            full_head, row_head, row_head,
        ],
        out_specs=(
            pl.BlockSpec((length, width), lambda j, at: (0, col(j))),
            pl.BlockSpec((length, width), lambda j, at: (0, grp(j))),
            pl.BlockSpec((1, STATE // 2, width), lambda j, at: (grp(j) // per, 0, lax.rem(grp(j), per))),
            pl.BlockSpec((1, STATE // 2, width), lambda j, at: (grp(j) // per, 0, lax.rem(grp(j), per))),
            full_head, full_head,
            pl.BlockSpec((1, width), lambda j, at: (0, grp(j))),
        ),
        scratch=[pltpu.VMEM((PAD + length, width), F32), pltpu.VMEM((GROUPS, length, STATE), BF16)],
    )(sides, x, halo, full, dt, step_b, decay)

    pair_et = lax.ppermute(et, "ctx", [(i, i ^ 1) for i in range(ranks)])
    starts = chain_states(own, send, et, pair_et, False)

    wide_spec = pl.BlockSpec((length, width), lambda g, at: (0, g))
    line_spec = pl.BlockSpec((1, width), lambda g, at: (0, g))
    k_at = inner // STATE
    q_at = k_at + GROUPS
    half = (1, STATE // 2, width)
    state_spec = pl.BlockSpec(half, lambda g, at: (at[2] + g // per, 0, lax.rem(g, per)))
    grad_spec = pl.BlockSpec(half, lambda g, at: (g // per, 0, lax.rem(g, per)))
    dy, dyp, grad_gate, own, send, sums, a1 = grid_call(
        lambda *refs: middle_kernel(per_group, *refs), "middle", GROUPS,
        out_shape=(
            jax.ShapeDtypeStruct((length, inner), BF16),
            jax.ShapeDtypeStruct((length, inner), BF16),
            jax.ShapeDtypeStruct((length, inner), BF16),
            state_shape,
            state_shape,
            jax.ShapeDtypeStruct((8, inner), F32),
            jax.ShapeDtypeStruct((length, heads), F32),
        ),
        in_specs=[
            wide_spec,
            pl.BlockSpec((length, STATE), lambda g, at: (0, k_at + g)),
            pl.BlockSpec((length, STATE), lambda g, at: (0, q_at + g)),
            wide_spec, state_spec, state_spec, full_head, wide_spec, wide_spec, line_spec, line_spec,
        ],
        out_specs=(wide_spec, wide_spec, wide_spec, grad_spec, grad_spec, pl.BlockSpec((8, width), lambda g, at: (0, g)), full_head),
    )(sides, mixed, mixed, mixed, vp, *starts, ec, gate, og, gain, skip_x)

    ends = chain_states(own, send, et, pair_et, True)

    def cap(j):
        return jnp.minimum(j, GROUPS - 1)

    wide_cap = pl.BlockSpec((length, width), lambda j, at: (0, cap(j)))
    line_cap = pl.BlockSpec((1, width), lambda j, at: (0, cap(j)))
    start_cap = pl.BlockSpec(half, lambda j, at: (at[2] + cap(j) // per, 0, lax.rem(cap(j), per)))
    end_cap = pl.BlockSpec(half, lambda j, at: (at[3] + cap(j) // per, 0, lax.rem(cap(j), per)))
    eight = pl.BlockSpec((8, width), lambda j, at: (0, j))
    wide_all = pl.BlockSpec((length, width), lambda j, at: (0, j))
    gx, edge, wr, grad_dt, hs = grid_call(
        lambda *refs: back_kernel(per_group, *refs), "back", blocks,
        out_shape=(
            jax.ShapeDtypeStruct((length, channels), BF16),
            jax.ShapeDtypeStruct((8, channels), F32),
            jax.ShapeDtypeStruct((8, channels), F32),
            jax.ShapeDtypeStruct((length, heads), F32),
            jax.ShapeDtypeStruct((8, heads), F32),
        ),
        in_specs=[
            wide_cap,
            pl.BlockSpec((length, STATE), lambda j, at: (0, k_at + cap(j))),
            pl.BlockSpec((length, STATE), lambda j, at: (0, q_at + cap(j))),
            wide_cap, start_cap, start_cap, end_cap, end_cap, wide_cap, wide_cap,
            wide_all,
            pl.BlockSpec((HALO, width), lambda j, at: (0, j)),
            eight, line_cap, line_cap, full_head, full_head, full_head, row_head, row_head,
        ],
        out_specs=(wide_all, eight, eight, full_head, pl.BlockSpec((8, heads), lambda j, at: (0, 0))),
        scratch=[
            pltpu.VMEM((PAD + length, width), F32),
            pltpu.VMEM((PAD + length, width), F32),
            pltpu.VMEM((length, width), F32),
            pltpu.VMEM((2, length, width), F32),
            pltpu.VMEM((length, heads), F32),
            pltpu.VMEM((8, heads), F32),
        ],
    )(sides, mixed, mixed, mixed, vp, *starts, *ends, dy, dyp, x, halo, full, skip_x, et, ei, a1, dt, step_b, decay)

    next_gp = lax.ppermute(edge[:HALO], "ctx", behind)
    fixed = []
    for i in range(HALO):
        row = edge[HALO + i]
        for k in range(i + 1):
            row = row + full[k] * next_gp[i - k]
        fixed.append(row)
    grad_xbc = lax.dynamic_update_slice(gx, jnp.stack(fixed).astype(BF16), (length - HALO, 0))

    skip_grad = jnp.sum(sums[1].reshape(heads, HEAD_DIM), axis=1)
    extra_row = pack_row(
        sums[0].reshape(shards, g_loc), hs[0].reshape(shards, h_loc), hs[1].reshape(shards, h_loc),
        skip_grad.reshape(shards, h_loc)).reshape(1, channels)
    parts = jnp.concatenate([wr[: KERNEL + 1], extra_row, jnp.zeros((8 - KERNEL - 2, channels), F32)], axis=0)
    split = ranks // 8
    piece = c_loc // split
    parts = parts.reshape(8, shards, split, piece).transpose(0, 2, 1, 3).reshape(ranks * shards, piece)
    summed = jnp.sum(lax.all_to_all(parts, ("ctx", "fsdp"), 0, 0, tiled=True), axis=0)
    summed = summed * (1.0 / math.sqrt(length * ranks * shards))
    copies = jnp.broadcast_to(summed[None], (ranks, piece))
    mine = lax.all_to_all(copies, "ctx", 0, 0, tiled=True).reshape(8, c_loc)
    tail = mine[KERNEL + 1]
    return (
        grad_xbc[None],
        grad_dt[None],
        grad_gate[None],
        mine[:KERNEL],
        mine[KERNEL],
        tail[g_loc : g_loc + h_loc],
        tail[g_loc + h_loc : g_loc + 2 * h_loc],
        tail[g_loc + 2 * h_loc : g_loc + 3 * h_loc],
        tail[:g_loc],
    )


def solution(mesh):
    data = P("fsdp", "ctx", None)
    one = P("fsdp")
    return jax.shard_map(
        body,
        mesh=mesh,
        in_specs=(data, data, data, data, P(None, "fsdp"), one, one, one, one, one),
        out_specs=(data, data, data, P(None, "fsdp"), one, one, one, one, one),
        check_vma=False,
    )
```

```python
import math

import jax
import jax.numpy as jnp
from jax import lax
from jax.experimental import pallas as pl
from jax.experimental.pallas import tpu as pltpu
from jax.sharding import PartitionSpec as P

HEAD_DIM = 64
STATE = 128
GROUPS = 8
KERNEL = 4
EPSILON = 1e-05
HALO = KERNEL - 1
PAD = 8
CHUNKS = 4
F32 = jnp.float32
BF16 = jnp.bfloat16
HIGHEST = lax.Precision.HIGHEST


def mm(a, b):
    return jnp.dot(a, b, preferred_element_type=F32)


def mm_nt(a, b):
    return lax.dot_general(a, b, (((1,), (1,)), ((), ())), preferred_element_type=F32)


def sigmoid(v):
    return 0.5 * jnp.tanh(0.5 * v) + 0.5


def softplus(v):
    return jnp.maximum(v, 0.0) + jnp.log(1.0 + jnp.exp(-jnp.abs(v)))


def spread_heads(table, group, per_group):
    heads = table.shape[1]
    table = pltpu.roll(table, lax.rem(heads - group * per_group, heads), 1)
    rows = table.shape[0]
    pair = 128 // HEAD_DIM
    lane = lax.broadcasted_iota(jnp.int32, (rows, 128), 1)
    tiles = []
    for i in range(per_group // pair):
        tile = jnp.broadcast_to(table[:, pair * i : pair * i + 1], (rows, 128))
        for p in range(1, pair):
            col = jnp.broadcast_to(table[:, pair * i + p : pair * i + p + 1], (rows, 128))
            tile = jnp.where(lane >= p * HEAD_DIM, col, tile)
        tiles.append(tile)
    return jnp.concatenate(tiles, axis=1)


def sum_heads(values, group, per_group, heads):
    width = values.shape[1]
    row = lax.broadcasted_iota(jnp.int32, (width, heads), 0) // HEAD_DIM + group * per_group
    col = lax.broadcasted_iota(jnp.int32, (width, heads), 1)
    pick = jnp.where(row == col, 1.0, 0.0).astype(BF16)
    high = values.astype(BF16)
    low = (values - high.astype(F32)).astype(BF16)
    return mm(high, pick) + mm(low, pick)


def lower_mask(n):
    return lax.broadcasted_iota(jnp.int32, (n, n), 0) >= lax.broadcasted_iota(jnp.int32, (n, n), 1)


def upper_mask(n):
    return lax.broadcasted_iota(jnp.int32, (n, n), 0) <= lax.broadcasted_iota(jnp.int32, (n, n), 1)


def conv_pre(x_ref, halo_ref, w_ref, xs):
    length = x_ref.shape[0]
    xs[PAD - HALO : PAD, :] = halo_ref[...].astype(F32)
    xs[PAD : PAD + length, :] = x_ref[...].astype(F32)
    pre = jnp.broadcast_to(w_ref[KERNEL : KERNEL + 1, :], (length, x_ref.shape[1]))
    for k in range(KERNEL):
        pre = pre + w_ref[k : k + 1, :] * xs[PAD - HALO + k : PAD - HALO + k + length, :]
    return pre


def split_halves(state, mine, own_ref, send_ref):
    half = state.shape[0] // 2
    low, high = state[:half].astype(BF16), state[half:].astype(BF16)
    shape = own_ref.shape
    own_ref[...] = jnp.where(mine == 0, low, high).reshape(shape)
    send_ref[...] = jnp.where(mine == 0, high, low).reshape(shape)


def keys_kernel(per_group, x_ref, halo_ref, w_ref, dt_ref, sb_ref, dl_ref, kq_ref, ec_ref, ei_ref, et_ref, xs):
    length = x_ref.shape[0]

    @pl.when(pl.program_id(0) == 0)
    def _():
        step = softplus(dt_ref[...].astype(F32) + sb_ref[...])
        ld = -jnp.exp(dl_ref[...]) * step
        tril = jnp.where(lower_mask(length), 1.0, 0.0).astype(F32)
        cum = jnp.dot(tril, ld, precision=HIGHEST, preferred_element_type=F32)
        ec = jnp.exp(cum)
        ec_ref[...] = ec
        ei_ref[...] = jnp.exp(-cum) * step
        width = per_group * HEAD_DIM
        for g in range(GROUPS):
            et_ref[:, g * width : (g + 1) * width] = spread_heads(ec[length - 8 :, :], g, per_group)[7:8, :]

    pre = conv_pre(x_ref, halo_ref, w_ref, xs)
    kq_ref[...] = (pre * sigmoid(pre)).astype(BF16)


def front_kernel(per_group, first, x_ref, halo_ref, w_ref, k_ref, ei_ref, et_ref,
                 side_ref, mixed_ref, vp_ref, own_ref, send_ref, xs):
    g = first + pl.program_id(0)
    pre = conv_pre(x_ref, halo_ref, w_ref, xs)
    mixed = (pre * sigmoid(pre)).astype(BF16)
    mixed_ref[...] = mixed
    vp = (mixed.astype(F32) * spread_heads(ei_ref[...], g, per_group)).astype(BF16)
    vp_ref[...] = vp
    ut = mm(k_ref[...].astype(F32).T.astype(BF16), vp) * et_ref[...]
    split_halves(ut, side_ref[0], own_ref, send_ref)


def choose(refs, pick):
    value = refs[0][...]
    for i in range(1, len(refs)):
        value = jnp.where(pick == i, refs[i][...], value)
    return value


def join_halves(own, other, mine):
    return jnp.concatenate([jnp.where(mine == 0, own, other), jnp.where(mine == 0, other, own)], axis=0)


def middle_kernel(per_group, first, depth, v_ref, k_ref, q_ref, vp_ref, ec_ref, gate_ref, og_ref, gain_ref, skip_ref,
                  side_ref, *refs):
    keeps, backs = refs[:depth], refs[depth : 2 * depth]
    dy_ref, dyp_ref, st_ref, own_ref, send_ref, a1_ref, gg_ref, rows_ref = refs[2 * depth :]
    st = join_halves(choose(keeps, side_ref[2]), choose(backs, side_ref[2]), side_ref[0])
    st_ref[...] = st
    g = first + pl.program_id(0)
    length, width = v_ref.shape
    heads = ec_ref.shape[1]
    q = q_ref[...]
    z = jnp.where(lower_mask(length), mm_nt(q, k_ref[...]), 0.0).astype(BF16)
    yn = mm(jnp.concatenate([z, q], axis=1), jnp.concatenate([vp_ref[...], st], axis=0))
    ecx = spread_heads(ec_ref[...], g, per_group)
    v = v_ref[...].astype(F32)
    y = (ecx * yn + skip_ref[...] * v).astype(BF16).astype(F32)
    gate = gate_ref[...].astype(F32)
    og = og_ref[...].astype(F32)
    sig = sigmoid(gate)
    act = gate * sig
    gated = y * act
    scale = lax.rsqrt(jnp.sum(gated * gated, axis=1, keepdims=True) * (1.0 / width) + EPSILON)
    dgn = og * gain_ref[...]
    inner = jnp.sum(dgn * gated, axis=1, keepdims=True) * (1.0 / width)
    dgated = scale * dgn - gated * (scale * scale * scale * inner)
    dyb = (dgated * act).astype(BF16)
    dy_ref[...] = dyb
    gg_ref[...] = (dgated * y * (sig + act * (1.0 - sig))).astype(BF16)
    dy = dyb.astype(F32)
    dyp = (ecx * dy).astype(BF16)
    dyp_ref[...] = dyp
    gt = mm(q.astype(F32).T.astype(BF16), dyp)
    split_halves(gt, side_ref[1], own_ref, send_ref)
    rows_ref[...] = jnp.zeros(rows_ref.shape, F32)
    rows_ref[0:1, :] = jnp.sum(og * gated * scale, axis=0, keepdims=True)
    rows_ref[1:2, :] = jnp.sum(dy * v, axis=0, keepdims=True)

    @pl.when(pl.program_id(0) == 0)
    def _():
        a1_ref[...] = jnp.zeros(a1_ref.shape, F32)

    a1_ref[...] += sum_heads(dyp.astype(F32) * yn, g, per_group, heads)


def conv_back(grads, x_ref, halo_ref, w_ref, gx_ref, edge_ref, wr_ref, xs, gs):
    length = x_ref.shape[0]
    pre = conv_pre(x_ref, halo_ref, w_ref, xs)
    sig = sigmoid(pre)
    gp = grads * (sig * (1.0 + pre * (1.0 - sig)))
    gs[0:length, :] = gp
    gs[length:, :] = jnp.zeros((gs.shape[0] - length, gs.shape[1]), F32)
    wr_ref[...] = jnp.zeros(wr_ref.shape, F32)
    total = jnp.zeros(gp.shape, F32)
    for k in range(KERNEL):
        lead = HALO - k
        total = total + w_ref[k : k + 1, :] * gs[lead : lead + length, :]
        wr_ref[k : k + 1, :] = jnp.sum(gp * xs[PAD - HALO + k : PAD - HALO + k + length, :], axis=0, keepdims=True)
    wr_ref[KERNEL : KERNEL + 1, :] = jnp.sum(gp, axis=0, keepdims=True)
    gx_ref[...] = total.astype(BF16)
    edge_ref[...] = jnp.zeros(edge_ref.shape, F32)
    edge_ref[0:HALO, :] = gp[0:HALO, :]
    edge_ref[HALO : 2 * HALO, :] = total[length - HALO : length, :]


def back_kernel(per_group, first, depth, k_ref, q_ref, vp_ref, st_ref, dy_ref, dyp_ref, x_ref, halo_ref, w_ref,
                skip_ref, et_ref, ei_ref, side_ref, *refs):
    keeps, backs = refs[:depth], refs[depth : 2 * depth]
    dkq_ref, a2_ref, last_ref, gx_ref, edge_ref, wr_ref, xs, gs = refs[2 * depth :]
    j = first + pl.program_id(0)
    length, width = x_ref.shape
    heads = ei_ref.shape[1]

    @pl.when(pl.program_id(0) == 0)
    def _():
        a2_ref[...] = jnp.zeros(a2_ref.shape, F32)
        last_ref[...] = jnp.zeros(last_ref.shape, F32)

    k = k_ref[...]
    q = q_ref[...]
    vp = vp_ref[...]
    dyp = dyp_ref[...]
    st = st_ref[...]
    en = join_halves(choose(keeps, side_ref[3]), choose(backs, side_ref[3]), side_ref[1])
    en = (et_ref[...] * en.astype(F32)).astype(BF16)
    zt = jnp.where(upper_mask(length), mm_nt(k, q), 0.0).astype(BF16)
    dvp = mm(jnp.concatenate([zt, k], axis=1), jnp.concatenate([dyp, en], axis=0))
    grads = spread_heads(ei_ref[...], j, per_group) * dvp + skip_ref[...] * dy_ref[...].astype(F32)
    a2_ref[...] += sum_heads(vp.astype(F32) * dvp, j, per_group, heads)
    ends = en.astype(F32) * (st.astype(F32) + mm(k.astype(F32).T.astype(BF16), vp))
    ends = jnp.broadcast_to(jnp.sum(ends, axis=0, keepdims=True), (8, width))
    last_ref[...] += sum_heads(ends, j, per_group, heads)
    dz = jnp.where(lower_mask(length), mm_nt(dyp, vp), 0.0)
    dkq_ref[0] = mm(dz.T.astype(BF16), q) + mm_nt(vp, en)
    dkq_ref[1] = mm(dz.astype(BF16), k) + mm_nt(dyp, st)
    conv_back(grads, x_ref, halo_ref, w_ref, gx_ref, edge_ref, wr_ref, xs, gs)


def last_kernel(count, x_ref, halo_ref, w_ref, dt_ref, sb_ref, dl_ref, *refs):
    dkq, a1, a2, last = (refs[i * count : (i + 1) * count] for i in range(4))
    gdt_ref, hs_ref, gx_ref, edge_ref, wr_ref, xs, gs = refs[4 * count :]
    grads = jnp.concatenate([ref[0] for ref in dkq], axis=1)
    conv_back(grads, x_ref, halo_ref, w_ref, gx_ref, edge_ref, wr_ref, xs, gs)

    @pl.when(pl.program_id(0) == 0)
    def _():
        length, heads = dt_ref.shape
        raw = dt_ref[...].astype(F32) + sb_ref[...]
        step = softplus(raw)
        rate = jnp.exp(dl_ref[...])
        row = lax.broadcasted_iota(jnp.int32, (length, heads), 0)
        down = sum(ref[...] for ref in a2)
        end = sum(ref[...] for ref in last)[0:1, :]
        dcum = sum(ref[...] for ref in a1) - down + jnp.where(row == length - 1, end, 0.0)
        triu = jnp.where(upper_mask(length), 1.0, 0.0).astype(F32)
        dld = jnp.dot(triu, dcum, precision=HIGHEST, preferred_element_type=F32)
        gdt = (down / step - rate * dld) * sigmoid(raw)
        gdt_ref[...] = gdt
        hs_ref[...] = jnp.zeros(hs_ref.shape, F32)
        hs_ref[0:1, :] = jnp.sum(-rate * step * dld, axis=0, keepdims=True)
        hs_ref[1:2, :] = jnp.sum(gdt, axis=0, keepdims=True)


PARAMS = pltpu.CompilerParams(vmem_limit_bytes=40 * 1024 * 1024)


def grid_call(kernel, name, steps, in_specs, out_specs, out_shape, scratch=(), into=()):
    given = len(in_specs)
    anywhere = pl.BlockSpec(memory_space=pl.ANY)

    def place(s):
        return s if s.shape[0] == STATE // 2 else pltpu.HBM(s.shape, s.dtype)

    call = pl.pallas_call(
        lambda *refs: kernel(*refs[:given], *refs[given + len(into) :]),
        out_shape=tuple(place(s) for s in out_shape),
        grid=(steps,),
        in_specs=[*in_specs, *[anywhere] * len(into)],
        out_specs=out_specs,
        scratch_shapes=scratch,
        input_output_aliases={given + i: len(out_shape) - len(into) + i for i in range(len(into))},
        compiler_params=PARAMS,
        name=name,
    )

    def run(*values):
        kept = [v if s.memory_space == pltpu.SMEM or v.shape[0] == STATE // 2 else in_hbm(v)
                for v, s in zip(values, in_specs, strict=True)]
        return call(*kept, *[in_hbm(v) for v in into])

    return run


def hop_kernel(has_carry, choices, chunk, side, mine_ref, pair_ref, *refs):
    own, got = choose(refs[:choices], chunk), choose(refs[choices : 2 * choices], chunk)
    refs = refs[2 * choices :]
    if has_carry:
        carry_ref, next_ref, give_ref, keep_ref = refs
        carry = carry_ref[...].astype(F32)
    else:
        next_ref, give_ref, keep_ref = refs
        carry = jnp.zeros(next_ref.shape, F32)
    first = side == 0
    own, got = own.astype(F32), got.astype(F32)
    mine, pair = mine_ref[...], pair_ref[...]
    inner = jnp.where(first, mine, pair) * carry + jnp.where(first, own, got)
    next_ref[...] = (jnp.where(first, pair, mine) * inner + jnp.where(first, got, own)).astype(BF16)
    give_ref[...] = jnp.where(first, inner, carry).astype(BF16)
    keep_ref[...] = jnp.where(first, carry, inner).astype(BF16)


def in_hbm(value):
    return pltpu.with_memory_space_constraint(value, pltpu.HBM)


class Chain:
    def __init__(self, count, rates, sides, flip):
        self.count, self.rates, self.sides, self.flip = count, rates, sides, flip
        self.ranks = lax.axis_size("ctx")
        self.depth = self.ranks // 2
        self.steps = count + self.depth - 1
        self.carry = None

    def physical(self, r):
        return self.ranks - 1 - r if self.flip else r

    def live(self, s):
        return [z for z in range(self.depth) if 0 <= s - z < self.count]

    def swap(self, value, s=None):
        places = range(self.depth) if s is None else self.live(s)
        pairs = [(self.physical(2 * z + p), self.physical(2 * z + 1 - p)) for z in places for p in range(2)]
        return lax.ppermute(value, "ctx", pairs)

    def up(self, value, s):
        live = [z for z in self.live(s) if z + 1 < self.depth]
        pairs = [(self.physical(2 * z + p), self.physical(2 * z + 2 + p)) for z in live for p in range(2)]
        return lax.ppermute(value, "ctx", pairs) if pairs else None

    def step(self, s, owns, gots):
        rows, lanes = gots[0].shape
        owns, gots = owns[: s + 1], gots[: s + 1]
        tile = lanes // 2
        per = lanes // tile
        flat = pl.BlockSpec((rows, tile), lambda i, at: (0, i))
        flip, count = int(self.flip), self.count

        def chunk(at):
            return jnp.clip(s - at[2 + flip], 0, count - 1)

        line = pl.BlockSpec((1, tile), lambda i, at: (0, chunk(at) * per + i))
        carries = [] if self.carry is None else [self.carry]
        operands = [*self.rates, *owns, *gots, *carries]
        after, give, keep = pl.pallas_call(
            lambda at, *refs: hop_kernel(len(carries) > 0, len(owns), chunk(at), at[flip], *refs),
            out_shape=(jax.ShapeDtypeStruct((rows, lanes), BF16),) * 3,
            grid_spec=pltpu.PrefetchScalarGridSpec(
                num_scalar_prefetch=1,
                grid=(per,),
                in_specs=[line, line] + [flat] * (len(operands) - 2),
                out_specs=[flat] * 3,
            ),
            compiler_params=PARAMS,
            name="hop_back" if self.flip else "hop",
        )(self.sides, *operands)
        self.carry = self.up(after, s)
        return keep, self.swap(give, s)

def body(proj_xbc, proj_dt, proj_gate, out_grad, conv_weight, conv_bias, decay_log, step_bias, skip_gain, norm_gain):
    x, dt, gate, og = proj_xbc[0], proj_dt[0], proj_gate[0], out_grad[0]
    length, channels = x.shape
    heads = dt.shape[1]
    inner = heads * HEAD_DIM
    ranks = lax.axis_size("ctx")
    shards = lax.axis_size("fsdp")
    per_group = heads // GROUPS
    width = per_group * HEAD_DIM
    side = lax.axis_index("ctx") % 2
    place = lax.axis_index("ctx") // 2
    sides = jnp.stack([side, 1 - side, place, ranks // 2 - 1 - place]).astype(jnp.int32)
    part = inner // CHUNKS
    per = part // width
    c_loc, g_loc, h_loc = channels // shards, inner // shards, heads // shards
    spare = c_loc - g_loc - 3 * h_loc
    groups = GROUPS
    blocks = channels // width

    ahead = [(i, i + 1) for i in range(ranks - 1)]
    behind = [(i + 1, i) for i in range(ranks - 1)]
    halo = lax.ppermute(x[length - HALO :, :], "ctx", ahead)

    def pack_row(gain, decay, step, skip):
        return jnp.concatenate([gain, decay, step, skip, jnp.zeros(gain.shape[:-1] + (spare,), F32)], axis=-1)

    packed = jnp.concatenate(
        [conv_weight, conv_bias[None], pack_row(norm_gain, decay_log, step_bias, skip_gain)[None],
         jnp.zeros((8 - KERNEL - 2, c_loc), F32)], axis=0)
    full = lax.all_gather(packed, "fsdp", axis=1, tiled=True)
    extra = full[KERNEL + 1].reshape(shards, c_loc)
    gain = extra[:, :g_loc].reshape(1, inner)
    decay = extra[:, g_loc : g_loc + h_loc].reshape(1, heads)
    step_b = extra[:, g_loc + h_loc : g_loc + 2 * h_loc].reshape(1, heads)
    skip = extra[:, g_loc + 2 * h_loc : g_loc + 3 * h_loc].reshape(1, heads)
    skip_x = jnp.repeat(skip, HEAD_DIM, axis=1)

    def spec(shape, where):
        return pl.BlockSpec(shape, where)

    def shape(dims, kind):
        return jax.ShapeDtypeStruct(dims, kind)

    table = spec((length, heads), lambda i: (0, 0))
    row_head = spec((1, heads), lambda i: (0, 0))
    scalars = pl.BlockSpec(memory_space=pltpu.SMEM)
    wide_out = spec((length, width), lambda i: (0, i))
    half_out = spec((STATE // 2, width), lambda i: (0, i))
    window = pltpu.VMEM((PAD + length, width), F32)
    wide_bf, half_bf = shape((length, part), BF16), shape((STATE // 2, part), BF16)
    grad_shapes = (shape((length, channels), BF16), shape((8, channels), F32), shape((8, channels), F32))

    def conv_specs(first):
        return [spec((rows, width), lambda i: (0, first + i)) for rows in (length, HALO, 8)]

    def cols(rows, first):
        return spec((rows, width), lambda i: (0, first + i))

    def head_cols(first):
        return [spec((length, STATE), lambda i: (0, first + i)), spec((length, STATE), lambda i: (0, GROUPS + first + i))]

    kq, ec, ei, et = grid_call(
        lambda *refs: keys_kernel(per_group, *refs), "keys", 2,
        out_shape=(shape((length, 2 * width), BF16), shape((length, heads), F32), shape((length, heads), F32),
                   shape((1, inner), F32)),
        in_specs=conv_specs(GROUPS) + [table, row_head, row_head],
        out_specs=(wide_out, table, table, spec((1, inner), lambda i: (0, 0))),
        scratch=[window],
    )(x, halo, full, dt, step_b, decay)
    rates = (et, lax.ppermute(et, "ctx", [(i, i ^ 1) for i in range(ranks)]))

    def front(c):
        first = c * per
        return grid_call(
            lambda *refs: front_kernel(per_group, first, *refs), "front", per,
            out_shape=(wide_bf, wide_bf, half_bf, half_bf),
            in_specs=conv_specs(first) + head_cols(first)[:1] + [table, cols(1, first), scalars],
            out_specs=(wide_out, wide_out, half_out, half_out),
            scratch=[window],
        )(x, halo, full, kq, ei, et, sides)

    def middle(c):
        first = c * per
        near = starts[c : c + depth]
        return grid_call(
            lambda *refs: middle_kernel(per_group, first, depth, *refs), "middle", per,
            out_shape=(wide_bf, wide_bf, shape((STATE, part), BF16), half_bf, half_bf, shape((length, heads), F32),
                       shape((length, inner), BF16), shape((8, inner), F32)),
            in_specs=[wide_out, *head_cols(first), wide_out, table, cols(length, first), cols(length, first),
                      cols(1, first), cols(1, first), scalars] + [half_out] * (2 * depth),
            out_specs=(wide_out, wide_out, spec((STATE, width), lambda i: (0, i)), half_out, half_out, table,
                       cols(length, first), cols(8, first)),
            into=mids[-1][6:] if mids else (),
        )(fronts[c][0], kq, kq, fronts[c][1], ec, gate, og, gain, skip_x, sides,
          *[n[0] for n in near], *[n[1] for n in near])

    def back(c):
        first = c * per
        near = ends[c : c + depth]
        dy, dyp, st = mids[c][:3]
        return grid_call(
            lambda *refs: back_kernel(per_group, first, depth, *refs), "back", per,
            out_shape=(shape((2, length, per * STATE), F32), shape((length, heads), F32), shape((8, heads), F32),
                       *grad_shapes),
            in_specs=[*head_cols(first), wide_out, spec((STATE, width), lambda i: (0, i)), wide_out, wide_out,
                      *conv_specs(first), cols(1, first), cols(1, first), table, scalars] + [half_out] * (2 * depth),
            out_specs=(spec((2, length, STATE), lambda i: (0, 0, i)), table, spec((8, heads), lambda i: (0, 0)),
                       cols(length, first), cols(8, first), cols(8, first)),
            scratch=[window, window],
            into=backs[-1][3:] if backs else (),
        )(kq, kq, fronts[c][1], st, dy, dyp, x, halo, full, skip_x, et, ei, sides,
          *[n[0] for n in near], *[n[1] for n in near])

    fore, aft = Chain(CHUNKS, rates, sides, False), Chain(CHUNKS, rates, sides, True)
    depth, steps = fore.depth, fore.steps
    fronts, mids, backs, starts, ends, got, got_back = [], [], [], [], [], [], []
    for u in range(CHUNKS + 2 * depth + 1):
        if u < CHUNKS:
            fronts.append(front(u))
            got.append(fore.swap(fronts[u][3]))
        if u < steps:
            starts.append(fore.step(u, [f[2] for f in fronts], got))
        if depth <= u < depth + CHUNKS:
            mids.append(middle(u - depth))
            got_back.append(fore.swap(mids[-1][4]))
        if depth + 1 <= u < depth + 1 + steps:
            ends.append(aft.step(u - depth - 1, [m[3] for m in mids], got_back))
        if u >= 2 * depth + 1:
            backs.append(back(u - 2 * depth - 1))

    grad_dt, hs, gx, edge, wr = grid_call(
        lambda *refs: last_kernel(CHUNKS, *refs), "last", 2,
        out_shape=(shape((length, heads), F32), shape((8, heads), F32), *grad_shapes),
        in_specs=conv_specs(GROUPS) + [table, row_head, row_head]
        + [spec((1, length, per * STATE), lambda i: (i, 0, 0))] * CHUNKS + [table] * (2 * CHUNKS)
        + [spec((8, heads), lambda i: (0, 0))] * CHUNKS,
        out_specs=(table, spec((8, heads), lambda i: (0, 0)), cols(length, GROUPS), cols(8, GROUPS), cols(8, GROUPS)),
        scratch=[window, window],
        into=backs[-1][3:],
    )(x, halo, full, dt, step_b, decay, *[b[0] for b in backs], *[m[5] for m in mids], *[b[1] for b in backs],
      *[b[2] for b in backs])
    grad_gate, sums = mids[-1][6:]

    next_gp = lax.ppermute(edge[:HALO], "ctx", behind)
    fixed = []
    for i in range(HALO):
        row = edge[HALO + i]
        for k in range(i + 1):
            row = row + full[k] * next_gp[i - k]
        fixed.append(row)
    grad_xbc = lax.dynamic_update_slice(gx, jnp.stack(fixed).astype(BF16), (length - HALO, 0))

    skip_grad = jnp.sum(sums[1].reshape(heads, HEAD_DIM), axis=1)
    extra_row = pack_row(
        sums[0].reshape(shards, g_loc), hs[0].reshape(shards, h_loc), hs[1].reshape(shards, h_loc),
        skip_grad.reshape(shards, h_loc)).reshape(1, channels)
    parts = jnp.concatenate([wr[: KERNEL + 1], extra_row, jnp.zeros((8 - KERNEL - 2, channels), F32)], axis=0)
    split = ranks // 8
    piece = c_loc // split
    parts = parts.reshape(8, shards, split, piece).transpose(0, 2, 1, 3).reshape(ranks * shards, piece)
    summed = jnp.sum(lax.all_to_all(parts, ("ctx", "fsdp"), 0, 0, tiled=True), axis=0)
    summed = summed * (1.0 / math.sqrt(length * ranks * shards))
    copies = jnp.broadcast_to(summed[None], (ranks, piece))
    mine = lax.all_to_all(copies, "ctx", 0, 0, tiled=True).reshape(8, c_loc)
    tail = mine[KERNEL + 1]
    return (
        grad_xbc[None],
        grad_dt[None],
        grad_gate[None],
        mine[:KERNEL],
        mine[KERNEL],
        tail[g_loc : g_loc + h_loc],
        tail[g_loc + h_loc : g_loc + 2 * h_loc],
        tail[g_loc + 2 * h_loc : g_loc + 3 * h_loc],
        tail[:g_loc],
    )


def solution(mesh):
    data = P("fsdp", "ctx", None)
    one = P("fsdp")
    return jax.shard_map(
        body,
        mesh=mesh,
        in_specs=(data, data, data, data, P(None, "fsdp"), one, one, one, one, one),
        out_specs=(data, data, data, P(None, "fsdp"), one, one, one, one, one),
        check_vma=False,
    )
```

```python
import math

import jax
import jax.numpy as jnp
from jax import lax
from jax.experimental import pallas as pl
from jax.experimental.pallas import tpu as pltpu
from jax.sharding import PartitionSpec as P

HEAD_DIM = 64
STATE = 128
GROUPS = 8
KERNEL = 4
EPSILON = 1e-05
HALO = KERNEL - 1
PAD = 8
CHUNKS = 4
F32 = jnp.float32
BF16 = jnp.bfloat16
HIGHEST = lax.Precision.HIGHEST


def mm(a, b):
    return jnp.dot(a, b, preferred_element_type=F32)


def mm_nt(a, b):
    return lax.dot_general(a, b, (((1,), (1,)), ((), ())), preferred_element_type=F32)


def sigmoid(v):
    return 0.5 * jnp.tanh(0.5 * v) + 0.5


def softplus(v):
    return jnp.maximum(v, 0.0) + jnp.log(1.0 + jnp.exp(-jnp.abs(v)))


def spread_heads(table, group, per_group):
    heads = table.shape[1]
    table = pltpu.roll(table, lax.rem(heads - group * per_group, heads), 1)
    rows = table.shape[0]
    pair = 128 // HEAD_DIM
    lane = lax.broadcasted_iota(jnp.int32, (rows, 128), 1)
    tiles = []
    for i in range(per_group // pair):
        tile = jnp.broadcast_to(table[:, pair * i : pair * i + 1], (rows, 128))
        for p in range(1, pair):
            col = jnp.broadcast_to(table[:, pair * i + p : pair * i + p + 1], (rows, 128))
            tile = jnp.where(lane >= p * HEAD_DIM, col, tile)
        tiles.append(tile)
    return jnp.concatenate(tiles, axis=1)


def sum_heads(values, group, per_group, heads):
    width = values.shape[1]
    row = lax.broadcasted_iota(jnp.int32, (width, heads), 0) // HEAD_DIM + group * per_group
    col = lax.broadcasted_iota(jnp.int32, (width, heads), 1)
    pick = jnp.where(row == col, 1.0, 0.0).astype(BF16)
    high = values.astype(BF16)
    low = (values - high.astype(F32)).astype(BF16)
    return mm(high, pick) + mm(low, pick)


def lower_mask(n):
    return lax.broadcasted_iota(jnp.int32, (n, n), 0) >= lax.broadcasted_iota(jnp.int32, (n, n), 1)


def upper_mask(n):
    return lax.broadcasted_iota(jnp.int32, (n, n), 0) <= lax.broadcasted_iota(jnp.int32, (n, n), 1)


def conv_pre(x_ref, halo_ref, w_ref, xs):
    length = x_ref.shape[0]
    xs[PAD - HALO : PAD, :] = halo_ref[...].astype(F32)
    xs[PAD : PAD + length, :] = x_ref[...].astype(F32)
    pre = jnp.broadcast_to(w_ref[KERNEL : KERNEL + 1, :], (length, x_ref.shape[1]))
    for k in range(KERNEL):
        pre = pre + w_ref[k : k + 1, :] * xs[PAD - HALO + k : PAD - HALO + k + length, :]
    return pre


def split_halves(state, mine, own_ref, send_ref):
    half = state.shape[0] // 2
    low, high = state[:half].astype(BF16), state[half:].astype(BF16)
    shape = own_ref.shape
    own_ref[...] = jnp.where(mine == 0, low, high).reshape(shape)
    send_ref[...] = jnp.where(mine == 0, high, low).reshape(shape)


def keys_kernel(per_group, x_ref, halo_ref, w_ref, dt_ref, sb_ref, dl_ref, kq_ref, ec_ref, ei_ref, et_ref, xs):
    length = x_ref.shape[0]

    @pl.when(pl.program_id(0) == 0)
    def _():
        step = softplus(dt_ref[...].astype(F32) + sb_ref[...])
        ld = -jnp.exp(dl_ref[...]) * step
        tril = jnp.where(lower_mask(length), 1.0, 0.0).astype(F32)
        cum = jnp.dot(tril, ld, precision=HIGHEST, preferred_element_type=F32)
        ec = jnp.exp(cum)
        ec_ref[...] = ec
        ei_ref[...] = jnp.exp(-cum) * step
        width = per_group * HEAD_DIM
        for g in range(GROUPS):
            et_ref[:, g * width : (g + 1) * width] = spread_heads(ec[length - 8 :, :], g, per_group)[7:8, :]

    pre = conv_pre(x_ref, halo_ref, w_ref, xs)
    kq_ref[...] = (pre * sigmoid(pre)).astype(BF16)


def front_kernel(per_group, first, x_ref, halo_ref, w_ref, k_ref, ei_ref, et_ref,
                 side_ref, mixed_ref, vp_ref, own_ref, send_ref, xs):
    g = first + pl.program_id(0)
    pre = conv_pre(x_ref, halo_ref, w_ref, xs)
    mixed = (pre * sigmoid(pre)).astype(BF16)
    mixed_ref[...] = mixed
    vp = (mixed.astype(F32) * spread_heads(ei_ref[...], g, per_group)).astype(BF16)
    vp_ref[...] = vp
    ut = mm(k_ref[...].astype(F32).T.astype(BF16), vp) * et_ref[...]
    split_halves(ut, side_ref[0], own_ref, send_ref)


def choose(refs, pick):
    value = refs[0][...]
    for i in range(1, len(refs)):
        value = jnp.where(pick == i, refs[i][...], value)
    return value


def join_halves(own, other, mine):
    return jnp.concatenate([jnp.where(mine == 0, own, other), jnp.where(mine == 0, other, own)], axis=0)


def middle_kernel(per_group, first, depth, v_ref, k_ref, q_ref, vp_ref, ec_ref, gate_ref, og_ref, gain_ref, skip_ref,
                  side_ref, *refs):
    keeps, backs = refs[:depth], refs[depth : 2 * depth]
    dy_ref, dyp_ref, st_ref, own_ref, send_ref, a1_ref, gg_ref, rows_ref = refs[2 * depth :]
    st = join_halves(choose(keeps, side_ref[2]), choose(backs, side_ref[2]), side_ref[0])
    st_ref[...] = st
    g = first + pl.program_id(0)
    length, width = v_ref.shape
    heads = ec_ref.shape[1]
    q = q_ref[...]
    z = jnp.where(lower_mask(length), mm_nt(q, k_ref[...]), 0.0).astype(BF16)
    yn = mm(jnp.concatenate([z, q], axis=1), jnp.concatenate([vp_ref[...], st], axis=0))
    ecx = spread_heads(ec_ref[...], g, per_group)
    v = v_ref[...].astype(F32)
    y = (ecx * yn + skip_ref[...] * v).astype(BF16).astype(F32)
    gate = gate_ref[...].astype(F32)
    og = og_ref[...].astype(F32)
    sig = sigmoid(gate)
    act = gate * sig
    gated = y * act
    scale = lax.rsqrt(jnp.sum(gated * gated, axis=1, keepdims=True) * (1.0 / width) + EPSILON)
    dgn = og * gain_ref[...]
    inner = jnp.sum(dgn * gated, axis=1, keepdims=True) * (1.0 / width)
    dgated = scale * dgn - gated * (scale * scale * scale * inner)
    dyb = (dgated * act).astype(BF16)
    dy_ref[...] = dyb
    gg_ref[...] = (dgated * y * (sig + act * (1.0 - sig))).astype(BF16)
    dy = dyb.astype(F32)
    dyp = (ecx * dy).astype(BF16)
    dyp_ref[...] = dyp
    gt = mm(q.astype(F32).T.astype(BF16), dyp)
    split_halves(gt, side_ref[1], own_ref, send_ref)
    rows_ref[...] = jnp.zeros(rows_ref.shape, F32)
    rows_ref[0:1, :] = jnp.sum(og * gated * scale, axis=0, keepdims=True)
    rows_ref[1:2, :] = jnp.sum(dy * v, axis=0, keepdims=True)

    @pl.when(pl.program_id(0) == 0)
    def _():
        a1_ref[...] = jnp.zeros(a1_ref.shape, F32)

    a1_ref[...] += sum_heads(dyp.astype(F32) * yn, g, per_group, heads)


def conv_back(grads, x_ref, halo_ref, w_ref, gx_ref, edge_ref, wr_ref, xs, gs):
    length = x_ref.shape[0]
    pre = conv_pre(x_ref, halo_ref, w_ref, xs)
    sig = sigmoid(pre)
    gp = grads * (sig * (1.0 + pre * (1.0 - sig)))
    gs[0:length, :] = gp
    gs[length:, :] = jnp.zeros((gs.shape[0] - length, gs.shape[1]), F32)
    wr_ref[...] = jnp.zeros(wr_ref.shape, F32)
    total = jnp.zeros(gp.shape, F32)
    for k in range(KERNEL):
        lead = HALO - k
        total = total + w_ref[k : k + 1, :] * gs[lead : lead + length, :]
        wr_ref[k : k + 1, :] = jnp.sum(gp * xs[PAD - HALO + k : PAD - HALO + k + length, :], axis=0, keepdims=True)
    wr_ref[KERNEL : KERNEL + 1, :] = jnp.sum(gp, axis=0, keepdims=True)
    gx_ref[...] = total.astype(BF16)
    edge_ref[...] = jnp.zeros(edge_ref.shape, F32)
    edge_ref[0:HALO, :] = gp[0:HALO, :]
    edge_ref[HALO : 2 * HALO, :] = total[length - HALO : length, :]


def back_kernel(per_group, first, depth, k_ref, q_ref, vp_ref, st_ref, dy_ref, dyp_ref, x_ref, halo_ref, w_ref,
                skip_ref, et_ref, ei_ref, side_ref, *refs):
    keeps, backs = refs[:depth], refs[depth : 2 * depth]
    dkq_ref, a2_ref, last_ref, gx_ref, edge_ref, wr_ref, xs, gs = refs[2 * depth :]
    j = first + pl.program_id(0)
    length, width = x_ref.shape
    heads = ei_ref.shape[1]

    @pl.when(pl.program_id(0) == 0)
    def _():
        a2_ref[...] = jnp.zeros(a2_ref.shape, F32)
        last_ref[...] = jnp.zeros(last_ref.shape, F32)

    k = k_ref[...]
    q = q_ref[...]
    vp = vp_ref[...]
    dyp = dyp_ref[...]
    st = st_ref[...]
    en = join_halves(choose(keeps, side_ref[3]), choose(backs, side_ref[3]), side_ref[1])
    en = (et_ref[...] * en.astype(F32)).astype(BF16)
    zt = jnp.where(upper_mask(length), mm_nt(k, q), 0.0).astype(BF16)
    dvp = mm(jnp.concatenate([zt, k], axis=1), jnp.concatenate([dyp, en], axis=0))
    grads = spread_heads(ei_ref[...], j, per_group) * dvp + skip_ref[...] * dy_ref[...].astype(F32)
    a2_ref[...] += sum_heads(vp.astype(F32) * dvp, j, per_group, heads)
    ends = en.astype(F32) * (st.astype(F32) + mm(k.astype(F32).T.astype(BF16), vp))
    ends = jnp.broadcast_to(jnp.sum(ends, axis=0, keepdims=True), (8, width))
    last_ref[...] += sum_heads(ends, j, per_group, heads)
    dz = jnp.where(lower_mask(length), mm_nt(dyp, vp), 0.0)
    dkq_ref[0] = mm(dz.T.astype(BF16), q) + mm_nt(vp, en)
    dkq_ref[1] = mm(dz.astype(BF16), k) + mm_nt(dyp, st)
    conv_back(grads, x_ref, halo_ref, w_ref, gx_ref, edge_ref, wr_ref, xs, gs)


def last_kernel(count, x_ref, halo_ref, w_ref, dt_ref, sb_ref, dl_ref, *refs):
    dkq, a1, a2, last = (refs[i * count : (i + 1) * count] for i in range(4))
    gdt_ref, hs_ref, gx_ref, edge_ref, wr_ref, xs, gs = refs[4 * count :]
    grads = jnp.concatenate([ref[0] for ref in dkq], axis=1)
    conv_back(grads, x_ref, halo_ref, w_ref, gx_ref, edge_ref, wr_ref, xs, gs)

    @pl.when(pl.program_id(0) == 0)
    def _():
        length, heads = dt_ref.shape
        raw = dt_ref[...].astype(F32) + sb_ref[...]
        step = softplus(raw)
        rate = jnp.exp(dl_ref[...])
        row = lax.broadcasted_iota(jnp.int32, (length, heads), 0)
        down = sum(ref[...] for ref in a2)
        end = sum(ref[...] for ref in last)[0:1, :]
        dcum = sum(ref[...] for ref in a1) - down + jnp.where(row == length - 1, end, 0.0)
        triu = jnp.where(upper_mask(length), 1.0, 0.0).astype(F32)
        dld = jnp.dot(triu, dcum, precision=HIGHEST, preferred_element_type=F32)
        gdt = (down / step - rate * dld) * sigmoid(raw)
        gdt_ref[...] = gdt
        hs_ref[...] = jnp.zeros(hs_ref.shape, F32)
        hs_ref[0:1, :] = jnp.sum(-rate * step * dld, axis=0, keepdims=True)
        hs_ref[1:2, :] = jnp.sum(gdt, axis=0, keepdims=True)


PARAMS = pltpu.CompilerParams(vmem_limit_bytes=40 * 1024 * 1024)


def grid_call(kernel, name, steps, in_specs, out_specs, out_shape, scratch=(), into=()):
    given = len(in_specs)
    anywhere = pl.BlockSpec(memory_space=pl.ANY)

    def stays(s):
        return s.shape[0] == STATE // 2 or s.shape == (8, STATE)

    def place(s):
        return s if stays(s) else pltpu.HBM(s.shape, s.dtype)

    call = pl.pallas_call(
        lambda *refs: kernel(*refs[:given], *refs[given + len(into) :]),
        out_shape=tuple(place(s) for s in out_shape),
        grid=(steps,),
        in_specs=[*in_specs, *[anywhere] * len(into)],
        out_specs=out_specs,
        scratch_shapes=scratch,
        input_output_aliases={given + i: len(out_shape) - len(into) + i for i in range(len(into))},
        compiler_params=PARAMS,
        name=name,
    )

    def run(*values):
        kept = [v if s.memory_space == pltpu.SMEM or stays(v) else in_hbm(v)
                for v, s in zip(values, in_specs, strict=True)]
        return call(*kept, *[in_hbm(v) for v in into])

    return run


def hop_kernel(has_carry, choices, chunk, side, mine_ref, pair_ref, *refs):
    own, got = choose(refs[:choices], chunk), choose(refs[choices : 2 * choices], chunk)
    refs = refs[2 * choices :]
    if has_carry:
        carry_ref, next_ref, give_ref, keep_ref = refs
        carry = carry_ref[...].astype(F32)
    else:
        next_ref, give_ref, keep_ref = refs
        carry = jnp.zeros(next_ref.shape, F32)
    first = side == 0
    own, got = own.astype(F32), got.astype(F32)
    mine, pair = mine_ref[...], pair_ref[...]
    inner = jnp.where(first, mine, pair) * carry + jnp.where(first, own, got)
    next_ref[...] = (jnp.where(first, pair, mine) * inner + jnp.where(first, got, own)).astype(BF16)
    give_ref[...] = jnp.where(first, inner, carry).astype(BF16)
    keep_ref[...] = jnp.where(first, carry, inner).astype(BF16)


def in_hbm(value):
    return pltpu.with_memory_space_constraint(value, pltpu.HBM)


class Chain:
    def __init__(self, count, rates, sides, flip):
        self.count, self.rates, self.sides, self.flip = count, rates, sides, flip
        self.ranks = lax.axis_size("ctx")
        self.depth = self.ranks // 2
        self.steps = count + self.depth - 1
        self.carry = None
        self.starts = []

    def physical(self, r):
        return self.ranks - 1 - r if self.flip else r

    def live(self, s):
        return [z for z in range(self.depth) if 0 <= s - z < self.count]

    def swap(self, value, s=None):
        places = range(self.depth) if s is None else self.live(s)
        pairs = [(self.physical(2 * z + p), self.physical(2 * z + 1 - p)) for z in places for p in range(2)]
        return lax.ppermute(value, "ctx", pairs)

    def up(self, value, s):
        live = [z for z in self.live(s) if z + 1 < self.depth]
        pairs = [(self.physical(2 * z + p), self.physical(2 * z + 2 + p)) for z in live for p in range(2)]
        return lax.ppermute(value, "ctx", pairs) if pairs else None

    def step(self, s, owns, gots, *first):
        if self.carry is not None and self.flip:
            keep, back = self.starts[-1]
            self.carry, back, *_ = lax.optimization_barrier((self.carry, back, *first))
            self.starts[-1] = (keep, back)
        rows, lanes = gots[0].shape
        owns, gots = owns[: s + 1], gots[: s + 1]
        tile = lanes // 2
        per = lanes // tile
        flat = pl.BlockSpec((rows, tile), lambda i, at: (0, i))
        flip, count = int(self.flip), self.count

        def chunk(at):
            return jnp.clip(s - at[2 + flip], 0, count - 1)

        line = pl.BlockSpec((1, tile), lambda i, at: (0, chunk(at) * per + i))
        carries = [] if self.carry is None else [self.carry]
        operands = [*self.rates, *owns, *gots, *carries]
        after, give, keep = pl.pallas_call(
            lambda at, *refs: hop_kernel(len(carries) > 0, len(owns), chunk(at), at[flip], *refs),
            out_shape=(jax.ShapeDtypeStruct((rows, lanes), BF16),) * 3,
            grid_spec=pltpu.PrefetchScalarGridSpec(
                num_scalar_prefetch=1,
                grid=(per,),
                in_specs=[line, line] + [flat] * (len(operands) - 2),
                out_specs=[flat] * 3,
            ),
            compiler_params=PARAMS,
            name="hop_back" if self.flip else "hop",
        )(self.sides, *operands)
        self.carry = self.up(after, s)
        self.starts.append((keep, self.swap(give, s)))

def body(proj_xbc, proj_dt, proj_gate, out_grad, conv_weight, conv_bias, decay_log, step_bias, skip_gain, norm_gain):
    x, dt, gate, og = proj_xbc[0], proj_dt[0], proj_gate[0], out_grad[0]
    length, channels = x.shape
    heads = dt.shape[1]
    inner = heads * HEAD_DIM
    ranks = lax.axis_size("ctx")
    shards = lax.axis_size("fsdp")
    per_group = heads // GROUPS
    width = per_group * HEAD_DIM
    side = lax.axis_index("ctx") % 2
    place = lax.axis_index("ctx") // 2
    sides = jnp.stack([side, 1 - side, place, ranks // 2 - 1 - place]).astype(jnp.int32)
    part = inner // CHUNKS
    per = part // width
    c_loc, g_loc, h_loc = channels // shards, inner // shards, heads // shards
    spare = c_loc - g_loc - 3 * h_loc
    groups = GROUPS
    blocks = channels // width

    ahead = [(i, i + 1) for i in range(ranks - 1)]
    behind = [(i + 1, i) for i in range(ranks - 1)]
    halo = lax.ppermute(x[length - HALO :, :], "ctx", ahead)

    def pack_row(gain, decay, step, skip):
        return jnp.concatenate([gain, decay, step, skip, jnp.zeros(gain.shape[:-1] + (spare,), F32)], axis=-1)

    packed = jnp.concatenate(
        [conv_weight, conv_bias[None], pack_row(norm_gain, decay_log, step_bias, skip_gain)[None],
         jnp.zeros((8 - KERNEL - 2, c_loc), F32)], axis=0)
    full = lax.all_gather(packed, "fsdp", axis=1, tiled=True)
    extra = full[KERNEL + 1].reshape(shards, c_loc)
    gain = extra[:, :g_loc].reshape(1, inner)
    decay = extra[:, g_loc : g_loc + h_loc].reshape(1, heads)
    step_b = extra[:, g_loc + h_loc : g_loc + 2 * h_loc].reshape(1, heads)
    skip = extra[:, g_loc + 2 * h_loc : g_loc + 3 * h_loc].reshape(1, heads)
    skip_x = jnp.repeat(skip, HEAD_DIM, axis=1)

    def spec(shape, where):
        return pl.BlockSpec(shape, where)

    def shape(dims, kind):
        return jax.ShapeDtypeStruct(dims, kind)

    table = spec((length, heads), lambda i: (0, 0))
    row_head = spec((1, heads), lambda i: (0, 0))
    scalars = pl.BlockSpec(memory_space=pltpu.SMEM)
    wide_out = spec((length, width), lambda i: (0, i))
    half_out = spec((STATE // 2, width), lambda i: (0, i))
    window = pltpu.VMEM((PAD + length, width), F32)
    wide_bf, half_bf = shape((length, part), BF16), shape((STATE // 2, part), BF16)
    grad_shapes = (shape((length, channels), BF16), shape((8, channels), F32), shape((8, channels), F32))

    def conv_specs(first):
        return [spec((rows, width), lambda i: (0, first + i)) for rows in (length, HALO, 8)]

    def cols(rows, first):
        return spec((rows, width), lambda i: (0, first + i))

    def head_cols(first):
        return [spec((length, STATE), lambda i: (0, first + i)), spec((length, STATE), lambda i: (0, GROUPS + first + i))]

    kq, ec, ei, et = grid_call(
        lambda *refs: keys_kernel(per_group, *refs), "keys", 2,
        out_shape=(shape((length, 2 * width), BF16), shape((length, heads), F32), shape((length, heads), F32),
                   shape((1, inner), F32)),
        in_specs=conv_specs(GROUPS) + [table, row_head, row_head],
        out_specs=(wide_out, table, table, spec((1, inner), lambda i: (0, 0))),
        scratch=[window],
    )(x, halo, full, dt, step_b, decay)
    rates = (et, lax.ppermute(et, "ctx", [(i, i ^ 1) for i in range(ranks)]))

    def front(c):
        first = c * per
        return grid_call(
            lambda *refs: front_kernel(per_group, first, *refs), "front", per,
            out_shape=(wide_bf, wide_bf, half_bf, half_bf),
            in_specs=conv_specs(first) + head_cols(first)[:1] + [table, cols(1, first), scalars],
            out_specs=(wide_out, wide_out, half_out, half_out),
            scratch=[window],
        )(x, halo, full, kq, ei, et, sides)

    def middle(c):
        first = c * per
        near = fore.starts[c : c + depth]
        return grid_call(
            lambda *refs: middle_kernel(per_group, first, depth, *refs), "middle", per,
            out_shape=(wide_bf, wide_bf, shape((STATE, part), BF16), half_bf, half_bf, shape((length, heads), F32),
                       shape((length, inner), BF16), shape((8, inner), F32)),
            in_specs=[wide_out, *head_cols(first), wide_out, table, cols(length, first), cols(length, first),
                      cols(1, first), cols(1, first), scalars] + [half_out] * (2 * depth),
            out_specs=(wide_out, wide_out, spec((STATE, width), lambda i: (0, i)), half_out, half_out, table,
                       cols(length, first), cols(8, first)),
            into=mids[-1][6:] if mids else (),
        )(fronts[c][0], kq, kq, fronts[c][1], ec, gate, og, gain, skip_x, sides,
          *[n[0] for n in near], *[n[1] for n in near])

    def back(c):
        first = c * per
        near = aft.starts[c : c + depth]
        dy, dyp, st = mids[c][:3]
        return grid_call(
            lambda *refs: back_kernel(per_group, first, depth, *refs), "back", per,
            out_shape=(shape((2, length, per * STATE), F32), shape((length, heads), F32), shape((8, heads), F32),
                       *grad_shapes),
            in_specs=[*head_cols(first), wide_out, spec((STATE, width), lambda i: (0, i)), wide_out, wide_out,
                      *conv_specs(first), cols(1, first), cols(1, first), table, scalars] + [half_out] * (2 * depth),
            out_specs=(spec((2, length, STATE), lambda i: (0, 0, i)), table, spec((8, heads), lambda i: (0, 0)),
                       cols(length, first), cols(8, first), cols(8, first)),
            scratch=[window, window],
            into=backs[-1][3:] if backs else (),
        )(kq, kq, fronts[c][1], st, dy, dyp, x, halo, full, skip_x, et, ei, sides,
          *[n[0] for n in near], *[n[1] for n in near])

    fore, aft = Chain(CHUNKS, rates, sides, False), Chain(CHUNKS, rates, sides, True)
    depth, steps = fore.depth, fore.steps
    fronts, mids, backs, got, got_back = [], [], [], [], []
    for u in range(CHUNKS + 2 * depth + 1):
        if u < CHUNKS:
            fronts.append(front(u))
            got.append(fore.swap(fronts[u][3]))
        if u < steps:
            fore.step(u, [f[2] for f in fronts], got)
        if depth <= u < depth + CHUNKS:
            mids.append(middle(u - depth))
            got_back.append(fore.swap(mids[-1][4]))
        if depth + 1 <= u < depth + 1 + steps:
            aft.step(u - depth - 1, [m[3] for m in mids], got_back, *[b[2] for b in backs[-1:]])
        if u >= 2 * depth + 1:
            backs.append(back(u - 2 * depth - 1))

    grad_dt, hs, gx, edge, wr = grid_call(
        lambda *refs: last_kernel(CHUNKS, *refs), "last", 2,
        out_shape=(shape((length, heads), F32), shape((8, heads), F32), *grad_shapes),
        in_specs=conv_specs(GROUPS) + [table, row_head, row_head]
        + [spec((1, length, per * STATE), lambda i: (i, 0, 0))] * CHUNKS + [table] * (2 * CHUNKS)
        + [spec((8, heads), lambda i: (0, 0))] * CHUNKS,
        out_specs=(table, spec((8, heads), lambda i: (0, 0)), cols(length, GROUPS), cols(8, GROUPS), cols(8, GROUPS)),
        scratch=[window, window],
        into=backs[-1][3:],
    )(x, halo, full, dt, step_b, decay, *[b[0] for b in backs], *[m[5] for m in mids], *[b[1] for b in backs],
      *[b[2] for b in backs])
    grad_gate, sums = mids[-1][6:]

    next_gp = lax.ppermute(edge[:HALO], "ctx", behind)
    fixed = []
    for i in range(HALO):
        row = edge[HALO + i]
        for k in range(i + 1):
            row = row + full[k] * next_gp[i - k]
        fixed.append(row)
    grad_xbc = lax.dynamic_update_slice(gx, jnp.stack(fixed).astype(BF16), (length - HALO, 0))

    skip_grad = jnp.sum(sums[1].reshape(heads, HEAD_DIM), axis=1)
    extra_row = pack_row(
        sums[0].reshape(shards, g_loc), hs[0].reshape(shards, h_loc), hs[1].reshape(shards, h_loc),
        skip_grad.reshape(shards, h_loc)).reshape(1, channels)
    parts = jnp.concatenate([wr[: KERNEL + 1], extra_row, jnp.zeros((8 - KERNEL - 2, channels), F32)], axis=0)
    split = ranks // 8
    piece = c_loc // split
    parts = parts.reshape(8, shards, split, piece).transpose(0, 2, 1, 3).reshape(ranks * shards, piece)
    summed = jnp.sum(lax.all_to_all(parts, ("ctx", "fsdp"), 0, 0, tiled=True), axis=0)
    summed = summed * (1.0 / math.sqrt(length * ranks * shards))
    copies = jnp.broadcast_to(summed[None], (ranks, piece))
    mine = lax.all_to_all(copies, "ctx", 0, 0, tiled=True).reshape(8, c_loc)
    tail = mine[KERNEL + 1]
    return (
        grad_xbc[None],
        grad_dt[None],
        grad_gate[None],
        mine[:KERNEL],
        mine[KERNEL],
        tail[g_loc : g_loc + h_loc],
        tail[g_loc + h_loc : g_loc + 2 * h_loc],
        tail[g_loc + 2 * h_loc : g_loc + 3 * h_loc],
        tail[:g_loc],
    )


def solution(mesh):
    data = P("fsdp", "ctx", None)
    one = P("fsdp")
    return jax.shard_map(
        body,
        mesh=mesh,
        in_specs=(data, data, data, data, P(None, "fsdp"), one, one, one, one, one),
        out_specs=(data, data, data, P(None, "fsdp"), one, one, one, one, one),
        check_vma=False,
    )
```

```python
import math

import jax
import jax.numpy as jnp
from jax import lax
from jax.experimental import pallas as pl
from jax.experimental.pallas import tpu as pltpu
from jax.sharding import PartitionSpec as P

HEAD_DIM = 64
STATE = 128
GROUPS = 8
KERNEL = 4
EPSILON = 1e-05
HALO = KERNEL - 1
PAD = 8
CHUNKS = 4
F32 = jnp.float32
BF16 = jnp.bfloat16
HIGHEST = lax.Precision.HIGHEST


def mm(a, b):
    return jnp.dot(a, b, preferred_element_type=F32)


def mm_nt(a, b):
    return lax.dot_general(a, b, (((1,), (1,)), ((), ())), preferred_element_type=F32)


def sigmoid(v):
    return 0.5 * jnp.tanh(0.5 * v) + 0.5


def softplus(v):
    return jnp.maximum(v, 0.0) + jnp.log(1.0 + jnp.exp(-jnp.abs(v)))


def spread_heads(table, group, per_group):
    heads = table.shape[1]
    table = pltpu.roll(table, lax.rem(heads - group * per_group, heads), 1)
    rows = table.shape[0]
    pair = 128 // HEAD_DIM
    lane = lax.broadcasted_iota(jnp.int32, (rows, 128), 1)
    tiles = []
    for i in range(per_group // pair):
        tile = jnp.broadcast_to(table[:, pair * i : pair * i + 1], (rows, 128))
        for p in range(1, pair):
            col = jnp.broadcast_to(table[:, pair * i + p : pair * i + p + 1], (rows, 128))
            tile = jnp.where(lane >= p * HEAD_DIM, col, tile)
        tiles.append(tile)
    return jnp.concatenate(tiles, axis=1)


def sum_heads(values, group, per_group, heads):
    width = values.shape[1]
    row = lax.broadcasted_iota(jnp.int32, (width, heads), 0) // HEAD_DIM + group * per_group
    col = lax.broadcasted_iota(jnp.int32, (width, heads), 1)
    pick = jnp.where(row == col, 1.0, 0.0).astype(BF16)
    high = values.astype(BF16)
    low = (values - high.astype(F32)).astype(BF16)
    return mm(high, pick) + mm(low, pick)


def lower_mask(n):
    return lax.broadcasted_iota(jnp.int32, (n, n), 0) >= lax.broadcasted_iota(jnp.int32, (n, n), 1)


def upper_mask(n):
    return lax.broadcasted_iota(jnp.int32, (n, n), 0) <= lax.broadcasted_iota(jnp.int32, (n, n), 1)


def conv_pre(x_ref, halo_ref, w_ref, xs):
    length = x_ref.shape[0]
    xs[PAD - HALO : PAD, :] = halo_ref[...].astype(F32)
    xs[PAD : PAD + length, :] = x_ref[...].astype(F32)
    pre = jnp.broadcast_to(w_ref[KERNEL : KERNEL + 1, :], (length, x_ref.shape[1]))
    for k in range(KERNEL):
        pre = pre + w_ref[k : k + 1, :] * xs[PAD - HALO + k : PAD - HALO + k + length, :]
    return pre


def split_halves(state, mine, own_ref, send_ref):
    half = state.shape[0] // 2
    low, high = state[:half].astype(BF16), state[half:].astype(BF16)
    shape = own_ref.shape
    own_ref[...] = jnp.where(mine == 0, low, high).reshape(shape)
    send_ref[...] = jnp.where(mine == 0, high, low).reshape(shape)


def keys_kernel(per_group, x_ref, halo_ref, w_ref, dt_ref, sb_ref, dl_ref, kq_ref, ec_ref, ei_ref, et_ref, xs):
    length = x_ref.shape[0]

    @pl.when(pl.program_id(0) == 0)
    def _():
        step = softplus(dt_ref[...].astype(F32) + sb_ref[...])
        ld = -jnp.exp(dl_ref[...]) * step
        tril = jnp.where(lower_mask(length), 1.0, 0.0).astype(F32)
        cum = jnp.dot(tril, ld, precision=HIGHEST, preferred_element_type=F32)
        ec = jnp.exp(cum)
        ec_ref[...] = ec
        ei_ref[...] = jnp.exp(-cum) * step
        width = per_group * HEAD_DIM
        for g in range(GROUPS):
            et_ref[:, g * width : (g + 1) * width] = spread_heads(ec[length - 8 :, :], g, per_group)[7:8, :]

    pre = conv_pre(x_ref, halo_ref, w_ref, xs)
    kq_ref[...] = (pre * sigmoid(pre)).astype(BF16)


def front_kernel(per_group, first, x_ref, halo_ref, w_ref, k_ref, ei_ref, et_ref,
                 side_ref, mixed_ref, vp_ref, own_ref, send_ref, xs):
    g = first + pl.program_id(0)
    pre = conv_pre(x_ref, halo_ref, w_ref, xs)
    mixed = (pre * sigmoid(pre)).astype(BF16)
    mixed_ref[...] = mixed
    vp = (mixed.astype(F32) * spread_heads(ei_ref[...], g, per_group)).astype(BF16)
    vp_ref[...] = vp
    ut = mm(k_ref[...].astype(F32).T.astype(BF16), vp) * et_ref[...]
    split_halves(ut, side_ref[0], own_ref, send_ref)


def choose(refs, pick):
    value = refs[0][...]
    for i in range(1, len(refs)):
        value = jnp.where(pick == i, refs[i][...], value)
    return value


def join_halves(own, other, mine):
    return jnp.concatenate([jnp.where(mine == 0, own, other), jnp.where(mine == 0, other, own)], axis=0)


def middle_kernel(per_group, first, depth, v_ref, k_ref, q_ref, vp_ref, ec_ref, gate_ref, og_ref, gain_ref, skip_ref,
                  side_ref, *refs):
    keeps, backs = refs[:depth], refs[depth : 2 * depth]
    dy_ref, dyp_ref, st_ref, own_ref, send_ref, a1_ref, gg_ref, rows_ref = refs[2 * depth :]
    st = join_halves(choose(keeps, side_ref[2]), choose(backs, side_ref[2]), side_ref[0])
    st_ref[...] = st
    g = first + pl.program_id(0)
    length, width = v_ref.shape
    heads = ec_ref.shape[1]
    q = q_ref[...]
    z = jnp.where(lower_mask(length), mm_nt(q, k_ref[...]), 0.0).astype(BF16)
    yn = mm(jnp.concatenate([z, q], axis=1), jnp.concatenate([vp_ref[...], st], axis=0))
    ecx = spread_heads(ec_ref[...], g, per_group)
    v = v_ref[...].astype(F32)
    y = (ecx * yn + skip_ref[...] * v).astype(BF16).astype(F32)
    gate = gate_ref[...].astype(F32)
    og = og_ref[...].astype(F32)
    sig = sigmoid(gate)
    act = gate * sig
    gated = y * act
    scale = lax.rsqrt(jnp.sum(gated * gated, axis=1, keepdims=True) * (1.0 / width) + EPSILON)
    dgn = og * gain_ref[...]
    inner = jnp.sum(dgn * gated, axis=1, keepdims=True) * (1.0 / width)
    dgated = scale * dgn - gated * (scale * scale * scale * inner)
    dyb = (dgated * act).astype(BF16)
    dy_ref[...] = dyb
    gg_ref[...] = (dgated * y * (sig + act * (1.0 - sig))).astype(BF16)
    dy = dyb.astype(F32)
    dyp = (ecx * dy).astype(BF16)
    dyp_ref[...] = dyp
    gt = mm(q.astype(F32).T.astype(BF16), dyp)
    split_halves(gt, side_ref[1], own_ref, send_ref)
    rows_ref[...] = jnp.zeros(rows_ref.shape, F32)
    rows_ref[0:1, :] = jnp.sum(og * gated * scale, axis=0, keepdims=True)
    rows_ref[1:2, :] = jnp.sum(dy * v, axis=0, keepdims=True)

    @pl.when(pl.program_id(0) == 0)
    def _():
        a1_ref[...] = jnp.zeros(a1_ref.shape, F32)

    a1_ref[...] += sum_heads(dyp.astype(F32) * yn, g, per_group, heads)


def conv_back(grads, x_ref, halo_ref, w_ref, gx_ref, lead_ref, tail_ref, wr_ref, xs, gs):
    length = x_ref.shape[0]
    pre = conv_pre(x_ref, halo_ref, w_ref, xs)
    sig = sigmoid(pre)
    gp = grads * (sig * (1.0 + pre * (1.0 - sig)))
    gs[0:length, :] = gp
    gs[length:, :] = jnp.zeros((gs.shape[0] - length, gs.shape[1]), F32)
    wr_ref[...] = jnp.zeros(wr_ref.shape, F32)
    total = jnp.zeros(gp.shape, F32)
    for k in range(KERNEL):
        lead = HALO - k
        total = total + w_ref[k : k + 1, :] * gs[lead : lead + length, :]
        wr_ref[k : k + 1, :] = jnp.sum(gp * xs[PAD - HALO + k : PAD - HALO + k + length, :], axis=0, keepdims=True)
    wr_ref[KERNEL : KERNEL + 1, :] = jnp.sum(gp, axis=0, keepdims=True)
    gx_ref[...] = total.astype(BF16)
    lead_ref[...] = gp[0:HALO, :]
    tail_ref[...] = total[length - HALO : length, :]


def back_kernel(per_group, first, depth, k_ref, q_ref, vp_ref, st_ref, dy_ref, dyp_ref, x_ref, halo_ref, w_ref,
                skip_ref, et_ref, ei_ref, side_ref, *refs):
    keeps, backs = refs[:depth], refs[depth : 2 * depth]
    dkq_ref, a2_ref, last_ref, gx_ref, lead_ref, tail_ref, wr_ref, xs, gs = refs[2 * depth :]
    j = first + pl.program_id(0)
    length, width = x_ref.shape
    heads = ei_ref.shape[1]

    @pl.when(pl.program_id(0) == 0)
    def _():
        a2_ref[...] = jnp.zeros(a2_ref.shape, F32)
        last_ref[...] = jnp.zeros(last_ref.shape, F32)

    k = k_ref[...]
    q = q_ref[...]
    vp = vp_ref[...]
    dyp = dyp_ref[...]
    st = st_ref[...]
    en = join_halves(choose(keeps, side_ref[3]), choose(backs, side_ref[3]), side_ref[1])
    en = (et_ref[...] * en.astype(F32)).astype(BF16)
    zt = jnp.where(upper_mask(length), mm_nt(k, q), 0.0).astype(BF16)
    dvp = mm(jnp.concatenate([zt, k], axis=1), jnp.concatenate([dyp, en], axis=0))
    grads = spread_heads(ei_ref[...], j, per_group) * dvp + skip_ref[...] * dy_ref[...].astype(F32)
    a2_ref[...] += sum_heads(vp.astype(F32) * dvp, j, per_group, heads)
    ends = en.astype(F32) * (st.astype(F32) + mm(k.astype(F32).T.astype(BF16), vp))
    ends = jnp.broadcast_to(jnp.sum(ends, axis=0, keepdims=True), (8, width))
    last_ref[...] += sum_heads(ends, j, per_group, heads)
    dz = jnp.where(lower_mask(length), mm_nt(dyp, vp), 0.0)
    dkq_ref[0] = mm(dz.T.astype(BF16), q) + mm_nt(vp, en)
    dkq_ref[1] = mm(dz.astype(BF16), k) + mm_nt(dyp, st)
    conv_back(grads, x_ref, halo_ref, w_ref, gx_ref, lead_ref, tail_ref, wr_ref, xs, gs)


def last_kernel(count, x_ref, halo_ref, w_ref, dt_ref, sb_ref, dl_ref, *refs):
    dkq, a1, a2, last = (refs[i * count : (i + 1) * count] for i in range(4))
    gdt_ref, hs_ref, gx_ref, lead_ref, tail_ref, wr_ref, xs, gs = refs[4 * count :]
    grads = jnp.concatenate([ref[0] for ref in dkq], axis=1)
    conv_back(grads, x_ref, halo_ref, w_ref, gx_ref, lead_ref, tail_ref, wr_ref, xs, gs)

    @pl.when(pl.program_id(0) == 0)
    def _():
        length, heads = dt_ref.shape
        raw = dt_ref[...].astype(F32) + sb_ref[...]
        step = softplus(raw)
        rate = jnp.exp(dl_ref[...])
        row = lax.broadcasted_iota(jnp.int32, (length, heads), 0)
        down = sum(ref[...] for ref in a2)
        end = sum(ref[...] for ref in last)[0:1, :]
        dcum = sum(ref[...] for ref in a1) - down + jnp.where(row == length - 1, end, 0.0)
        triu = jnp.where(upper_mask(length), 1.0, 0.0).astype(F32)
        dld = jnp.dot(triu, dcum, precision=HIGHEST, preferred_element_type=F32)
        gdt = (down / step - rate * dld) * sigmoid(raw)
        gdt_ref[...] = gdt
        hs_ref[...] = jnp.zeros(hs_ref.shape, F32)
        hs_ref[0:1, :] = jnp.sum(-rate * step * dld, axis=0, keepdims=True)
        hs_ref[1:2, :] = jnp.sum(gdt, axis=0, keepdims=True)


PARAMS = pltpu.CompilerParams(vmem_limit_bytes=40 * 1024 * 1024)


def grid_call(kernel, name, steps, in_specs, out_specs, out_shape, scratch=(), into=()):
    given = len(in_specs)
    anywhere = pl.BlockSpec(memory_space=pl.ANY)

    def stays(s):
        return s.shape[0] == STATE // 2 or s.shape == (8, STATE)

    def place(s):
        return s if stays(s) else pltpu.HBM(s.shape, s.dtype)

    call = pl.pallas_call(
        lambda *refs: kernel(*refs[:given], *refs[given + len(into) :]),
        out_shape=tuple(place(s) for s in out_shape),
        grid=(steps,),
        in_specs=[*in_specs, *[anywhere] * len(into)],
        out_specs=out_specs,
        scratch_shapes=scratch,
        input_output_aliases={given + i: len(out_shape) - len(into) + i for i in range(len(into))},
        compiler_params=PARAMS,
        name=name,
    )

    def run(*values):
        kept = [v if s.memory_space == pltpu.SMEM or stays(v) else in_hbm(v)
                for v, s in zip(values, in_specs, strict=True)]
        return call(*kept, *[in_hbm(v) for v in into])

    return run


def hop_kernel(has_carry, choices, chunk, side, mine_ref, pair_ref, *refs):
    own, got = choose(refs[:choices], chunk), choose(refs[choices : 2 * choices], chunk)
    refs = refs[2 * choices :]
    if has_carry:
        carry_ref, next_ref, give_ref, keep_ref = refs
        carry = carry_ref[...].astype(F32)
    else:
        next_ref, give_ref, keep_ref = refs
        carry = jnp.zeros(next_ref.shape, F32)
    first = side == 0
    own, got = own.astype(F32), got.astype(F32)
    mine, pair = mine_ref[...], pair_ref[...]
    inner = jnp.where(first, mine, pair) * carry + jnp.where(first, own, got)
    next_ref[...] = (jnp.where(first, pair, mine) * inner + jnp.where(first, got, own)).astype(BF16)
    give_ref[...] = jnp.where(first, inner, carry).astype(BF16)
    keep_ref[...] = jnp.where(first, carry, inner).astype(BF16)


def in_hbm(value):
    return pltpu.with_memory_space_constraint(value, pltpu.HBM)


class Chain:
    def __init__(self, count, rates, sides, flip):
        self.count, self.rates, self.sides, self.flip = count, rates, sides, flip
        self.ranks = lax.axis_size("ctx")
        self.depth = self.ranks // 2
        self.steps = count + self.depth - 1
        self.carry = None
        self.starts = []

    def physical(self, r):
        return self.ranks - 1 - r if self.flip else r

    def live(self, s):
        return [z for z in range(self.depth) if 0 <= s - z < self.count]

    def swap(self, value, s=None):
        places = range(self.depth) if s is None else self.live(s)
        pairs = [(self.physical(2 * z + p), self.physical(2 * z + 1 - p)) for z in places for p in range(2)]
        return lax.ppermute(value, "ctx", pairs)

    def up(self, value, s):
        live = [z for z in self.live(s) if z + 1 < self.depth]
        pairs = [(self.physical(2 * z + p), self.physical(2 * z + 2 + p)) for z in live for p in range(2)]
        return lax.ppermute(value, "ctx", pairs) if pairs else None

    def step(self, s, owns, gots, *first):
        if self.carry is not None and self.flip:
            keep, back = self.starts[-1]
            self.carry, back, *_ = lax.optimization_barrier((self.carry, back, *first))
            self.starts[-1] = (keep, back)
        rows, lanes = gots[0].shape
        owns, gots = owns[: s + 1], gots[: s + 1]
        tile = lanes
        per = lanes // tile
        flat = pl.BlockSpec((rows, tile), lambda i, at: (0, i))
        flip, count = int(self.flip), self.count

        def chunk(at):
            return jnp.clip(s - at[2 + flip], 0, count - 1)

        line = pl.BlockSpec((1, tile), lambda i, at: (0, chunk(at) * per + i))
        carries = [] if self.carry is None else [self.carry]
        operands = [*self.rates, *owns, *gots, *carries]
        after, give, keep = pl.pallas_call(
            lambda at, *refs: hop_kernel(len(carries) > 0, len(owns), chunk(at), at[flip], *refs),
            out_shape=(jax.ShapeDtypeStruct((rows, lanes), BF16),) * 3,
            grid_spec=pltpu.PrefetchScalarGridSpec(
                num_scalar_prefetch=1,
                grid=(per,),
                in_specs=[line, line] + [flat] * (len(operands) - 2),
                out_specs=[flat] * 3,
            ),
            compiler_params=PARAMS,
            name="hop_back" if self.flip else "hop",
        )(self.sides, *operands)
        self.carry = self.up(after, s)
        self.starts.append((keep, self.swap(give, s)))

def body(proj_xbc, proj_dt, proj_gate, out_grad, conv_weight, conv_bias, decay_log, step_bias, skip_gain, norm_gain):
    x, dt, gate, og = proj_xbc[0], proj_dt[0], proj_gate[0], out_grad[0]
    length, channels = x.shape
    heads = dt.shape[1]
    inner = heads * HEAD_DIM
    ranks = lax.axis_size("ctx")
    shards = lax.axis_size("fsdp")
    per_group = heads // GROUPS
    width = per_group * HEAD_DIM
    side = lax.axis_index("ctx") % 2
    place = lax.axis_index("ctx") // 2
    sides = jnp.stack([side, 1 - side, place, ranks // 2 - 1 - place]).astype(jnp.int32)
    part = inner // CHUNKS
    per = part // width
    c_loc, g_loc, h_loc = channels // shards, inner // shards, heads // shards
    spare = c_loc - g_loc - 3 * h_loc
    groups = GROUPS
    blocks = channels // width

    ahead = [(i, i + 1) for i in range(ranks - 1)]
    behind = [(i + 1, i) for i in range(ranks - 1)]
    halo = lax.ppermute(x[length - HALO :, :], "ctx", ahead)

    def pack_row(gain, decay, step, skip):
        return jnp.concatenate([gain, decay, step, skip, jnp.zeros(gain.shape[:-1] + (spare,), F32)], axis=-1)

    packed = jnp.concatenate(
        [conv_weight, conv_bias[None], pack_row(norm_gain, decay_log, step_bias, skip_gain)[None],
         jnp.zeros((8 - KERNEL - 2, c_loc), F32)], axis=0)
    full = lax.all_gather(packed, "fsdp", axis=1, tiled=True)
    extra = full[KERNEL + 1].reshape(shards, c_loc)
    gain = extra[:, :g_loc].reshape(1, inner)
    decay = extra[:, g_loc : g_loc + h_loc].reshape(1, heads)
    step_b = extra[:, g_loc + h_loc : g_loc + 2 * h_loc].reshape(1, heads)
    skip = extra[:, g_loc + 2 * h_loc : g_loc + 3 * h_loc].reshape(1, heads)
    skip_x = jnp.repeat(skip, HEAD_DIM, axis=1)

    def spec(shape, where):
        return pl.BlockSpec(shape, where)

    def shape(dims, kind):
        return jax.ShapeDtypeStruct(dims, kind)

    table = spec((length, heads), lambda i: (0, 0))
    row_head = spec((1, heads), lambda i: (0, 0))
    scalars = pl.BlockSpec(memory_space=pltpu.SMEM)
    wide_out = spec((length, width), lambda i: (0, i))
    half_out = spec((STATE // 2, width), lambda i: (0, i))
    window = pltpu.VMEM((PAD + length, width), F32)
    wide_bf, half_bf = shape((length, part), BF16), shape((STATE // 2, part), BF16)
    grad_shapes = (shape((length, channels), BF16), shape((HALO, channels), F32), shape((HALO, channels), F32),
                   shape((8, channels), F32))

    def conv_specs(first):
        return [spec((rows, width), lambda i: (0, first + i)) for rows in (length, HALO, 8)]

    def cols(rows, first):
        return spec((rows, width), lambda i: (0, first + i))

    def head_cols(first):
        return [spec((length, STATE), lambda i: (0, first + i)), spec((length, STATE), lambda i: (0, GROUPS + first + i))]

    kq, ec, ei, et = grid_call(
        lambda *refs: keys_kernel(per_group, *refs), "keys", 2,
        out_shape=(shape((length, 2 * width), BF16), shape((length, heads), F32), shape((length, heads), F32),
                   shape((1, inner), F32)),
        in_specs=conv_specs(GROUPS) + [table, row_head, row_head],
        out_specs=(wide_out, table, table, spec((1, inner), lambda i: (0, 0))),
        scratch=[window],
    )(x, halo, full, dt, step_b, decay)
    rates = (et, lax.ppermute(et, "ctx", [(i, i ^ 1) for i in range(ranks)]))

    def front(c):
        first = c * per
        return grid_call(
            lambda *refs: front_kernel(per_group, first, *refs), "front", per,
            out_shape=(wide_bf, wide_bf, half_bf, half_bf),
            in_specs=conv_specs(first) + head_cols(first)[:1] + [table, cols(1, first), scalars],
            out_specs=(wide_out, wide_out, half_out, half_out),
            scratch=[window],
        )(x, halo, full, kq, ei, et, sides)

    def middle(c):
        first = c * per
        near = fore.starts[c : c + depth]
        return grid_call(
            lambda *refs: middle_kernel(per_group, first, depth, *refs), "middle", per,
            out_shape=(wide_bf, wide_bf, shape((STATE, part), BF16), half_bf, half_bf, shape((length, heads), F32),
                       shape((length, inner), BF16), shape((8, inner), F32)),
            in_specs=[wide_out, *head_cols(first), wide_out, table, cols(length, first), cols(length, first),
                      cols(1, first), cols(1, first), scalars] + [half_out] * (2 * depth),
            out_specs=(wide_out, wide_out, spec((STATE, width), lambda i: (0, i)), half_out, half_out, table,
                       cols(length, first), cols(8, first)),
            into=mids[-1][6:] if mids else (),
        )(fronts[c][0], kq, kq, fronts[c][1], ec, gate, og, gain, skip_x, sides,
          *[n[0] for n in near], *[n[1] for n in near])

    def back(c):
        first = c * per
        near = aft.starts[c : c + depth]
        dy, dyp, st = mids[c][:3]
        return grid_call(
            lambda *refs: back_kernel(per_group, first, depth, *refs), "back", per,
            out_shape=(shape((2, length, per * STATE), F32), shape((length, heads), F32), shape((8, heads), F32),
                       *grad_shapes),
            in_specs=[*head_cols(first), wide_out, spec((STATE, width), lambda i: (0, i)), wide_out, wide_out,
                      *conv_specs(first), cols(1, first), cols(1, first), table, scalars] + [half_out] * (2 * depth),
            out_specs=(spec((2, length, STATE), lambda i: (0, 0, i)), table, spec((8, heads), lambda i: (0, 0)),
                       cols(length, first), cols(HALO, first), cols(HALO, first), cols(8, first)),
            scratch=[window, window],
            into=backs[-1][3:] if backs else (),
        )(kq, kq, fronts[c][1], st, dy, dyp, x, halo, full, skip_x, et, ei, sides,
          *[n[0] for n in near], *[n[1] for n in near])

    fore, aft = Chain(CHUNKS, rates, sides, False), Chain(CHUNKS, rates, sides, True)
    depth, steps = fore.depth, fore.steps
    fronts, mids, backs, got, got_back = [], [], [], [], []
    for u in range(CHUNKS + 2 * depth + 1):
        if u < CHUNKS:
            fronts.append(front(u))
            got.append(fore.swap(fronts[u][3]))
        if u < steps:
            fore.step(u, [f[2] for f in fronts], got)
        if depth <= u < depth + CHUNKS:
            mids.append(middle(u - depth))
            got_back.append(fore.swap(mids[-1][4]))
        if depth + 1 <= u < depth + 1 + steps:
            aft.step(u - depth - 1, [m[3] for m in mids], got_back, *[b[2] for b in backs[-1:]])
        if u >= 2 * depth + 1:
            backs.append(back(u - 2 * depth - 1))

    grad_dt, hs, gx, lead, tail, wr = grid_call(
        lambda *refs: last_kernel(CHUNKS, *refs), "last", 2,
        out_shape=(shape((length, heads), F32), shape((8, heads), F32), *grad_shapes),
        in_specs=conv_specs(GROUPS) + [table, row_head, row_head]
        + [spec((1, length, per * STATE), lambda i: (i, 0, 0))] * CHUNKS + [table] * (2 * CHUNKS)
        + [spec((8, heads), lambda i: (0, 0))] * CHUNKS,
        out_specs=(table, spec((8, heads), lambda i: (0, 0)), cols(length, GROUPS), cols(HALO, GROUPS),
                   cols(HALO, GROUPS), cols(8, GROUPS)),
        scratch=[window, window],
        into=backs[-1][3:],
    )(x, halo, full, dt, step_b, decay, *[b[0] for b in backs], *[m[5] for m in mids], *[b[1] for b in backs],
      *[b[2] for b in backs])
    grad_gate, sums = mids[-1][6:]

    next_gp = lax.ppermute(lead, "ctx", behind)
    fixed = []
    for i in range(HALO):
        row = tail[i]
        for k in range(i + 1):
            row = row + full[k] * next_gp[i - k]
        fixed.append(row)
    grad_xbc = lax.dynamic_update_slice(gx, jnp.stack(fixed).astype(BF16), (length - HALO, 0))

    skip_grad = jnp.sum(sums[1].reshape(heads, HEAD_DIM), axis=1)
    extra_row = pack_row(
        sums[0].reshape(shards, g_loc), hs[0].reshape(shards, h_loc), hs[1].reshape(shards, h_loc),
        skip_grad.reshape(shards, h_loc)).reshape(1, channels)
    parts = jnp.concatenate([wr[: KERNEL + 1], extra_row, jnp.zeros((8 - KERNEL - 2, channels), F32)], axis=0)
    split = ranks // 8
    piece = c_loc // split
    parts = parts.reshape(8, shards, split, piece).transpose(0, 2, 1, 3).reshape(ranks * shards, piece)
    summed = jnp.sum(lax.all_to_all(parts, ("ctx", "fsdp"), 0, 0, tiled=True), axis=0)
    summed = summed * (1.0 / math.sqrt(length * ranks * shards))
    copies = jnp.broadcast_to(summed[None], (ranks, piece))
    mine = lax.all_to_all(copies, "ctx", 0, 0, tiled=True).reshape(8, c_loc)
    ends = mine[KERNEL + 1]
    return (
        grad_xbc[None],
        grad_dt[None],
        grad_gate[None],
        mine[:KERNEL],
        mine[KERNEL],
        ends[g_loc : g_loc + h_loc],
        ends[g_loc + h_loc : g_loc + 2 * h_loc],
        ends[g_loc + 2 * h_loc : g_loc + 3 * h_loc],
        ends[:g_loc],
    )


def solution(mesh):
    data = P("fsdp", "ctx", None)
    one = P("fsdp")
    return jax.shard_map(
        body,
        mesh=mesh,
        in_specs=(data, data, data, data, P(None, "fsdp"), one, one, one, one, one),
        out_specs=(data, data, data, P(None, "fsdp"), one, one, one, one, one),
        check_vma=False,
    )
```

```python
import math

import jax
import jax.numpy as jnp
from jax import lax
from jax.experimental import pallas as pl
from jax.experimental.pallas import tpu as pltpu
from jax.sharding import PartitionSpec as P

HEAD_DIM = 64
STATE = 128
GROUPS = 8
KERNEL = 4
EPSILON = 1e-05
HALO = KERNEL - 1
PAD = 8
CHUNKS = 4
F32 = jnp.float32
BF16 = jnp.bfloat16
HIGHEST = lax.Precision.HIGHEST


def mm(a, b):
    return jnp.dot(a, b, preferred_element_type=F32)


def mm_nt(a, b):
    return lax.dot_general(a, b, (((1,), (1,)), ((), ())), preferred_element_type=F32)


def sigmoid(v):
    return 0.5 * jnp.tanh(0.5 * v) + 0.5


def softplus(v):
    return jnp.maximum(v, 0.0) + jnp.log(1.0 + jnp.exp(-jnp.abs(v)))


def spread_heads(table, group, per_group):
    heads = table.shape[1]
    table = pltpu.roll(table, lax.rem(heads - group * per_group, heads), 1)
    rows = table.shape[0]
    pair = 128 // HEAD_DIM
    lane = lax.broadcasted_iota(jnp.int32, (rows, 128), 1)
    tiles = []
    for i in range(per_group // pair):
        tile = jnp.broadcast_to(table[:, pair * i : pair * i + 1], (rows, 128))
        for p in range(1, pair):
            col = jnp.broadcast_to(table[:, pair * i + p : pair * i + p + 1], (rows, 128))
            tile = jnp.where(lane >= p * HEAD_DIM, col, tile)
        tiles.append(tile)
    return jnp.concatenate(tiles, axis=1)


def sum_heads(values, group, per_group, heads):
    width = values.shape[1]
    row = lax.broadcasted_iota(jnp.int32, (width, heads), 0) // HEAD_DIM + group * per_group
    col = lax.broadcasted_iota(jnp.int32, (width, heads), 1)
    pick = jnp.where(row == col, 1.0, 0.0).astype(BF16)
    high = values.astype(BF16)
    low = (values - high.astype(F32)).astype(BF16)
    return mm(high, pick) + mm(low, pick)


def lower_mask(n):
    return lax.broadcasted_iota(jnp.int32, (n, n), 0) >= lax.broadcasted_iota(jnp.int32, (n, n), 1)


def upper_mask(n):
    return lax.broadcasted_iota(jnp.int32, (n, n), 0) <= lax.broadcasted_iota(jnp.int32, (n, n), 1)


def fill_window(x_ref, halo_ref, xs):
    xs[PAD - HALO : PAD, :] = halo_ref[...].astype(F32)
    xs[PAD : PAD + x_ref.shape[0], :] = x_ref[...].astype(F32)


def conv_pre(x_ref, halo_ref, w_ref, xs):
    length = x_ref.shape[0]
    fill_window(x_ref, halo_ref, xs)
    pre = jnp.broadcast_to(w_ref[KERNEL : KERNEL + 1, :], (length, x_ref.shape[1]))
    for k in range(KERNEL):
        pre = pre + w_ref[k : k + 1, :] * xs[PAD - HALO + k : PAD - HALO + k + length, :]
    return pre


def split_halves(state, mine, own_ref, send_ref):
    half = state.shape[0] // 2
    low, high = state[:half].astype(BF16), state[half:].astype(BF16)
    shape = own_ref.shape
    own_ref[...] = jnp.where(mine == 0, low, high).reshape(shape)
    send_ref[...] = jnp.where(mine == 0, high, low).reshape(shape)


def keys_kernel(per_group, x_ref, halo_ref, w_ref, dt_ref, sb_ref, dl_ref, kq_ref, ec_ref, ei_ref, et_ref, xs):
    length = x_ref.shape[0]

    @pl.when(pl.program_id(0) == 0)
    def _():
        step = softplus(dt_ref[...].astype(F32) + sb_ref[...])
        ld = -jnp.exp(dl_ref[...]) * step
        tril = jnp.where(lower_mask(length), 1.0, 0.0).astype(F32)
        cum = jnp.dot(tril, ld, precision=HIGHEST, preferred_element_type=F32)
        ec = jnp.exp(cum)
        ec_ref[...] = ec
        ei_ref[...] = jnp.exp(-cum) * step
        width = per_group * HEAD_DIM
        for g in range(GROUPS):
            et_ref[:, g * width : (g + 1) * width] = spread_heads(ec[length - 8 :, :], g, per_group)[7:8, :]

    pre = conv_pre(x_ref, halo_ref, w_ref, xs)
    kq_ref[...] = (pre * sigmoid(pre)).astype(BF16)


def front_kernel(per_group, first, x_ref, halo_ref, w_ref, k_ref, ei_ref, et_ref,
                 side_ref, mixed_ref, vp_ref, own_ref, send_ref, xs):
    g = first + pl.program_id(0)
    pre = conv_pre(x_ref, halo_ref, w_ref, xs)
    mixed = (pre * sigmoid(pre)).astype(BF16)
    mixed_ref[...] = mixed
    vp = (mixed.astype(F32) * spread_heads(ei_ref[...], g, per_group)).astype(BF16)
    vp_ref[...] = vp
    ut = mm(k_ref[...].astype(F32).T.astype(BF16), vp) * et_ref[...]
    split_halves(ut, side_ref[0], own_ref, send_ref)


def choose(refs, pick):
    value = refs[0][...]
    for i in range(1, len(refs)):
        value = jnp.where(pick == i, refs[i][...], value)
    return value


def join_halves(own, other, mine):
    return jnp.concatenate([jnp.where(mine == 0, own, other), jnp.where(mine == 0, other, own)], axis=0)


def middle_kernel(per_group, first, depth, v_ref, k_ref, q_ref, vp_ref, ec_ref, gate_ref, og_ref, gain_ref, skip_ref,
                  side_ref, *refs):
    keeps, backs = refs[:depth], refs[depth : 2 * depth]
    dy_ref, dyp_ref, st_ref, own_ref, send_ref, a1_ref, gg_ref, rows_ref = refs[2 * depth :]
    st = join_halves(choose(keeps, side_ref[2]), choose(backs, side_ref[2]), side_ref[0])
    st_ref[...] = st
    g = first + pl.program_id(0)
    length, width = v_ref.shape
    heads = ec_ref.shape[1]
    q = q_ref[...]
    z = jnp.where(lower_mask(length), mm_nt(q, k_ref[...]), 0.0).astype(BF16)
    yn = mm(jnp.concatenate([z, q], axis=1), jnp.concatenate([vp_ref[...], st], axis=0))
    ecx = spread_heads(ec_ref[...], g, per_group)
    v = v_ref[...].astype(F32)
    y = (ecx * yn + skip_ref[...] * v).astype(BF16).astype(F32)
    gate = gate_ref[...].astype(F32)
    og = og_ref[...].astype(F32)
    sig = sigmoid(gate)
    act = gate * sig
    gated = y * act
    scale = lax.rsqrt(jnp.sum(gated * gated, axis=1, keepdims=True) * (1.0 / width) + EPSILON)
    dgn = og * gain_ref[...]
    inner = jnp.sum(dgn * gated, axis=1, keepdims=True) * (1.0 / width)
    dgated = scale * dgn - gated * (scale * scale * scale * inner)
    dyb = (dgated * act).astype(BF16)
    dy_ref[...] = dyb
    gg_ref[...] = (dgated * y * (sig + act * (1.0 - sig))).astype(BF16)
    dy = dyb.astype(F32)
    dyp = (ecx * dy).astype(BF16)
    dyp_ref[...] = dyp
    gt = mm(q.astype(F32).T.astype(BF16), dyp)
    split_halves(gt, side_ref[1], own_ref, send_ref)
    rows_ref[...] = jnp.zeros(rows_ref.shape, F32)
    rows_ref[0:1, :] = jnp.sum(og * gated * scale, axis=0, keepdims=True)
    rows_ref[1:2, :] = jnp.sum(dy * v, axis=0, keepdims=True)

    @pl.when(pl.program_id(0) == 0)
    def _():
        a1_ref[...] = jnp.zeros(a1_ref.shape, F32)

    a1_ref[...] += sum_heads(dyp.astype(F32) * yn, g, per_group, heads)


def slope_of(pre):
    sig = sigmoid(pre)
    return sig * (1.0 + pre * (1.0 - sig))


def conv_back(gp, w_ref, gx_ref, lead_ref, tail_ref, wr_ref, xs, gs):
    length = gp.shape[0]
    gs[0:length, :] = gp
    gs[length:, :] = jnp.zeros((gs.shape[0] - length, gs.shape[1]), F32)
    wr_ref[...] = jnp.zeros(wr_ref.shape, F32)
    total = jnp.zeros(gp.shape, F32)
    for k in range(KERNEL):
        lead = HALO - k
        total = total + w_ref[k : k + 1, :] * gs[lead : lead + length, :]
        wr_ref[k : k + 1, :] = jnp.sum(gp * xs[PAD - HALO + k : PAD - HALO + k + length, :], axis=0, keepdims=True)
    wr_ref[KERNEL : KERNEL + 1, :] = jnp.sum(gp, axis=0, keepdims=True)
    gx_ref[...] = total.astype(BF16)
    lead_ref[...] = gp[0:HALO, :]
    tail_ref[...] = total[length - HALO : length, :]


def back_kernel(per_group, first, depth, k_ref, q_ref, vp_ref, st_ref, dy_ref, dyp_ref, x_ref, halo_ref, w_ref,
                skip_ref, et_ref, ei_ref, side_ref, *refs):
    keeps, backs = refs[:depth], refs[depth : 2 * depth]
    dkq_ref, a2_ref, last_ref, gx_ref, lead_ref, tail_ref, wr_ref, xs, gs = refs[2 * depth :]
    j = first + pl.program_id(0)
    length, width = x_ref.shape
    heads = ei_ref.shape[1]

    @pl.when(pl.program_id(0) == 0)
    def _():
        a2_ref[...] = jnp.zeros(a2_ref.shape, F32)
        last_ref[...] = jnp.zeros(last_ref.shape, F32)

    k = k_ref[...]
    q = q_ref[...]
    vp = vp_ref[...]
    dyp = dyp_ref[...]
    st = st_ref[...]
    en = join_halves(choose(keeps, side_ref[3]), choose(backs, side_ref[3]), side_ref[1])
    en = (et_ref[...] * en.astype(F32)).astype(BF16)
    zt = jnp.where(upper_mask(length), mm_nt(k, q), 0.0).astype(BF16)
    dvp = mm(jnp.concatenate([zt, k], axis=1), jnp.concatenate([dyp, en], axis=0))
    grads = spread_heads(ei_ref[...], j, per_group) * dvp + skip_ref[...] * dy_ref[...].astype(F32)
    a2_ref[...] += sum_heads(vp.astype(F32) * dvp, j, per_group, heads)
    ends = en.astype(F32) * (st.astype(F32) + mm(k.astype(F32).T.astype(BF16), vp))
    ends = jnp.broadcast_to(jnp.sum(ends, axis=0, keepdims=True), (8, width))
    last_ref[...] += sum_heads(ends, j, per_group, heads)
    dz = jnp.where(lower_mask(length), mm_nt(dyp, vp), 0.0)
    dkq_ref[0] = mm(dz.T.astype(BF16), q) + mm_nt(vp, en)
    dkq_ref[1] = mm(dz.astype(BF16), k) + mm_nt(dyp, st)
    gp = grads * slope_of(conv_pre(x_ref, halo_ref, w_ref, xs))
    conv_back(gp, w_ref, gx_ref, lead_ref, tail_ref, wr_ref, xs, gs)


def before_kernel(k_ref, q_ref, vp_ref, st_ref, dyp_ref, x_ref, halo_ref, w_ref,
                  dkq_ref, dvp_ref, slope_ref, both_ref, xs):
    length = x_ref.shape[0]
    k, q, vp, dyp, st = k_ref[...], q_ref[...], vp_ref[...], dyp_ref[...], st_ref[...]
    zt = jnp.where(upper_mask(length), mm_nt(k, q), 0.0).astype(BF16)
    dvp_ref[...] = mm(zt, dyp)
    both_ref[...] = st.astype(F32) + mm(k.astype(F32).T.astype(BF16), vp)
    dz = jnp.where(lower_mask(length), mm_nt(dyp, vp), 0.0)
    dkq_ref[0] = mm(dz.T.astype(BF16), q)
    dkq_ref[1] = mm(dz.astype(BF16), k) + mm_nt(dyp, st)
    slope_ref[...] = slope_of(conv_pre(x_ref, halo_ref, w_ref, xs))


def after_kernel(per_group, first, depth, k_ref, vp_ref, dkq0_ref, dvp_ref, slope_ref, both_ref, dy_ref, x_ref, halo_ref,
                w_ref, skip_ref, et_ref, ei_ref, side_ref, *refs):
    keeps, backs = refs[:depth], refs[depth : 2 * depth]
    dkq_ref, a2_ref, last_ref, gx_ref, lead_ref, tail_ref, wr_ref, xs, gs = refs[2 * depth :]
    j = first + pl.program_id(0)
    width = x_ref.shape[1]
    heads = ei_ref.shape[1]

    @pl.when(pl.program_id(0) == 0)
    def _():
        a2_ref[...] = jnp.zeros(a2_ref.shape, F32)
        last_ref[...] = jnp.zeros(last_ref.shape, F32)

    vp = vp_ref[...]
    en = join_halves(choose(keeps, side_ref[3]), choose(backs, side_ref[3]), side_ref[1])
    en = (et_ref[...] * en.astype(F32)).astype(BF16)
    dvp = dvp_ref[...] + mm(k_ref[...], en)
    grads = spread_heads(ei_ref[...], j, per_group) * dvp + skip_ref[...] * dy_ref[...].astype(F32)
    a2_ref[...] += sum_heads(vp.astype(F32) * dvp, j, per_group, heads)
    ends = jnp.broadcast_to(jnp.sum(en.astype(F32) * both_ref[...], axis=0, keepdims=True), (8, width))
    last_ref[...] += sum_heads(ends, j, per_group, heads)
    dkq_ref[0] = dkq0_ref[0] + mm_nt(vp, en)
    dkq_ref[1] = dkq0_ref[1]
    fill_window(x_ref, halo_ref, xs)
    conv_back(grads * slope_ref[...], w_ref, gx_ref, lead_ref, tail_ref, wr_ref, xs, gs)


def last_kernel(count, x_ref, halo_ref, w_ref, dt_ref, sb_ref, dl_ref, *refs):
    dkq, a1, a2, last = (refs[i * count : (i + 1) * count] for i in range(4))
    gdt_ref, hs_ref, gx_ref, lead_ref, tail_ref, wr_ref, xs, gs = refs[4 * count :]
    grads = jnp.concatenate([ref[0] for ref in dkq], axis=1)
    gp = grads * slope_of(conv_pre(x_ref, halo_ref, w_ref, xs))
    conv_back(gp, w_ref, gx_ref, lead_ref, tail_ref, wr_ref, xs, gs)

    @pl.when(pl.program_id(0) == 0)
    def _():
        length, heads = dt_ref.shape
        raw = dt_ref[...].astype(F32) + sb_ref[...]
        step = softplus(raw)
        rate = jnp.exp(dl_ref[...])
        row = lax.broadcasted_iota(jnp.int32, (length, heads), 0)
        down = sum(ref[...] for ref in a2)
        end = sum(ref[...] for ref in last)[0:1, :]
        dcum = sum(ref[...] for ref in a1) - down + jnp.where(row == length - 1, end, 0.0)
        triu = jnp.where(upper_mask(length), 1.0, 0.0).astype(F32)
        dld = jnp.dot(triu, dcum, precision=HIGHEST, preferred_element_type=F32)
        gdt = (down / step - rate * dld) * sigmoid(raw)
        gdt_ref[...] = gdt
        hs_ref[...] = jnp.zeros(hs_ref.shape, F32)
        hs_ref[0:1, :] = jnp.sum(-rate * step * dld, axis=0, keepdims=True)
        hs_ref[1:2, :] = jnp.sum(gdt, axis=0, keepdims=True)


PARAMS = pltpu.CompilerParams(vmem_limit_bytes=40 * 1024 * 1024)


def grid_call(kernel, name, steps, in_specs, out_specs, out_shape, scratch=(), into=()):
    given = len(in_specs)
    anywhere = pl.BlockSpec(memory_space=pl.ANY)

    def stays(s):
        return s.shape[0] in (2, STATE // 2) or s.shape == (8, STATE)

    def place(s):
        return s if stays(s) else pltpu.HBM(s.shape, s.dtype)

    call = pl.pallas_call(
        lambda *refs: kernel(*refs[:given], *refs[given + len(into) :]),
        out_shape=tuple(place(s) for s in out_shape),
        grid=(steps,),
        in_specs=[*in_specs, *[anywhere] * len(into)],
        out_specs=out_specs,
        scratch_shapes=scratch,
        input_output_aliases={given + i: len(out_shape) - len(into) + i for i in range(len(into))},
        compiler_params=PARAMS,
        name=name,
    )

    def run(*values):
        kept = [v if s.memory_space == pltpu.SMEM or stays(v) else in_hbm(v)
                for v, s in zip(values, in_specs, strict=True)]
        return call(*kept, *[in_hbm(v) for v in into])

    return run


def hop_kernel(has_carry, choices, chunk, side, mine_ref, pair_ref, *refs):
    own, got = choose(refs[:choices], chunk), choose(refs[choices : 2 * choices], chunk)
    refs = refs[2 * choices :]
    if has_carry:
        carry_ref, next_ref, give_ref, keep_ref = refs
        carry = carry_ref[...].astype(F32)
    else:
        next_ref, give_ref, keep_ref = refs
        carry = jnp.zeros(next_ref.shape, F32)
    first = side == 0
    own, got = own.astype(F32), got.astype(F32)
    mine, pair = mine_ref[...], pair_ref[...]
    inner = jnp.where(first, mine, pair) * carry + jnp.where(first, own, got)
    next_ref[...] = (jnp.where(first, pair, mine) * inner + jnp.where(first, got, own)).astype(BF16)
    give_ref[...] = jnp.where(first, inner, carry).astype(BF16)
    keep_ref[...] = jnp.where(first, carry, inner).astype(BF16)


def in_hbm(value):
    return pltpu.with_memory_space_constraint(value, pltpu.HBM)


class Chain:
    def __init__(self, count, rates, sides, flip):
        self.count, self.rates, self.sides, self.flip = count, rates, sides, flip
        self.ranks = lax.axis_size("ctx")
        self.depth = self.ranks // 2
        self.steps = count + self.depth - 1
        self.carry = None
        self.starts = []

    def physical(self, r):
        return self.ranks - 1 - r if self.flip else r

    def live(self, s):
        return [z for z in range(self.depth) if 0 <= s - z < self.count]

    def swap(self, value, s=None):
        places = range(self.depth) if s is None else self.live(s)
        pairs = [(self.physical(2 * z + p), self.physical(2 * z + 1 - p)) for z in places for p in range(2)]
        return lax.ppermute(value, "ctx", pairs)

    def up(self, value, s):
        live = [z for z in self.live(s) if z + 1 < self.depth]
        pairs = [(self.physical(2 * z + p), self.physical(2 * z + 2 + p)) for z in live for p in range(2)]
        return lax.ppermute(value, "ctx", pairs) if pairs else None

    def step(self, s, owns, gots, *first):
        if self.carry is not None and self.flip:
            keep, back = self.starts[-1]
            self.carry, back, *_ = lax.optimization_barrier((self.carry, back, *first))
            self.starts[-1] = (keep, back)
        rows, lanes = gots[0].shape
        owns, gots = owns[: s + 1], gots[: s + 1]
        tile = lanes
        per = lanes // tile
        flat = pl.BlockSpec((rows, tile), lambda i, at: (0, i))
        flip, count = int(self.flip), self.count

        def chunk(at):
            return jnp.clip(s - at[2 + flip], 0, count - 1)

        line = pl.BlockSpec((1, tile), lambda i, at: (0, chunk(at) * per + i))
        carries = [] if self.carry is None else [self.carry]
        operands = [*self.rates, *owns, *gots, *carries]
        after, give, keep = pl.pallas_call(
            lambda at, *refs: hop_kernel(len(carries) > 0, len(owns), chunk(at), at[flip], *refs),
            out_shape=(jax.ShapeDtypeStruct((rows, lanes), BF16),) * 3,
            grid_spec=pltpu.PrefetchScalarGridSpec(
                num_scalar_prefetch=1,
                grid=(per,),
                in_specs=[line, line] + [flat] * (len(operands) - 2),
                out_specs=[flat] * 3,
            ),
            compiler_params=PARAMS,
            name="hop_back" if self.flip else "hop",
        )(self.sides, *operands)
        self.carry = self.up(after, s)
        self.starts.append((keep, self.swap(give, s)))

def body(proj_xbc, proj_dt, proj_gate, out_grad, conv_weight, conv_bias, decay_log, step_bias, skip_gain, norm_gain):
    x, dt, gate, og = proj_xbc[0], proj_dt[0], proj_gate[0], out_grad[0]
    length, channels = x.shape
    heads = dt.shape[1]
    inner = heads * HEAD_DIM
    ranks = lax.axis_size("ctx")
    shards = lax.axis_size("fsdp")
    per_group = heads // GROUPS
    width = per_group * HEAD_DIM
    side = lax.axis_index("ctx") % 2
    place = lax.axis_index("ctx") // 2
    sides = jnp.stack([side, 1 - side, place, ranks // 2 - 1 - place]).astype(jnp.int32)
    part = inner // CHUNKS
    per = part // width
    c_loc, g_loc, h_loc = channels // shards, inner // shards, heads // shards
    spare = c_loc - g_loc - 3 * h_loc
    groups = GROUPS
    blocks = channels // width

    ahead = [(i, i + 1) for i in range(ranks - 1)]
    behind = [(i + 1, i) for i in range(ranks - 1)]
    halo = lax.ppermute(x[length - HALO :, :], "ctx", ahead)

    def pack_row(gain, decay, step, skip):
        return jnp.concatenate([gain, decay, step, skip, jnp.zeros(gain.shape[:-1] + (spare,), F32)], axis=-1)

    packed = jnp.concatenate(
        [conv_weight, conv_bias[None], pack_row(norm_gain, decay_log, step_bias, skip_gain)[None],
         jnp.zeros((8 - KERNEL - 2, c_loc), F32)], axis=0)
    full = lax.all_gather(packed, "fsdp", axis=1, tiled=True)
    extra = full[KERNEL + 1].reshape(shards, c_loc)
    gain = extra[:, :g_loc].reshape(1, inner)
    decay = extra[:, g_loc : g_loc + h_loc].reshape(1, heads)
    step_b = extra[:, g_loc + h_loc : g_loc + 2 * h_loc].reshape(1, heads)
    skip = extra[:, g_loc + 2 * h_loc : g_loc + 3 * h_loc].reshape(1, heads)
    skip_x = jnp.repeat(skip, HEAD_DIM, axis=1)

    def spec(shape, where):
        return pl.BlockSpec(shape, where)

    def shape(dims, kind):
        return jax.ShapeDtypeStruct(dims, kind)

    table = spec((length, heads), lambda i: (0, 0))
    row_head = spec((1, heads), lambda i: (0, 0))
    scalars = pl.BlockSpec(memory_space=pltpu.SMEM)
    wide_out = spec((length, width), lambda i: (0, i))
    half_out = spec((STATE // 2, width), lambda i: (0, i))
    window = pltpu.VMEM((PAD + length, width), F32)
    wide_bf, half_bf = shape((length, part), BF16), shape((STATE // 2, part), BF16)
    grad_shapes = (shape((length, channels), BF16), shape((HALO, channels), F32), shape((HALO, channels), F32),
                   shape((8, channels), F32))

    def conv_specs(first):
        return [spec((rows, width), lambda i: (0, first + i)) for rows in (length, HALO, 8)]

    def cols(rows, first):
        return spec((rows, width), lambda i: (0, first + i))

    def head_cols(first):
        return [spec((length, STATE), lambda i: (0, first + i)), spec((length, STATE), lambda i: (0, GROUPS + first + i))]

    kq, ec, ei, et = grid_call(
        lambda *refs: keys_kernel(per_group, *refs), "keys", 2,
        out_shape=(shape((length, 2 * width), BF16), shape((length, heads), F32), shape((length, heads), F32),
                   shape((1, inner), F32)),
        in_specs=conv_specs(GROUPS) + [table, row_head, row_head],
        out_specs=(wide_out, table, table, spec((1, inner), lambda i: (0, 0))),
        scratch=[window],
    )(x, halo, full, dt, step_b, decay)
    rates = (et, lax.ppermute(et, "ctx", [(i, i ^ 1) for i in range(ranks)]))

    def front(c):
        first = c * per
        return grid_call(
            lambda *refs: front_kernel(per_group, first, *refs), "front", per,
            out_shape=(wide_bf, wide_bf, half_bf, half_bf),
            in_specs=conv_specs(first) + head_cols(first)[:1] + [table, cols(1, first), scalars],
            out_specs=(wide_out, wide_out, half_out, half_out),
            scratch=[window],
        )(x, halo, full, kq, ei, et, sides)

    def middle(c):
        first = c * per
        near = fore.starts[c : c + depth]
        return grid_call(
            lambda *refs: middle_kernel(per_group, first, depth, *refs), "middle", per,
            out_shape=(wide_bf, wide_bf, shape((STATE, part), BF16), half_bf, half_bf, shape((length, heads), F32),
                       shape((length, inner), BF16), shape((8, inner), F32)),
            in_specs=[wide_out, *head_cols(first), wide_out, table, cols(length, first), cols(length, first),
                      cols(1, first), cols(1, first), scalars] + [half_out] * (2 * depth),
            out_specs=(wide_out, wide_out, spec((STATE, width), lambda i: (0, i)), half_out, half_out, table,
                       cols(length, first), cols(8, first)),
            into=mids[-1][6:] if mids else (),
        )(fronts[c][0], kq, kq, fronts[c][1], ec, gate, og, gain, skip_x, sides,
          *[n[0] for n in near], *[n[1] for n in near])

    def back(c):
        first = c * per
        near = aft.starts[c : c + depth]
        dy, dyp, st = mids[c][:3]
        return grid_call(
            lambda *refs: back_kernel(per_group, first, depth, *refs), "back", per,
            out_shape=(shape((2, length, per * STATE), F32), shape((length, heads), F32), shape((8, heads), F32),
                       *grad_shapes),
            in_specs=[*head_cols(first), wide_out, spec((STATE, width), lambda i: (0, i)), wide_out, wide_out,
                      *conv_specs(first), cols(1, first), cols(1, first), table, scalars] + [half_out] * (2 * depth),
            out_specs=(spec((2, length, STATE), lambda i: (0, 0, i)), table, spec((8, heads), lambda i: (0, 0)),
                       cols(length, first), cols(HALO, first), cols(HALO, first), cols(8, first)),
            scratch=[window, window],
            into=backs[-1][3:] if backs else (),
        )(kq, kq, fronts[c][1], st, dy, dyp, x, halo, full, skip_x, et, ei, sides,
          *[n[0] for n in near], *[n[1] for n in near])

    def before(c, gate):
        first = c * per
        dyp, st = mids[c][1:3]
        near_halo, _ = lax.optimization_barrier((halo, gate))
        return grid_call(
            before_kernel, "before", per,
            out_shape=(shape((2, length, per * STATE), F32), shape((length, part), F32), shape((length, part), F32),
                       shape((STATE, part), F32)),
            in_specs=[*head_cols(first), wide_out, spec((STATE, width), lambda i: (0, i)), wide_out, *conv_specs(first)],
            out_specs=(spec((2, length, STATE), lambda i: (0, 0, i)), wide_out, wide_out,
                       spec((STATE, width), lambda i: (0, i))),
            scratch=[window],
        )(kq, kq, fronts[c][1], st, dyp, x, near_halo, full)

    def after(c):
        first = c * per
        near = aft.starts[c : c + depth]
        return grid_call(
            lambda *refs: after_kernel(per_group, first, depth, *refs), "after", per,
            out_shape=(shape((2, length, per * STATE), F32), shape((length, heads), F32), shape((8, heads), F32),
                       *grad_shapes),
            in_specs=[head_cols(first)[0], wide_out, spec((2, length, STATE), lambda i: (0, 0, i)), wide_out, wide_out,
                      spec((STATE, width), lambda i: (0, i)), wide_out, *conv_specs(first), cols(1, first),
                      cols(1, first), table, scalars] + [half_out] * (2 * depth),
            out_specs=(spec((2, length, STATE), lambda i: (0, 0, i)), table, spec((8, heads), lambda i: (0, 0)),
                       cols(length, first), cols(HALO, first), cols(HALO, first), cols(8, first)),
            scratch=[window, window],
            into=backs[-1][3:] if backs else (),
        )(kq, fronts[c][1], *pres[c - CHUNKS // 2], mids[c][0], x, halo, full, skip_x, et, ei, sides,
          *[n[0] for n in near], *[n[1] for n in near])

    fore, aft = Chain(CHUNKS, rates, sides, False), Chain(CHUNKS, rates, sides, True)
    depth, steps = fore.depth, fore.steps
    fronts, mids, pres, backs, got, got_back = [], [], [], [], [], []
    for u in range(CHUNKS + 2 * depth + 1):
        if u < CHUNKS:
            fronts.append(front(u))
            got.append(fore.swap(fronts[u][3]))
        if u < steps:
            fore.step(u, [f[2] for f in fronts], got)
        if depth <= u < depth + CHUNKS:
            mids.append(middle(u - depth))
            got_back.append(fore.swap(mids[-1][4]))
        if depth + 1 <= u < depth + 1 + steps:
            aft.step(u - depth - 1, [m[3] for m in mids], got_back, *[b[2] for b in backs[-1:]],
                     *[p[0] for p in pres[-1:]])
            if depth - 2 <= u - depth - 1 < depth - 2 + CHUNKS // 2:
                pres.append(before(len(pres) + CHUNKS // 2, aft.starts[-1][0]))
        if u >= 2 * depth + 1:
            c = u - 2 * depth - 1
            backs.append(back(c) if c < CHUNKS // 2 else after(c))

    grad_dt, hs, gx, lead, tail, wr = grid_call(
        lambda *refs: last_kernel(CHUNKS, *refs), "last", 2,
        out_shape=(shape((length, heads), F32), shape((8, heads), F32), *grad_shapes),
        in_specs=conv_specs(GROUPS) + [table, row_head, row_head]
        + [spec((1, length, per * STATE), lambda i: (i, 0, 0))] * CHUNKS + [table] * (2 * CHUNKS)
        + [spec((8, heads), lambda i: (0, 0))] * CHUNKS,
        out_specs=(table, spec((8, heads), lambda i: (0, 0)), cols(length, GROUPS), cols(HALO, GROUPS),
                   cols(HALO, GROUPS), cols(8, GROUPS)),
        scratch=[window, window],
        into=backs[-1][3:],
    )(x, halo, full, dt, step_b, decay, *[b[0] for b in backs], *[m[5] for m in mids], *[b[1] for b in backs],
      *[b[2] for b in backs])
    grad_gate, sums = mids[-1][6:]

    next_gp = lax.ppermute(lead, "ctx", behind)
    fixed = []
    for i in range(HALO):
        row = tail[i]
        for k in range(i + 1):
            row = row + full[k] * next_gp[i - k]
        fixed.append(row)
    grad_xbc = lax.dynamic_update_slice(gx, jnp.stack(fixed).astype(BF16), (length - HALO, 0))

    skip_grad = jnp.sum(sums[1].reshape(heads, HEAD_DIM), axis=1)
    extra_row = pack_row(
        sums[0].reshape(shards, g_loc), hs[0].reshape(shards, h_loc), hs[1].reshape(shards, h_loc),
        skip_grad.reshape(shards, h_loc)).reshape(1, channels)
    parts = jnp.concatenate([wr[: KERNEL + 1], extra_row, jnp.zeros((8 - KERNEL - 2, channels), F32)], axis=0)
    split = ranks // 8
    piece = c_loc // split
    parts = parts.reshape(8, shards, split, piece).transpose(0, 2, 1, 3).reshape(ranks * shards, piece)
    summed = jnp.sum(lax.all_to_all(parts, ("ctx", "fsdp"), 0, 0, tiled=True), axis=0)
    summed = summed * (1.0 / math.sqrt(length * ranks * shards))
    copies = jnp.broadcast_to(summed[None], (ranks, piece))
    mine = lax.all_to_all(copies, "ctx", 0, 0, tiled=True).reshape(8, c_loc)
    ends = mine[KERNEL + 1]
    return (
        grad_xbc[None],
        grad_dt[None],
        grad_gate[None],
        mine[:KERNEL],
        mine[KERNEL],
        ends[g_loc : g_loc + h_loc],
        ends[g_loc + h_loc : g_loc + 2 * h_loc],
        ends[g_loc + 2 * h_loc : g_loc + 3 * h_loc],
        ends[:g_loc],
    )


def solution(mesh):
    data = P("fsdp", "ctx", None)
    one = P("fsdp")
    return jax.shard_map(
        body,
        mesh=mesh,
        in_specs=(data, data, data, data, P(None, "fsdp"), one, one, one, one, one),
        out_specs=(data, data, data, P(None, "fsdp"), one, one, one, one, one),
        check_vma=False,
    )
```

```python
import math

import jax
import jax.numpy as jnp
from jax import lax
from jax.experimental import pallas as pl
from jax.experimental.pallas import tpu as pltpu
from jax.sharding import PartitionSpec as P

HEAD_DIM = 64
STATE = 128
GROUPS = 8
KERNEL = 4
EPSILON = 1e-05
HALO = KERNEL - 1
PAD = 8
CHUNKS = 4
F32 = jnp.float32
BF16 = jnp.bfloat16
HIGHEST = lax.Precision.HIGHEST


def mm(a, b):
    return jnp.dot(a, b, preferred_element_type=F32)


def mm_nt(a, b):
    return lax.dot_general(a, b, (((1,), (1,)), ((), ())), preferred_element_type=F32)


def sigmoid(v):
    return 0.5 * jnp.tanh(0.5 * v) + 0.5


def softplus(v):
    return jnp.maximum(v, 0.0) + jnp.log(1.0 + jnp.exp(-jnp.abs(v)))


def spread_heads(table, group, per_group):
    heads = table.shape[1]
    table = pltpu.roll(table, lax.rem(heads - group * per_group, heads), 1)
    rows = table.shape[0]
    pair = 128 // HEAD_DIM
    lane = lax.broadcasted_iota(jnp.int32, (rows, 128), 1)
    tiles = []
    for i in range(per_group // pair):
        tile = jnp.broadcast_to(table[:, pair * i : pair * i + 1], (rows, 128))
        for p in range(1, pair):
            col = jnp.broadcast_to(table[:, pair * i + p : pair * i + p + 1], (rows, 128))
            tile = jnp.where(lane >= p * HEAD_DIM, col, tile)
        tiles.append(tile)
    return jnp.concatenate(tiles, axis=1)


def sum_heads(values, group, per_group, heads):
    width = values.shape[1]
    row = lax.broadcasted_iota(jnp.int32, (width, heads), 0) // HEAD_DIM + group * per_group
    col = lax.broadcasted_iota(jnp.int32, (width, heads), 1)
    pick = jnp.where(row == col, 1.0, 0.0).astype(BF16)
    high = values.astype(BF16)
    low = (values - high.astype(F32)).astype(BF16)
    return mm(high, pick) + mm(low, pick)


def lower_mask(n):
    return lax.broadcasted_iota(jnp.int32, (n, n), 0) >= lax.broadcasted_iota(jnp.int32, (n, n), 1)


def upper_mask(n):
    return lax.broadcasted_iota(jnp.int32, (n, n), 0) <= lax.broadcasted_iota(jnp.int32, (n, n), 1)


def conv_pre(x_ref, halo_ref, w_ref, xs):
    length = x_ref.shape[0]
    xs[PAD - HALO : PAD, :] = halo_ref[...].astype(F32)
    xs[PAD : PAD + length, :] = x_ref[...].astype(F32)
    pre = jnp.broadcast_to(w_ref[KERNEL : KERNEL + 1, :], (length, x_ref.shape[1]))
    for k in range(KERNEL):
        pre = pre + w_ref[k : k + 1, :] * xs[PAD - HALO + k : PAD - HALO + k + length, :]
    return pre


def split_halves(state, mine, own_ref, send_ref):
    half = state.shape[0] // 2
    low, high = state[:half].astype(BF16), state[half:].astype(BF16)
    shape = own_ref.shape
    own_ref[...] = jnp.where(mine == 0, low, high).reshape(shape)
    send_ref[...] = jnp.where(mine == 0, high, low).reshape(shape)


def keys_kernel(per_group, x_ref, halo_ref, w_ref, dt_ref, sb_ref, dl_ref, kq_ref, ec_ref, ei_ref, et_ref, xs):
    length = x_ref.shape[0]

    @pl.when(pl.program_id(0) == 0)
    def _():
        step = softplus(dt_ref[...].astype(F32) + sb_ref[...])
        ld = -jnp.exp(dl_ref[...]) * step
        tril = jnp.where(lower_mask(length), 1.0, 0.0).astype(F32)
        cum = jnp.dot(tril, ld, precision=HIGHEST, preferred_element_type=F32)
        ec = jnp.exp(cum)
        ec_ref[...] = ec
        ei_ref[...] = jnp.exp(-cum) * step
        width = per_group * HEAD_DIM
        for g in range(GROUPS):
            et_ref[:, g * width : (g + 1) * width] = spread_heads(ec[length - 8 :, :], g, per_group)[7:8, :]

    pre = conv_pre(x_ref, halo_ref, w_ref, xs)
    kq_ref[...] = (pre * sigmoid(pre)).astype(BF16)


def front_kernel(per_group, first, x_ref, halo_ref, w_ref, k_ref, ei_ref, et_ref,
                 side_ref, mixed_ref, vp_ref, own_ref, send_ref, xs):
    g = first + pl.program_id(0)
    pre = conv_pre(x_ref, halo_ref, w_ref, xs)
    mixed = (pre * sigmoid(pre)).astype(BF16)
    mixed_ref[...] = mixed
    vp = (mixed.astype(F32) * spread_heads(ei_ref[...], g, per_group)).astype(BF16)
    vp_ref[...] = vp
    ut = mm(k_ref[...].astype(F32).T.astype(BF16), vp) * et_ref[...]
    split_halves(ut, side_ref[0], own_ref, send_ref)


def choose(refs, pick):
    value = refs[0][...]
    for i in range(1, len(refs)):
        value = jnp.where(pick == i, refs[i][...], value)
    return value


def join_halves(own, other, mine):
    return jnp.concatenate([jnp.where(mine == 0, own, other), jnp.where(mine == 0, other, own)], axis=0)


def middle_kernel(per_group, first, depth, v_ref, k_ref, q_ref, vp_ref, ec_ref, gate_ref, og_ref, gain_ref, skip_ref,
                  side_ref, *refs):
    keeps, backs = refs[:depth], refs[depth : 2 * depth]
    dy_ref, dyp_ref, st_ref, own_ref, send_ref, a1_ref, gg_ref, rows_ref = refs[2 * depth :]
    st = join_halves(choose(keeps, side_ref[2]), choose(backs, side_ref[2]), side_ref[0])
    st_ref[...] = st
    g = first + pl.program_id(0)
    length, width = v_ref.shape
    heads = ec_ref.shape[1]
    q = q_ref[...]
    z = jnp.where(lower_mask(length), mm_nt(q, k_ref[...]), 0.0).astype(BF16)
    yn = mm(jnp.concatenate([z, q], axis=1), jnp.concatenate([vp_ref[...], st], axis=0))
    ecx = spread_heads(ec_ref[...], g, per_group)
    v = v_ref[...].astype(F32)
    y = (ecx * yn + skip_ref[...] * v).astype(BF16).astype(F32)
    gate = gate_ref[...].astype(F32)
    og = og_ref[...].astype(F32)
    sig = sigmoid(gate)
    act = gate * sig
    gated = y * act
    scale = lax.rsqrt(jnp.sum(gated * gated, axis=1, keepdims=True) * (1.0 / width) + EPSILON)
    dgn = og * gain_ref[...]
    inner = jnp.sum(dgn * gated, axis=1, keepdims=True) * (1.0 / width)
    dgated = scale * dgn - gated * (scale * scale * scale * inner)
    dyb = (dgated * act).astype(BF16)
    dy_ref[...] = dyb
    gg_ref[...] = (dgated * y * (sig + act * (1.0 - sig))).astype(BF16)
    dy = dyb.astype(F32)
    dyp = (ecx * dy).astype(BF16)
    dyp_ref[...] = dyp
    gt = mm(q.astype(F32).T.astype(BF16), dyp)
    split_halves(gt, side_ref[1], own_ref, send_ref)
    rows_ref[...] = jnp.zeros(rows_ref.shape, F32)
    rows_ref[0:1, :] = jnp.sum(og * gated * scale, axis=0, keepdims=True)
    rows_ref[1:2, :] = jnp.sum(dy * v, axis=0, keepdims=True)

    @pl.when(pl.program_id(0) == 0)
    def _():
        a1_ref[...] = jnp.zeros(a1_ref.shape, F32)

    a1_ref[...] += sum_heads(dyp.astype(F32) * yn, g, per_group, heads)


def conv_back(grads, x_ref, halo_ref, w_ref, gx_ref, lead_ref, tail_ref, wr_ref, xs, gs):
    length = x_ref.shape[0]
    pre = conv_pre(x_ref, halo_ref, w_ref, xs)
    sig = sigmoid(pre)
    gp = grads * (sig * (1.0 + pre * (1.0 - sig)))
    gs[0:length, :] = gp
    gs[length:, :] = jnp.zeros((gs.shape[0] - length, gs.shape[1]), F32)
    wr_ref[...] = jnp.zeros(wr_ref.shape, F32)
    total = jnp.zeros(gp.shape, F32)
    for k in range(KERNEL):
        lead = HALO - k
        total = total + w_ref[k : k + 1, :] * gs[lead : lead + length, :]
        wr_ref[k : k + 1, :] = jnp.sum(gp * xs[PAD - HALO + k : PAD - HALO + k + length, :], axis=0, keepdims=True)
    wr_ref[KERNEL : KERNEL + 1, :] = jnp.sum(gp, axis=0, keepdims=True)
    gx_ref[...] = total.astype(BF16)
    lead_ref[...] = gp[0:HALO, :]
    tail_ref[...] = total[length - HALO : length, :]


def back_kernel(per_group, first, depth, k_ref, q_ref, vp_ref, st_ref, dy_ref, dyp_ref, x_ref, halo_ref, w_ref,
                skip_ref, et_ref, ei_ref, side_ref, *refs):
    keeps, backs = refs[:depth], refs[depth : 2 * depth]
    dkq_ref, a2_ref, last_ref, gx_ref, lead_ref, tail_ref, wr_ref, xs, gs = refs[2 * depth :]
    j = first + pl.program_id(0)
    length, width = x_ref.shape
    heads = ei_ref.shape[1]

    @pl.when(pl.program_id(0) == 0)
    def _():
        a2_ref[...] = jnp.zeros(a2_ref.shape, F32)
        last_ref[...] = jnp.zeros(last_ref.shape, F32)

    k = k_ref[...]
    q = q_ref[...]
    vp = vp_ref[...]
    dyp = dyp_ref[...]
    st = st_ref[...]
    en = join_halves(choose(keeps, side_ref[3]), choose(backs, side_ref[3]), side_ref[1])
    en = (et_ref[...] * en.astype(F32)).astype(BF16)
    zt = jnp.where(upper_mask(length), mm_nt(k, q), 0.0).astype(BF16)
    dvp = mm(jnp.concatenate([zt, k], axis=1), jnp.concatenate([dyp, en], axis=0))
    grads = spread_heads(ei_ref[...], j, per_group) * dvp + skip_ref[...] * dy_ref[...].astype(F32)
    a2_ref[...] += sum_heads(vp.astype(F32) * dvp, j, per_group, heads)
    ends = en.astype(F32) * (st.astype(F32) + mm(k.astype(F32).T.astype(BF16), vp))
    ends = jnp.broadcast_to(jnp.sum(ends, axis=0, keepdims=True), (8, width))
    last_ref[...] += sum_heads(ends, j, per_group, heads)
    dz = jnp.where(lower_mask(length), mm_nt(dyp, vp), 0.0)
    dkq_ref[0] = mm(dz.T.astype(BF16), q) + mm_nt(vp, en)
    dkq_ref[1] = mm(dz.astype(BF16), k) + mm_nt(dyp, st)
    conv_back(grads, x_ref, halo_ref, w_ref, gx_ref, lead_ref, tail_ref, wr_ref, xs, gs)


def last_kernel(count, x_ref, halo_ref, w_ref, dt_ref, sb_ref, dl_ref, *refs):
    dkq, a1, a2, last = (refs[i * count : (i + 1) * count] for i in range(4))
    gdt_ref, hs_ref, gx_ref, lead_ref, tail_ref, wr_ref, xs, gs = refs[4 * count :]
    grads = jnp.concatenate([ref[0] for ref in dkq], axis=1)
    conv_back(grads, x_ref, halo_ref, w_ref, gx_ref, lead_ref, tail_ref, wr_ref, xs, gs)

    @pl.when(pl.program_id(0) == 0)
    def _():
        length, heads = dt_ref.shape
        raw = dt_ref[...].astype(F32) + sb_ref[...]
        step = softplus(raw)
        rate = jnp.exp(dl_ref[...])
        row = lax.broadcasted_iota(jnp.int32, (length, heads), 0)
        down = sum(ref[...] for ref in a2)
        end = sum(ref[...] for ref in last)[0:1, :]
        dcum = sum(ref[...] for ref in a1) - down + jnp.where(row == length - 1, end, 0.0)
        triu = jnp.where(upper_mask(length), 1.0, 0.0).astype(F32)
        dld = jnp.dot(triu, dcum, precision=HIGHEST, preferred_element_type=F32)
        gdt = (down / step - rate * dld) * sigmoid(raw)
        gdt_ref[...] = gdt
        hs_ref[...] = jnp.zeros(hs_ref.shape, F32)
        hs_ref[0:1, :] = jnp.sum(-rate * step * dld, axis=0, keepdims=True)
        hs_ref[1:2, :] = jnp.sum(gdt, axis=0, keepdims=True)


PARAMS = pltpu.CompilerParams(vmem_limit_bytes=40 * 1024 * 1024)


def grid_call(kernel, name, steps, in_specs, out_specs, out_shape, scratch=(), into=()):
    given = len(in_specs)
    anywhere = pl.BlockSpec(memory_space=pl.ANY)

    def stays(s):
        return s.shape[0] == STATE // 2 or s.shape == (8, STATE)

    def place(s):
        return s if stays(s) else pltpu.HBM(s.shape, s.dtype)

    call = pl.pallas_call(
        lambda *refs: kernel(*refs[:given], *refs[given + len(into) :]),
        out_shape=tuple(place(s) for s in out_shape),
        grid=(steps,),
        in_specs=[*in_specs, *[anywhere] * len(into)],
        out_specs=out_specs,
        scratch_shapes=scratch,
        input_output_aliases={given + i: len(out_shape) - len(into) + i for i in range(len(into))},
        compiler_params=PARAMS,
        name=name,
    )

    def run(*values):
        kept = [v if s.memory_space == pltpu.SMEM or stays(v) else in_hbm(v)
                for v, s in zip(values, in_specs, strict=True)]
        return call(*kept, *[in_hbm(v) for v in into])

    return run


def hop_kernel(has_carry, choices, chunk, side, mine_ref, pair_ref, *refs):
    own, got = choose(refs[:choices], chunk), choose(refs[choices : 2 * choices], chunk)
    refs = refs[2 * choices :]
    if has_carry:
        carry_ref, next_ref, give_ref, keep_ref = refs
        carry = carry_ref[...].astype(F32)
    else:
        next_ref, give_ref, keep_ref = refs
        carry = jnp.zeros(next_ref.shape, F32)
    first = side == 0
    own, got = own.astype(F32), got.astype(F32)
    mine, pair = mine_ref[...], pair_ref[...]
    inner = jnp.where(first, mine, pair) * carry + jnp.where(first, own, got)
    next_ref[...] = (jnp.where(first, pair, mine) * inner + jnp.where(first, got, own)).astype(BF16)
    give_ref[...] = jnp.where(first, inner, carry).astype(BF16)
    keep_ref[...] = jnp.where(first, carry, inner).astype(BF16)


def in_hbm(value):
    return pltpu.with_memory_space_constraint(value, pltpu.HBM)


class Chain:
    def __init__(self, count, rates, sides, flip):
        self.count, self.rates, self.sides, self.flip = count, rates, sides, flip
        self.ranks = lax.axis_size("ctx")
        self.depth = self.ranks // 2
        self.steps = count + self.depth - 1
        self.carry = None
        self.starts = []

    def physical(self, r):
        return self.ranks - 1 - r if self.flip else r

    def live(self, s):
        return [z for z in range(self.depth) if 0 <= s - z < self.count]

    def swap(self, value, s=None):
        places = range(self.depth) if s is None else self.live(s)
        pairs = [(self.physical(2 * z + p), self.physical(2 * z + 1 - p)) for z in places for p in range(2)]
        return lax.ppermute(value, "ctx", pairs)

    def up(self, value, s):
        live = [z for z in self.live(s) if z + 1 < self.depth]
        pairs = [(self.physical(2 * z + p), self.physical(2 * z + 2 + p)) for z in live for p in range(2)]
        return lax.ppermute(value, "ctx", pairs) if pairs else None

    def step(self, s, owns, gots, *first):
        if self.carry is not None and self.flip:
            keep, back = self.starts[-1]
            self.carry, back, *_ = lax.optimization_barrier((self.carry, back, *first))
            self.starts[-1] = (keep, back)
        rows, lanes = gots[0].shape
        owns, gots = owns[: s + 1], gots[: s + 1]
        tile = lanes
        per = lanes // tile
        flat = pl.BlockSpec((rows, tile), lambda i, at: (0, i))
        flip, count = int(self.flip), self.count

        def chunk(at):
            return jnp.clip(s - at[2 + flip], 0, count - 1)

        line = pl.BlockSpec((1, tile), lambda i, at: (0, chunk(at) * per + i))
        carries = [] if self.carry is None else [self.carry]
        operands = [*self.rates, *owns, *gots, *carries]
        after, give, keep = pl.pallas_call(
            lambda at, *refs: hop_kernel(len(carries) > 0, len(owns), chunk(at), at[flip], *refs),
            out_shape=(jax.ShapeDtypeStruct((rows, lanes), BF16),) * 3,
            grid_spec=pltpu.PrefetchScalarGridSpec(
                num_scalar_prefetch=1,
                grid=(per,),
                in_specs=[line, line] + [flat] * (len(operands) - 2),
                out_specs=[flat] * 3,
            ),
            compiler_params=PARAMS,
            name="hop_back" if self.flip else "hop",
        )(self.sides, *operands)
        self.carry = self.up(after, s)
        self.starts.append((keep, self.swap(give, s)))

def body(proj_xbc, proj_dt, proj_gate, out_grad, conv_weight, conv_bias, decay_log, step_bias, skip_gain, norm_gain):
    x, dt, gate, og = proj_xbc[0], proj_dt[0], proj_gate[0], out_grad[0]
    length, channels = x.shape
    heads = dt.shape[1]
    inner = heads * HEAD_DIM
    ranks = lax.axis_size("ctx")
    shards = lax.axis_size("fsdp")
    per_group = heads // GROUPS
    width = per_group * HEAD_DIM
    side = lax.axis_index("ctx") % 2
    place = lax.axis_index("ctx") // 2
    sides = jnp.stack([side, 1 - side, place, ranks // 2 - 1 - place]).astype(jnp.int32)
    part = inner // CHUNKS
    per = part // width
    c_loc, g_loc, h_loc = channels // shards, inner // shards, heads // shards
    spare = c_loc - g_loc - 3 * h_loc
    groups = GROUPS
    blocks = channels // width

    ahead = [(i, i + 1) for i in range(ranks - 1)]
    behind = [(i + 1, i) for i in range(ranks - 1)]
    halo = lax.ppermute(x[length - HALO :, :], "ctx", ahead)

    def pack_row(gain, decay, step, skip):
        return jnp.concatenate([gain, decay, step, skip, jnp.zeros(gain.shape[:-1] + (spare,), F32)], axis=-1)

    packed = jnp.concatenate(
        [conv_weight, conv_bias[None], pack_row(norm_gain, decay_log, step_bias, skip_gain)[None],
         jnp.zeros((8 - KERNEL - 2, c_loc), F32)], axis=0)
    full = lax.all_gather(packed, "fsdp", axis=1, tiled=True)
    extra = full[KERNEL + 1].reshape(shards, c_loc)
    gain = extra[:, :g_loc].reshape(1, inner)
    decay = extra[:, g_loc : g_loc + h_loc].reshape(1, heads)
    step_b = extra[:, g_loc + h_loc : g_loc + 2 * h_loc].reshape(1, heads)
    skip = extra[:, g_loc + 2 * h_loc : g_loc + 3 * h_loc].reshape(1, heads)
    skip_x = jnp.repeat(skip, HEAD_DIM, axis=1)

    def spec(shape, where):
        return pl.BlockSpec(shape, where)

    def shape(dims, kind):
        return jax.ShapeDtypeStruct(dims, kind)

    table = spec((length, heads), lambda i: (0, 0))
    row_head = spec((1, heads), lambda i: (0, 0))
    scalars = pl.BlockSpec(memory_space=pltpu.SMEM)
    wide_out = spec((length, width), lambda i: (0, i))
    half_out = spec((STATE // 2, width), lambda i: (0, i))
    window = pltpu.VMEM((PAD + length, width), F32)
    wide_bf, half_bf = shape((length, part), BF16), shape((STATE // 2, part), BF16)
    grad_shapes = (shape((length, channels), BF16), shape((HALO, channels), F32), shape((HALO, channels), F32),
                   shape((8, channels), F32))

    def conv_specs(first):
        return [spec((rows, width), lambda i: (0, first + i)) for rows in (length, HALO, 8)]

    def cols(rows, first):
        return spec((rows, width), lambda i: (0, first + i))

    def head_cols(first):
        return [spec((length, STATE), lambda i: (0, first + i)), spec((length, STATE), lambda i: (0, GROUPS + first + i))]

    kq, ec, ei, et = grid_call(
        lambda *refs: keys_kernel(per_group, *refs), "keys", 2,
        out_shape=(shape((length, 2 * width), BF16), shape((length, heads), F32), shape((length, heads), F32),
                   shape((1, inner), F32)),
        in_specs=conv_specs(GROUPS) + [table, row_head, row_head],
        out_specs=(wide_out, table, table, spec((1, inner), lambda i: (0, 0))),
        scratch=[window],
    )(x, halo, full, dt, step_b, decay)
    rates = (et, lax.ppermute(et, "ctx", [(i, i ^ 1) for i in range(ranks)]))

    def front(c):
        first = c * per
        return grid_call(
            lambda *refs: front_kernel(per_group, first, *refs), "front", per,
            out_shape=(wide_bf, wide_bf, half_bf, half_bf),
            in_specs=conv_specs(first) + head_cols(first)[:1] + [table, cols(1, first), scalars],
            out_specs=(wide_out, wide_out, half_out, half_out),
            scratch=[window],
        )(x, halo, full, kq, ei, et, sides)

    def middle(c):
        first = c * per
        near = fore.starts[c : c + depth]
        return grid_call(
            lambda *refs: middle_kernel(per_group, first, depth, *refs), "middle", per,
            out_shape=(wide_bf, wide_bf, shape((STATE, part), BF16), half_bf, half_bf, shape((length, heads), F32),
                       shape((length, inner), BF16), shape((8, inner), F32)),
            in_specs=[wide_out, *head_cols(first), wide_out, table, cols(length, first), cols(length, first),
                      cols(1, first), cols(1, first), scalars] + [half_out] * (2 * depth),
            out_specs=(wide_out, wide_out, spec((STATE, width), lambda i: (0, i)), half_out, half_out, table,
                       cols(length, first), cols(8, first)),
            into=mids[-1][6:] if mids else (),
        )(fronts[c][0], kq, kq, fronts[c][1], ec, gate, og, gain, skip_x, sides,
          *[n[0] for n in near], *[n[1] for n in near])

    def back(c):
        first = c * per
        near = aft.starts[c : c + depth]
        dy, dyp, st = mids[c][:3]
        return grid_call(
            lambda *refs: back_kernel(per_group, first, depth, *refs), "back", per,
            out_shape=(shape((2, length, per * STATE), F32), shape((length, heads), F32), shape((8, heads), F32),
                       *grad_shapes),
            in_specs=[*head_cols(first), wide_out, spec((STATE, width), lambda i: (0, i)), wide_out, wide_out,
                      *conv_specs(first), cols(1, first), cols(1, first), table, scalars] + [half_out] * (2 * depth),
            out_specs=(spec((2, length, STATE), lambda i: (0, 0, i)), table, spec((8, heads), lambda i: (0, 0)),
                       cols(length, first), cols(HALO, first), cols(HALO, first), cols(8, first)),
            scratch=[window, window],
            into=backs[-1][3:] if backs else (),
        )(kq, kq, fronts[c][1], st, dy, dyp, x, halo, full, skip_x, et, ei, sides,
          *[n[0] for n in near], *[n[1] for n in near])

    fore, aft = Chain(CHUNKS, rates, sides, False), Chain(CHUNKS, rates, sides, True)
    depth, steps = fore.depth, fore.steps
    skip_grad = None
    fronts, mids, backs, got, got_back = [], [], [], [], []
    for u in range(CHUNKS + 2 * depth + 1):
        if u < CHUNKS:
            fronts.append(front(u))
            got.append(fore.swap(fronts[u][3]))
        if u < steps:
            fore.step(u, [f[2] for f in fronts], got)
        if depth <= u < depth + CHUNKS:
            mids.append(middle(u - depth))
            got_back.append(fore.swap(mids[-1][4]))
        skip_grads = [jnp.sum(mids[-1][7][1].reshape(heads, HEAD_DIM), axis=1)] if u == depth + CHUNKS else []
        skip_grad = skip_grads[0] if skip_grads else skip_grad
        if depth + 1 <= u < depth + 1 + steps:
            aft.step(u - depth - 1, [m[3] for m in mids], got_back, *[b[2] for b in backs[-1:]], *skip_grads)
        if u >= 2 * depth + 1:
            backs.append(back(u - 2 * depth - 1))

    grad_dt, hs, gx, lead, tail, wr = grid_call(
        lambda *refs: last_kernel(CHUNKS, *refs), "last", 2,
        out_shape=(shape((length, heads), F32), shape((8, heads), F32), *grad_shapes),
        in_specs=conv_specs(GROUPS) + [table, row_head, row_head]
        + [spec((1, length, per * STATE), lambda i: (i, 0, 0))] * CHUNKS + [table] * (2 * CHUNKS)
        + [spec((8, heads), lambda i: (0, 0))] * CHUNKS,
        out_specs=(table, spec((8, heads), lambda i: (0, 0)), cols(length, GROUPS), cols(HALO, GROUPS),
                   cols(HALO, GROUPS), cols(8, GROUPS)),
        scratch=[window, window],
        into=backs[-1][3:],
    )(x, halo, full, dt, step_b, decay, *[b[0] for b in backs], *[m[5] for m in mids], *[b[1] for b in backs],
      *[b[2] for b in backs])
    grad_gate, sums = mids[-1][6:]

    next_gp = lax.ppermute(lead, "ctx", behind)
    fixed = []
    for i in range(HALO):
        row = tail[i]
        for k in range(i + 1):
            row = row + full[k] * next_gp[i - k]
        fixed.append(row)
    grad_xbc = lax.dynamic_update_slice(gx, jnp.stack(fixed).astype(BF16), (length - HALO, 0))

    extra_row = pack_row(
        sums[0].reshape(shards, g_loc), hs[0].reshape(shards, h_loc), hs[1].reshape(shards, h_loc),
        skip_grad.reshape(shards, h_loc)).reshape(1, channels)
    parts = jnp.concatenate([wr[: KERNEL + 1], extra_row, jnp.zeros((8 - KERNEL - 2, channels), F32)], axis=0)
    split = ranks // 8
    piece = c_loc // split
    parts = parts.reshape(8, shards, split, piece).transpose(0, 2, 1, 3).reshape(ranks * shards, piece)
    summed = jnp.sum(lax.all_to_all(parts, ("ctx", "fsdp"), 0, 0, tiled=True), axis=0)
    summed = summed * (1.0 / math.sqrt(length * ranks * shards))
    copies = jnp.broadcast_to(summed[None], (ranks, piece))
    mine = lax.all_to_all(copies, "ctx", 0, 0, tiled=True).reshape(8, c_loc)
    ends = mine[KERNEL + 1]
    return (
        grad_xbc[None],
        grad_dt[None],
        grad_gate[None],
        mine[:KERNEL],
        mine[KERNEL],
        ends[g_loc : g_loc + h_loc],
        ends[g_loc + h_loc : g_loc + 2 * h_loc],
        ends[g_loc + 2 * h_loc : g_loc + 3 * h_loc],
        ends[:g_loc],
    )


def solution(mesh):
    data = P("fsdp", "ctx", None)
    one = P("fsdp")
    return jax.shard_map(
        body,
        mesh=mesh,
        in_specs=(data, data, data, data, P(None, "fsdp"), one, one, one, one, one),
        out_specs=(data, data, data, P(None, "fsdp"), one, one, one, one, one),
        check_vma=False,
    )
```
